32 devices in a mesh: batch: 8 (over y, x, core), ctx: 4 (over z).
Axes of the slice: x: 2, y: 2, z: 4, core: 2. Of those that a mesh axis runs over, the one named last changes fastest.
Arguments:
- tokens: bfloat16 [2, 8, 1024, 2048], P(None, 'batch', 'ctx'), may hold values from -6 to 6
- lengths: int32 [2, 8], P(None, 'batch'), may hold values from 256 to 1024, as said below
- expert_ids: int32 [2, 8, 1024, 8], P(None, 'batch', 'ctx'), may hold values from 0 to 15, all different within a row; in each aligned block of 256 rows (0 to 255, 256 to 511, ..., all dimensions but the last counted through in order) at most 160 rows name the same one
- route_levels: int32 [2, 8, 1024, 8], P(None, 'batch', 'ctx'), may hold values from 1 to 16
- w_query: bfloat16 [2048, 2048], P(('batch', 'ctx')), may hold values from -0.125 to 0.125
- w_key: bfloat16 [2048, 2048], P(('batch', 'ctx')), may hold values from -0.125 to 0.125
- w_value: bfloat16 [2048, 2048], P(('batch', 'ctx')), may hold values from -0.125 to 0.125
- w_out: bfloat16 [2048, 2048], P(('batch', 'ctx')), may hold values from -0.5 to 0.5
- attn_gain: bfloat16 [2048], P(('batch', 'ctx')), may hold values from 0.25 to 1.75
- query_gain: bfloat16 [2048], P(('batch', 'ctx')), may hold values from 0.25 to 1.75
- key_gain: bfloat16 [2048], P(('batch', 'ctx')), may hold values from 0.25 to 1.75
- ffn_gain: bfloat16 [2048], P(('batch', 'ctx')), may hold values from 0.25 to 1.75
- w_gate: bfloat16 [16, 2048, 1024], P('ctx', 'batch'), may hold values from -0.125 to 0.125
- w_up: bfloat16 [16, 2048, 1024], P('ctx', 'batch'), may hold values from -0.125 to 0.125
- w_down: bfloat16 [16, 1024, 2048], P('ctx', None, 'batch'), may hold values from -0.75 to 0.75
- cotangent: bfloat16 [2, 8, 1024, 2048], P(None, 'batch', 'ctx'), may hold values from -6 to 6
Outputs:
- out: bfloat16 [2, 8, 1024, 2048], P(None, 'batch', 'ctx')
- grad_tokens: float32 [2, 8, 1024, 2048], P(None, 'batch', 'ctx')
- grad_w_query: float32 [2048, 2048], P(('batch', 'ctx'))
- grad_w_key: float32 [2048, 2048], P(('batch', 'ctx'))
- grad_w_value: float32 [2048, 2048], P(('batch', 'ctx'))
- grad_w_out: float32 [2048, 2048], P(('batch', 'ctx'))
- grad_attn_gain: float32 [2048], P(('batch', 'ctx'))
- grad_query_gain: float32 [2048], P(('batch', 'ctx'))
- grad_key_gain: float32 [2048], P(('batch', 'ctx'))
- grad_ffn_gain: float32 [2048], P(('batch', 'ctx'))
- grad_w_gate: float32 [16, 2048, 1024], P('ctx', 'batch')
- grad_w_up: float32 [16, 2048, 1024], P('ctx', 'batch')
- grad_w_down: float32 [16, 1024, 2048], P('ctx', None, 'batch')
The draws below stay inside these ranges and needn't reach their ends.
Inputs may be any that keep to these rules, and one draw needn't show every extreme that they name: The first lengths[m, s] slots of sequence s of micro-batch m are live, the others padding. `expert_ids`: each row names 8 different experts; in each aligned block of 256 rows (one sequence's slots on one index of ctx) no expert is named by more than 160 rows.
All inputs are finite; a program needn't handle non-finite values.
Results may differ from the reference program's by a relative error of at most 0.019.
Values may be sent and summed in bfloat16 or wider, within the bound.
No kernel may reach another device: no remote copies, remote signals or barrier semaphores. Data moves between devices by JAX's collectives and lax.ppermute only.
A program may use at most 512 MiB of HBM per device.

```python
import math
import jax
import jax.numpy as jnp
import numpy as np
from jax import lax

D = 2048
HEADS = 16
HEAD_DIM = 128
FF = 1024
TOPK = 8
LEN = 1024
MICRO = 2
EXPERTS = 16
SEQS = 8
BLOCK = 256
CAP = 160
N_CTX = 4


def draw_lengths(key, part):
    first, second = jax.random.split(key)
    count = MICRO * SEQS
    drawn = jax.random.randint(first, (count,), LEN // 4, LEN + 1, dtype=jnp.int32)
    order = jax.random.permutation(second, count)
    drawn = drawn.at[order[0]].set(LEN).at[order[1]].set(LEN // 4)
    return drawn.reshape(MICRO, SEQS)


def place_ends(values, rng, smallest, top_value):
    longest = values.shape.index(max(values.shape))
    spots = []
    for shift in (0, 1):
        where = [jax.random.randint(jax.random.fold_in(rng, axis), (), 0, length) for axis, length in enumerate(values.shape)]
        where[longest] = (where[longest] + shift) % values.shape[longest]
        spots.append(tuple(where))
    return values.at[spots[0]].set(smallest).at[spots[1]].set(top_value)


def block_scale(stream_key, dims, shards, low, top_value):
    level = 1.0
    for axis_at, blocks in shards:
        steps = jax.random.uniform(jax.random.fold_in(jax.random.fold_in(stream_key, 6), axis_at), (blocks,), jnp.float32, low / len(shards), top_value / len(shards))
        level = level * jnp.repeat(jnp.exp(steps), dims[axis_at] // blocks).reshape((-1,) + (1,) * (len(dims) - 1 - axis_at))
    return level


def shared_out(rng, own, number, rows, amount, top, bound, lean):
    sequence = jax.random.permutation(rng, amount)
    heavy_load, usual = load_shares(amount, rows * top, bound, lean, True), load_shares(amount, rows * top, bound, lean, False)
    places = jnp.arange(amount)

    def named(sizes, rotation):
        used = int((sizes > 0).sum())
        fixed = max(1, used // 4)
        passed = fixed + (places - fixed + rotation * (used - fixed)) % max(1, amount - fixed)
        return jnp.zeros((amount,), jnp.int32).at[sequence[jnp.where(places < fixed, places, passed)]].set(jnp.asarray(sizes, jnp.int32))

    sizes = jnp.where(number % 4 == 0, named(heavy_load, number // 4), named(usual, number - number // 4 - 1))
    mixed = jax.random.permutation(jax.random.fold_in(own, 3), amount)
    source_of, taker = mixed[0:amount // 2 * 2:2], mixed[1:amount // 2 * 2:2]
    margin = jnp.minimum(sizes[source_of] - 1, bound - sizes[taker]) // 2
    margin = jnp.where((source_of == sequence[0]) | (taker == sequence[0]) | (sizes[taker] == 0), 0, jnp.maximum(margin, 0))
    passed = jax.random.randint(jax.random.fold_in(own, 4), (amount // 2,), 0, 1 << 20) % (margin + 1)
    sizes = sizes.at[source_of].add(-passed).at[taker].add(passed)
    items = jnp.searchsorted(jnp.cumsum(sizes), jnp.arange(rows * top), side="right").astype(jnp.int32)
    grid = items.reshape(top, rows).T
    grid = grid[jax.random.permutation(jax.random.fold_in(own, 1), rows)]
    rotation = jax.random.randint(jax.random.fold_in(own, 2), (rows, 1), 0, top)
    return jnp.take_along_axis(grid, (jnp.arange(top)[None, :] + rotation) % top, axis=1)


def load_shares(number_of, total, bound, slope, full):
    weights = [(1 << 20) // math.isqrt(rank ** slope) + 1 for rank in range(1, number_of + 1)]
    largest = bound if full else min(bound, max(-(-total // number_of), total * weights[0] // sum(weights)))
    least = 1 if total - largest >= number_of - 1 else 0
    holding, spare = [largest] + [least] * (number_of - 1), total - largest - least * (number_of - 1)
    while spare > 0:
        movable = [i for i in range(1, number_of) if holding[i] < largest] or [i for i in range(1, number_of) if holding[i] < bound]
        mass, budget = sum([weights[i] for i in movable]), spare
        for i in movable:
            more = min(bound - holding[i], max(1, budget * weights[i] // mass), spare)
            holding[i] = holding[i] + more
            spare = spare - more
    return np.array(holding)


def bell_draw(stream_key, shape, deviation, bound, pieces=(), held_as=jnp.bfloat16):
    level = block_scale(stream_key, shape, pieces, -0.22, 0.18) if pieces else 1.0
    entries = jax.random.normal(stream_key, shape, jnp.float32) * deviation * level
    return jnp.minimum(jnp.maximum(entries, -bound), bound).astype(held_as)


def setup_inputs(seed: int = 0) -> dict:
    arg_keys = jax.random.split(jax.random.key(seed), 17)
    tokens = bell_draw(arg_keys[0], (MICRO, SEQS, LEN, D), 1.0, 6.0, ((1, 8), (2, 4)))
    lengths = draw_lengths(jax.random.fold_in(arg_keys[16], 71), 0)
    expert_ids_keys = jax.random.split(jax.random.fold_in(arg_keys[2], 1), MICRO * SEQS * LEN // BLOCK)
    expert_ids_turns = jax.random.permutation(jax.random.fold_in(arg_keys[2], 3), MICRO * SEQS * LEN // BLOCK)
    expert_ids = jax.vmap(lambda own, number: shared_out(jax.random.fold_in(arg_keys[2], 2), own, number, BLOCK, EXPERTS, TOPK, CAP, 0))(expert_ids_keys, expert_ids_turns).reshape((MICRO, SEQS, LEN, TOPK))
    route_levels = place_ends(jax.random.randint(arg_keys[3], (MICRO, SEQS, LEN, TOPK), 1, 17), jax.random.fold_in(arg_keys[3], 1), 1, 16).astype(jnp.int32)
    w_query = bell_draw(arg_keys[4], (D, D), D ** -0.5, 0.125, ((0, 32),))
    w_key = bell_draw(arg_keys[5], (D, D), D ** -0.5, 0.125, ((0, 32),))
    w_value = bell_draw(arg_keys[6], (D, D), D ** -0.5, 0.125, ((0, 32),))
    w_out = bell_draw(arg_keys[7], (D, D), (D // 16) ** -0.5, 0.5, ((0, 32),))
    attn_gain = jnp.clip(1.0 + 0.15 * jax.random.normal(arg_keys[8], (D,), jnp.float32), 0.25, 1.75).astype(jnp.bfloat16)
    query_gain = jnp.clip(1.0 + 0.15 * jax.random.normal(arg_keys[9], (D,), jnp.float32), 0.25, 1.75).astype(jnp.bfloat16)
    key_gain = jnp.clip(1.0 + 0.15 * jax.random.normal(arg_keys[10], (D,), jnp.float32), 0.25, 1.75).astype(jnp.bfloat16)
    ffn_gain = jnp.clip(1.0 + 0.15 * jax.random.normal(arg_keys[11], (D,), jnp.float32), 0.25, 1.75).astype(jnp.bfloat16)
    w_gate = bell_draw(arg_keys[12], (EXPERTS, D, FF), D ** -0.5, 0.125, ((0, 4), (1, 8)))
    w_up = bell_draw(arg_keys[13], (EXPERTS, D, FF), D ** -0.5, 0.125, ((0, 4), (1, 8)))
    w_down = bell_draw(arg_keys[14], (EXPERTS, FF, D), (FF // 16) ** -0.5, 0.75, ((0, 4), (2, 8)))
    cotangent = bell_draw(arg_keys[15], (MICRO, SEQS, LEN, D), 1.0, 6.0, ((1, 8), (2, 4)))
    return dict(tokens=tokens, lengths=lengths, expert_ids=expert_ids, route_levels=route_levels, w_query=w_query, w_key=w_key, w_value=w_value, w_out=w_out, attn_gain=attn_gain, query_gain=query_gain, key_gain=key_gain, ffn_gain=ffn_gain, w_gate=w_gate, w_up=w_up, w_down=w_down, cotangent=cotangent)


EPS = 1e-05
THETA = 10000.0
MASKED = -1e+30
HIGH = lax.Precision.HIGHEST

@jax.custom_vjp
def low(v):
    return lax.optimization_barrier(v.astype(jnp.bfloat16)).astype(jnp.float32)

@jax.custom_vjp
def low_back(v):
    return v

def low_keep(v):
    return (low(v), None)

def low_pass(kept, grad):
    return (grad,)

def back_keep(v):
    return (v, None)

def back_low(kept, grad):
    return (low(grad),)
low.defvjp(low_keep, low_pass)
low_back.defvjp(back_keep, back_low)

def product(left, right):
    return jnp.dot(left, right, precision=HIGH, preferred_element_type=jnp.float32)

def norm_rows(values, gain):
    return values * lax.rsqrt(lax.optimization_barrier(jnp.mean(values * values, axis=-1, keepdims=True)) + EPS) * gain

def tables(positions, head_dim):
    half = head_dim // 2
    inverse = THETA ** (-(jnp.arange(half, dtype=jnp.float32) * 2.0) / head_dim)
    angle = positions.astype(jnp.float32)[:, None] * inverse[None, :]
    cosines = jnp.cos(angle)
    sines = jnp.sin(angle)
    return (jnp.concatenate([cosines, cosines], axis=-1), jnp.concatenate([sines, sines], axis=-1))

def rotate(projected, gain, cosines, sines):
    normed = norm_rows(projected, gain)
    count = normed.shape[0]
    head_dim = cosines.shape[-1]
    heads = normed.reshape(count, -1, head_dim)
    half = head_dim // 2
    turned = jnp.concatenate([-heads[..., half:], heads[..., :half]], axis=-1)
    return (heads * cosines[:, None, :] + turned * sines[:, None, :]).reshape(count, -1)

def swiglu(gate, upper):
    return gate * jax.nn.sigmoid(gate) * upper

def slot_table(chosen):
    blocks = chosen.reshape(N_CTX, BLOCK * TOPK).astype(jnp.int32)
    onehot = (blocks[:, :, None] == jnp.arange(EXPERTS, dtype=jnp.int32)[None, None, :]).astype(jnp.int32)
    rank = lax.optimization_barrier(jnp.sum(jnp.cumsum(onehot, axis=1) * onehot, axis=-1)) - 1
    per_expert = N_CTX * CAP
    place = blocks * per_expert + jnp.arange(N_CTX, dtype=jnp.int32)[:, None] * CAP + rank
    filled = jnp.full((EXPERTS * per_expert,), LEN * TOPK, jnp.int32)
    filled = filled.at[place.reshape(-1).astype(jnp.int32)].set(jnp.arange(LEN * TOPK, dtype=jnp.int32))
    return filled.reshape(EXPERTS, per_expert)

def sequence_forward(inputs, params, length, filled, mixing):
    query_w, key_w, value_w, out_w, gain_attn, gain_query, gain_key, gain_ffn, gate_w, up_w, down_w = params
    positions = jnp.arange(LEN, dtype=jnp.int32)
    live = positions < length
    cosines, sines = tables(positions, HEAD_DIM)
    normed_in = low(norm_rows(inputs, gain_attn))
    query_proj = low_back(product(normed_in, query_w))
    key_proj = low_back(product(normed_in, key_w))
    values = low(low_back(product(normed_in, value_w))).reshape(LEN, HEADS, HEAD_DIM)
    query_heads = low(rotate(query_proj, gain_query, cosines, sines)).reshape(LEN, HEADS, HEAD_DIM)
    key_heads = low(rotate(key_proj, gain_key, cosines, sines)).reshape(LEN, HEADS, HEAD_DIM)
    scores = jnp.einsum('qhd,khd->hqk', query_heads, key_heads, precision=HIGH) * HEAD_DIM ** (-0.5)
    scores = low_back(scores)
    allowed = (positions[None, :] <= positions[:, None]) & live[None, :]
    scores = jnp.where(allowed[None, :, :], scores, MASKED)
    peak = lax.optimization_barrier(jnp.max(scores, axis=-1, keepdims=True))
    raised = jnp.exp(scores - peak)
    probs = low(raised / lax.optimization_barrier(jnp.sum(raised, axis=-1, keepdims=True)))
    attended = low(low_back(jnp.einsum('hqk,khd->qhd', probs, values, precision=HIGH))).reshape(LEN, D)
    hidden = inputs + low_back(product(attended, out_w))
    normed_mid = low(norm_rows(hidden, gain_ffn))
    padded = jnp.concatenate([normed_mid, jnp.zeros((1, D), normed_mid.dtype)], axis=0)
    owner = filled // TOPK
    dispatched = low_back(padded[owner])
    gate = low_back(jnp.einsum('esd,edf->esf', dispatched, gate_w, precision=HIGH))
    upper = low_back(jnp.einsum('esd,edf->esf', dispatched, up_w, precision=HIGH))
    active = low(swiglu(gate, upper))
    produced = low(low_back(jnp.einsum('esf,efd->esd', active, down_w, precision=HIGH)))
    slot_weight = jnp.concatenate([mixing.reshape(-1), jnp.zeros((1,), mixing.dtype)], axis=0)[filled]
    mixture = jnp.zeros((LEN + 1, D), inputs.dtype).at[owner.reshape(-1)].add((produced * slot_weight[:, :, None]).reshape(-1, D))[:LEN]
    final = hidden + mixture
    return jnp.where(live[:, None], final, 0.0)

def reference(tokens, lengths, expert_ids, route_levels, w_query, w_key, w_value, w_out, attn_gain, query_gain, key_gain, ffn_gain, w_gate, w_up, w_down, cotangent):
    params = (w_query.astype(jnp.float32), w_key.astype(jnp.float32), w_value.astype(jnp.float32), w_out.astype(jnp.float32), attn_gain.astype(jnp.float32), query_gain.astype(jnp.float32), key_gain.astype(jnp.float32), ffn_gain.astype(jnp.float32), w_gate.astype(jnp.float32), w_up.astype(jnp.float32), w_down.astype(jnp.float32))
    count = MICRO * SEQS
    flat_tokens = tokens.reshape(count, LEN, D)
    flat_cot = cotangent.reshape(count, LEN, D)
    flat_len = lengths.reshape(count)
    flat_ids = expert_ids.reshape(count, LEN, TOPK)
    flat_levels = route_levels.reshape(count, LEN, TOPK)

    def one(totals, item):
        seq_tokens, seq_cot, length, chosen, levels = item
        filled = slot_table(chosen)
        level_f = levels.astype(jnp.float32)
        mixing = level_f / lax.optimization_barrier(jnp.sum(level_f, axis=-1, keepdims=True))

        def forward(inputs, weights):
            return sequence_forward(inputs, weights, length, filled, mixing)
        result, pullback = jax.vjp(forward, seq_tokens.astype(jnp.float32), params)
        grad_inputs, grad_params = pullback(seq_cot.astype(jnp.float32))
        totals = jax.tree.map(lambda left, right: left + right, totals, grad_params)
        return (totals, (result.astype(jnp.bfloat16), grad_inputs))
    zeros = jax.tree.map(jnp.zeros_like, params)
    totals, stacked = lax.scan(one, zeros, (flat_tokens, flat_cot, flat_len, flat_ids, flat_levels))
    results, grad_inputs = stacked
    grad_query, grad_key, grad_value, grad_outw, grad_ga, grad_gq, grad_gk, grad_gf, grad_gate, grad_up, grad_down = totals
    return (results.reshape(MICRO, SEQS, LEN, D), grad_inputs.reshape(MICRO, SEQS, LEN, D), grad_query, grad_key, grad_value, grad_outw, grad_ga, grad_gq, grad_gk, grad_gf, grad_gate, grad_up, grad_down)
```

```python
import jax
import jax.numpy as jnp
from jax import lax
from jax.experimental import pallas as pl
from jax.experimental.pallas import tpu as pltpu
from jax.sharding import PartitionSpec as P

HEAD_DIM = 128
EPS = 1e-05
THETA = 10000.0
MASKED = -1e30
LANES = 128
ROOM = 58 << 20

f32 = jnp.float32
bf16 = jnp.bfloat16


def dot(left, right, contract=((1,), (0,))):
    return lax.dot_general(left, right, (contract, ((), ())), preferred_element_type=f32)


def dot_nt(left, right):
    return dot(left, right, ((1,), (1,)))


def dot_tn(left, right):
    return dot(left, right, ((0,), (0,)))


def struct(shape, dtype):
    return jax.ShapeDtypeStruct(shape, dtype)


def cost(flops, *arrays):
    moved = sum(a.size * a.dtype.itemsize for a in arrays)
    return pl.CostEstimate(flops=int(flops), bytes_accessed=int(moved), transcendentals=0)


def whole(array):
    zeros = (0,) * len(array.shape)
    return pl.BlockSpec(array.shape, lambda *_: zeros, pipeline_mode=pl.Buffered(1))


def params(axes):
    return pltpu.CompilerParams(
        dimension_semantics=("arbitrary",) * axes, vmem_limit_bytes=ROOM
    )


def chunks_of(blocks, cap):
    parts = max(1, (blocks * cap) // 640)
    while blocks % parts:
        parts -= 1
    return parts


def project(pieces, gain, weight):
    count, (rows, width) = len(pieces), pieces[0].shape
    third = weight.shape[1] // 3
    total = count * rows
    step = 32
    part = min(total, 512)

    def kernel(*refs):
        xs, (gain_ref, w_ref), (n_ref, out_ref, ss_ref) = (
            refs[:count],
            refs[count : count + 2],
            refs[count + 2 :],
        )

        @pl.when(pl.program_id(0) == 0)
        def _():
            for i in range(count):

                @pl.loop(0, rows // step)
                def _(k):
                    v = xs[i][pl.ds(k * step, step), :].astype(f32)
                    r = lax.rsqrt(jnp.mean(v * v, axis=-1, keepdims=True) + EPS)
                    n_ref[pl.ds(i * rows + k * step, step), :] = (v * r * gain_ref[...]).astype(
                        bf16
                    )

        @pl.loop(0, total // part)
        def _(k):
            at = pl.ds(pl.multiple_of(k * part, part), part)
            p = dot(n_ref[at, :], w_ref[...])
            out_ref[at, :] = p
            ss_ref[0, at, :] = jnp.sum(p * p, axis=-1, keepdims=True)

    outs = (
        struct((total, width), bf16),
        struct((total, 3 * third), f32),
        struct((3, total, 1), f32),
    )
    return pl.pallas_call(
        kernel,
        grid=(3,),
        in_specs=[whole(x) for x in pieces]
        + [whole(gain), pl.BlockSpec((width, third), lambda t: (0, t))],
        out_specs=(
            pl.BlockSpec((total, width), lambda t: (0, 0)),
            pl.BlockSpec((total, third), lambda t: (0, t)),
            pl.BlockSpec((1, total, 1), lambda t: (t, 0, 0)),
        ),
        out_shape=outs,
        compiler_params=params(1),
        cost_estimate=cost(2 * total * width * 3 * third, *pieces, weight, *outs[:2]),
        name="project",
    )(*pieces, gain, weight)


def turn(v, cosines, sines):
    return v * cosines + pltpu.roll(v, HEAD_DIM // 2, 1) * sines


def turn_back(v, cosines, sines):
    return v * cosines + pltpu.roll(v * sines, HEAD_DIM // 2, 1)


def allowed_of(start, rows, count, length):
    row = start + lax.broadcasted_iota(jnp.int32, (rows, count), 0)
    col = lax.broadcasted_iota(jnp.int32, (rows, count), 1)
    return (col <= row) & (col < length)


def attention_forward(place, lengths, qkv, inverse, gains, cosines, sines):
    n, seqs, rows, wide = qkv.shape
    cols = wide // 3
    heads = cols // HEAD_DIM
    span = n * rows
    scale = HEAD_DIM ** (-0.5)

    def kernel(place_ref, len_ref, qi, ki, vi, inv, gain_ref, cos_ref, sin_ref, q_o, k_o, v_o, att, lse):
        here = place_ref[0]
        length = len_ref[pl.program_id(0)]
        for p in range(n):
            j = lax.rem(here + (n - p), n)
            at = slice(p * rows, (p + 1) * rows)
            for which, (src, dst) in enumerate(((qi, q_o), (ki, k_o))):
                z = src[j, 0] * inv[which, j, 0] * gain_ref[which]
                dst[0, at, :] = turn(z, cos_ref[p], sin_ref[p]).astype(bf16)
            v_o[0, at, :] = vi[j, 0].astype(bf16)
        for p in range(n):
            at = slice(p * rows, (p + 1) * rows)
            kv = (p + 1) * rows
            s = dot_nt(q_o[0, at, :], k_o[0, :kv, :]) * scale
            s = jnp.where(allowed_of(p * rows, rows, kv, length), s, MASKED)
            peak = jnp.max(s, axis=-1, keepdims=True)
            e = jnp.exp(s - peak)
            z = jnp.sum(e, axis=-1, keepdims=True)
            att[p, 0] = dot((e / z).astype(bf16), v_o[0, :kv, :]).astype(bf16)
            lse[0, 0, at, :] = peak + jnp.log(z)

    def part(k):
        return pl.BlockSpec((n, 1, rows, HEAD_DIM), lambda g, h, *_: (0, g, 0, k * heads + h))

    line = pl.BlockSpec((1, span, HEAD_DIM), lambda g, h, *_: (g, 0, h))
    outs = (struct((seqs, span, cols), bf16),) * 3 + (
        struct((n, seqs, rows, cols), bf16),
        struct((seqs, heads, span, 1), f32),
    )
    return pl.pallas_call(
        kernel,
        grid_spec=pltpu.PrefetchScalarGridSpec(
            num_scalar_prefetch=2,
            grid=(seqs, heads),
            in_specs=[
                part(0),
                part(1),
                part(2),
                pl.BlockSpec((2, n, 1, rows, 1), lambda g, h, *_: (0, 0, g, 0, 0)),
                pl.BlockSpec((2, 1, HEAD_DIM), lambda g, h, *_: (0, 0, h)),
                whole(cosines),
                whole(sines),
            ],
            out_specs=(
                line,
                line,
                line,
                pl.BlockSpec((n, 1, rows, HEAD_DIM), lambda g, h, *_: (0, g, 0, h)),
                pl.BlockSpec((1, 1, span, 1), lambda g, h, *_: (g, h, 0, 0)),
            ),
        ),
        out_shape=outs,
        compiler_params=params(2),
        cost_estimate=cost(3 * seqs * heads * span * span * HEAD_DIM, qkv, *outs[:4]),
        name="attention",
    )(place, lengths, qkv, qkv, qkv, inverse, gains, cosines, sines)


def attention_backward(place, lengths, q, k, v, grad, lse, qkv, inverse, gains, cosines, sines):
    n, seqs, rows, wide = qkv.shape
    cols = wide // 3
    heads = cols // HEAD_DIM
    span = n * rows
    scale = HEAD_DIM ** (-0.5)

    def kernel(
        place_ref, len_ref, q_i, k_i, v_i, do_i, lse_i, qp_i, kp_i, inv, gain_ref, cos_ref, sin_ref,
        dq_o, dk_o, dv_o, st_o, dg_o, dq_s, dk_s, dv_s,
    ):
        here = place_ref[0]
        length = len_ref[pl.program_id(0)]
        dk_s[...] = jnp.zeros_like(dk_s)
        dv_s[...] = jnp.zeros_like(dv_s)
        for p in range(n):
            at = slice(p * rows, (p + 1) * rows)
            kv = (p + 1) * rows
            query, keys, values, do = q_i[0, at, :], k_i[0, :kv, :], v_i[0, :kv, :], do_i[p, 0]
            s = dot_nt(query, keys) * scale
            probs = jnp.where(
                allowed_of(p * rows, rows, kv, length), jnp.exp(s - lse_i[0, 0, at, :]), 0.0
            )
            dp = dot_nt(do, values)
            ds = (probs * (dp - jnp.sum(probs * dp, axis=-1, keepdims=True))).astype(bf16)
            dq_s[at, :] = dot(ds, keys) * scale
            dk_s[:kv, :] += dot_tn(ds, query)
            dv_s[:kv, :] += dot_tn(probs.astype(bf16), do)
        dk_s[...] = dk_s[...] * scale
        sums = [jnp.zeros((1, HEAD_DIM), f32)] * 2
        for p in range(n):
            j = lax.rem(here + (n - p), n)
            at = slice(p * rows, (p + 1) * rows)
            for which, (src, raw, dst) in enumerate(((dq_s, qp_i, dq_o), (dk_s, kp_i, dk_o))):
                dz = turn_back(src[at, :], cos_ref[p], sin_ref[p])
                moved = raw[j, 0] * dz
                dst[j, 0] = dz
                st_o[which, 0, 0, j] = jnp.sum(moved * gain_ref[which], axis=-1, keepdims=True)
                sums[which] += jnp.sum(moved * inv[which, j, 0], axis=0, keepdims=True)
            dv_o[j, 0] = dv_s[at, :].astype(bf16)
        for which in range(2):
            dg_o[which, 0] = sums[which]

    def part(i):
        return pl.BlockSpec((n, 1, rows, HEAD_DIM), lambda g, h, *_: (0, g, 0, i * heads + h))

    line = pl.BlockSpec((1, span, HEAD_DIM), lambda g, h, *_: (g, 0, h))
    block = part(0)
    outs = (
        struct((n, seqs, rows, cols), f32),
        struct((n, seqs, rows, cols), f32),
        struct((n, seqs, rows, cols), bf16),
        struct((2, seqs, heads, n, rows, 1), f32),
        struct((2, seqs, 1, cols), f32),
    )
    return pl.pallas_call(
        kernel,
        grid_spec=pltpu.PrefetchScalarGridSpec(
            num_scalar_prefetch=2,
            grid=(seqs, heads),
            in_specs=[
                line,
                line,
                line,
                block,
                pl.BlockSpec((1, 1, span, 1), lambda g, h, *_: (g, h, 0, 0)),
                part(0),
                part(1),
                pl.BlockSpec((2, n, 1, rows, 1), lambda g, h, *_: (0, 0, g, 0, 0)),
                pl.BlockSpec((2, 1, HEAD_DIM), lambda g, h, *_: (0, 0, h)),
                whole(cosines),
                whole(sines),
            ],
            out_specs=(
                block,
                block,
                block,
                pl.BlockSpec((2, 1, 1, n, rows, 1), lambda g, h, *_: (0, g, h, 0, 0, 0)),
                pl.BlockSpec((2, 1, 1, HEAD_DIM), lambda g, h, *_: (0, g, 0, h)),
            ),
            scratch_shapes=[pltpu.VMEM((span, HEAD_DIM), f32)] * 3,
        ),
        out_shape=outs,
        compiler_params=params(2),
        cost_estimate=cost(7 * seqs * heads * span * span * HEAD_DIM, qkv, *outs[:3]),
        name="attention_back",
    )(place, lengths, q, k, v, grad, lse, qkv, qkv, inverse, gains, cosines, sines)


def picks(rank_ref, nb, cap):
    row = rank_ref[0, nb : nb + 1, :]
    return lax.broadcasted_iota(jnp.int32, (cap, row.shape[1]), 0) == row


def slot_weight(hot, coef_ref, nb):
    return jnp.sum(jnp.where(hot, coef_ref[0, nb : nb + 1, :], 0.0), axis=-1, keepdims=True)


def expert_forward(pieces, rank, gate_up, cap):
    experts, blocks, rows = rank.shape
    width, hidden = gate_up.shape[1:]
    slots = blocks * cap
    tile = min(256, hidden)
    parts = chunks_of(blocks, cap)
    part = slots // parts

    def kernel(*refs):
        xs, (rank_ref, wg, wu), (x_o, g_o, u_o, a_o) = (
            refs[:blocks],
            refs[blocks : blocks + 3],
            refs[blocks + 3 :],
        )

        @pl.when(pl.program_id(1) == 0)
        def _():
            for nb in range(blocks):
                hot = picks(rank_ref, nb, cap).astype(bf16)
                x_o[0, nb * cap : (nb + 1) * cap, :] = dot(hot, xs[nb][...]).astype(bf16)

        @pl.loop(0, parts)
        def _(i):
            at = pl.ds(pl.multiple_of(i * part, part), part)
            x = x_o[0, at, :]
            gate = dot(x, wg[0])
            upper = dot(x, wu[0])
            g_o[0, at, :] = gate.astype(bf16)
            u_o[0, at, :] = upper.astype(bf16)
            a_o[0, at, :] = (gate * jax.nn.sigmoid(gate) * upper).astype(bf16)

    tiled = pl.BlockSpec((1, slots, tile), lambda e, f: (e, 0, f))
    outs = (struct((experts, slots, width), bf16),) + (struct((experts, slots, hidden), bf16),) * 3
    return pl.pallas_call(
        kernel,
        grid=(experts, hidden // tile),
        in_specs=[whole(x) for x in pieces]
        + [
            pl.BlockSpec((1, blocks, rows), lambda e, f: (e, 0, 0)),
            pl.BlockSpec((1, width, tile), lambda e, f: (e, 0, f)),
            pl.BlockSpec((1, width, tile), lambda e, f: (experts + e, 0, f)),
        ],
        out_specs=(pl.BlockSpec((1, slots, width), lambda e, f: (e, 0, 0)), tiled, tiled, tiled),
        out_shape=outs,
        compiler_params=params(2),
        cost_estimate=cost(4 * experts * slots * width * hidden, *pieces, gate_up, *outs),
        name="expert_forward",
    )(*pieces, rank, gate_up, gate_up)


def expert_output(active, rank, coef, down, cap):
    experts, blocks, rows = rank.shape
    hidden, width = down.shape[1:]
    slots = blocks * cap
    tile = min(512, width)
    parts = chunks_of(blocks, cap)
    per = blocks // parts

    def kernel(a_i, rank_ref, coef_ref, wd, *rest):
        outs, acc = rest[:blocks], rest[blocks]
        e = pl.program_id(1)

        @pl.when(e == 0)
        def _():
            acc[...] = jnp.zeros_like(acc)

        for i in range(parts):
            y = dot(a_i[0, i * per * cap : (i + 1) * per * cap, :], wd[0])
            for m in range(per):
                nb = i * per + m
                hot = picks(rank_ref, nb, cap)
                weighed = y[m * cap : (m + 1) * cap, :] * slot_weight(hot, coef_ref, nb)
                acc[nb] += dot_tn(hot.astype(bf16), weighed.astype(bf16))

        @pl.when(e == experts - 1)
        def _():
            for nb in range(blocks):
                outs[nb][...] = acc[nb].astype(bf16)

    table = pl.BlockSpec((1, blocks, rows), lambda d, e: (e, 0, 0))
    outs = (struct((rows, width), bf16),) * blocks
    return pl.pallas_call(
        kernel,
        grid=(width // tile, experts),
        in_specs=[
            pl.BlockSpec((1, slots, hidden), lambda d, e: (e, 0, 0)),
            table,
            table,
            pl.BlockSpec((1, hidden, tile), lambda d, e: (e, 0, d)),
        ],
        out_specs=(pl.BlockSpec((rows, tile), lambda d, e: (0, d)),) * blocks,
        out_shape=outs,
        scratch_shapes=[pltpu.VMEM((blocks, rows, tile), f32)],
        compiler_params=params(2),
        cost_estimate=cost(2 * experts * slots * width * hidden, active, down, *outs),
        name="expert_output",
    )(active, rank, coef, down)


def expert_backward(pieces, rank, coef, down, gate, upper, active, cap):
    experts, blocks, rows = rank.shape
    hidden, width = down.shape[1:]
    slots = blocks * cap
    tile = min(256, hidden)
    parts = chunks_of(blocks, cap)
    part = slots // parts

    def kernel(*refs):
        ds, (rank_ref, coef_ref, wd, g_i, u_i, a_i), (dg_o, du_o, dw_o, dy) = (
            refs[:blocks],
            refs[blocks : blocks + 6],
            refs[blocks + 6 :],
        )

        @pl.when(pl.program_id(1) == 0)
        def _():
            for nb in range(blocks):
                hot = picks(rank_ref, nb, cap)
                picked = dot(hot.astype(bf16), ds[nb][...])
                dy[nb * cap : (nb + 1) * cap, :] = (
                    picked * slot_weight(hot, coef_ref, nb)
                ).astype(bf16)

        @pl.loop(0, parts)
        def _(i):
            at = pl.ds(pl.multiple_of(i * part, part), part)
            da = dot_nt(dy[at, :], wd[0])
            g = g_i[0, at, :].astype(f32)
            s = jax.nn.sigmoid(g)
            du_o[0, at, :] = (da * g * s).astype(bf16)
            dg_o[0, at, :] = (
                da * u_i[0, at, :].astype(f32) * s * (1.0 + g * (1.0 - s))
            ).astype(bf16)

        dw_o[0] = dot_tn(a_i[0], dy[...]).astype(bf16)

    table = pl.BlockSpec((1, blocks, rows), lambda e, f: (e, 0, 0))
    tiled = pl.BlockSpec((1, slots, tile), lambda e, f: (e, 0, f))
    line = pl.BlockSpec((1, tile, width), lambda e, f: (e, f, 0))
    outs = (struct((experts, slots, hidden), bf16),) * 2 + (struct((experts, hidden, width), bf16),)
    return pl.pallas_call(
        kernel,
        grid=(experts, hidden // tile),
        in_specs=[whole(x) for x in pieces] + [table, table, line, tiled, tiled, tiled],
        out_specs=(tiled, tiled, line),
        out_shape=outs,
        scratch_shapes=[pltpu.VMEM((slots, width), bf16)],
        compiler_params=params(2),
        cost_estimate=cost(
            4 * experts * slots * width * hidden, *pieces, down, gate, upper, active, *outs
        ),
        name="expert_backward",
    )(*pieces, rank, coef, down, gate, upper, active)


def expert_input_grad(dgate, dupper, rank, gate_up, cap):
    experts, blocks, rows = rank.shape
    width, hidden = gate_up.shape[1:]
    slots = blocks * cap
    tile = min(512, width)
    parts = chunks_of(blocks, cap)
    per = blocks // parts

    def kernel(dg_i, du_i, rank_ref, wg, wu, *rest):
        outs, acc = rest[:blocks], rest[blocks]
        e = pl.program_id(1)

        @pl.when(e == 0)
        def _():
            acc[...] = jnp.zeros_like(acc)

        for i in range(parts):
            at = slice(i * per * cap, (i + 1) * per * cap)
            dx = (dot_nt(dg_i[0, at, :], wg[0]) + dot_nt(du_i[0, at, :], wu[0])).astype(bf16)
            for m in range(per):
                nb = i * per + m
                hot = picks(rank_ref, nb, cap).astype(bf16)
                acc[nb] += dot_tn(hot, dx[m * cap : (m + 1) * cap, :])

        @pl.when(e == experts - 1)
        def _():
            for nb in range(blocks):
                outs[nb][...] = acc[nb].astype(bf16)

    line = pl.BlockSpec((1, slots, hidden), lambda d, e: (e, 0, 0))
    outs = (struct((rows, width), bf16),) * blocks
    return pl.pallas_call(
        kernel,
        grid=(width // tile, experts),
        in_specs=[
            line,
            line,
            pl.BlockSpec((1, blocks, rows), lambda d, e: (e, 0, 0)),
            pl.BlockSpec((1, tile, hidden), lambda d, e: (e, d, 0)),
            pl.BlockSpec((1, tile, hidden), lambda d, e: (experts + e, d, 0)),
        ],
        out_specs=(pl.BlockSpec((rows, tile), lambda d, e: (0, d)),) * blocks,
        out_shape=outs,
        scratch_shapes=[pltpu.VMEM((blocks, rows, tile), f32)],
        compiler_params=params(2),
        cost_estimate=cost(4 * experts * slots * width * hidden, dgate, dupper, gate_up, *outs),
        name="expert_input_grad",
    )(dgate, dupper, rank, gate_up, gate_up)


def expert_weight_grad(x, dgate, dupper):
    experts, slots, width = x.shape
    hidden = dgate.shape[2]
    tile = min(256, width)

    def kernel(x_i, dg_i, du_i, o):
        o[0, 0] = dot_tn(x_i[0], dg_i[0]).astype(bf16)
        o[1, 0] = dot_tn(x_i[0], du_i[0]).astype(bf16)

    line = pl.BlockSpec((1, slots, hidden), lambda e, d: (e, 0, 0))
    out = struct((2, experts, width, hidden), bf16)
    return pl.pallas_call(
        kernel,
        grid=(experts, width // tile),
        in_specs=[pl.BlockSpec((1, slots, tile), lambda e, d: (e, 0, d)), line, line],
        out_specs=pl.BlockSpec((2, 1, tile, hidden), lambda e, d: (0, e, d, 0)),
        out_shape=out,
        compiler_params=params(2),
        cost_estimate=cost(4 * experts * slots * width * hidden, x, dgate, dupper, out),
        name="expert_weight_grad",
    )(x, dgate, dupper).reshape(2 * experts, width, hidden)


def tables(positions):
    half = HEAD_DIM // 2
    inverse = THETA ** (-(jnp.arange(half, dtype=f32) * 2.0) / HEAD_DIM)
    angle = positions.astype(f32)[:, None] * inverse[None, :]
    cosines, sines = jnp.cos(angle), jnp.sin(angle)
    return (
        jnp.concatenate([cosines, cosines], axis=-1),
        jnp.concatenate([-sines, sines], axis=-1),
    )


def norm_back(v, gain, dz):
    r = lax.rsqrt(jnp.mean(v * v, axis=-1, keepdims=True) + EPS)
    moved = dz * gain
    return r * moved - v * (r * r * r) * jnp.mean(v * moved, axis=-1, keepdims=True), dz * v * r


def body(
    tokens, lengths, expert_ids, route_levels, w_query, w_key, w_value, w_out,
    attn_gain, query_gain, key_gain, ffn_gain, w_gate, w_up, w_down, cotangent,
):
    batches, sequences, rows, width = tokens.shape
    top = expert_ids.shape[-1]
    experts = w_gate.shape[0]
    n = lax.axis_size("ctx")
    groups = lax.axis_size("batch")
    here = lax.axis_index("ctx")
    seqs = batches * sequences
    cols = width // n
    own = w_query.shape[0]
    cap = rows * top * 5 // (4 * experts * n)
    cap = -(-cap // 16) * 16
    blocks = n * seqs
    up = [(i, (i + 1) % n) for i in range(n)]
    place = here.reshape(1).astype(jnp.int32)

    def gather_ring(piece):
        held = [piece]
        for _ in range(n - 1):
            held.append(lax.ppermute(held[-1], "ctx", up))
        return held

    def reduce_ring(parts):
        total = parts[1 % n]
        for j in range(2, n + 1):
            moved = lax.ppermute(total, "ctx", up).astype(f32) + parts[j % n].astype(f32)
            total = moved.astype(bf16) if j < n else moved
        return total

    def ctx_sum(x):
        total = x
        for k in range(1, n):
            got = lax.ppermute(x, "ctx", [(i, (i + k) % n) for i in range(n)])
            total = total + jnp.roll(got, k, axis=0)
        return total

    def to_owner(summed):
        pieces = summed.reshape(n, own, summed.shape[-1])
        return lax.all_to_all(pieces, "ctx", split_axis=0, concat_axis=0, tiled=True)

    mine = jnp.concatenate(
        [jnp.swapaxes(w.reshape(own, n, cols), 0, 1) for w in (w_query, w_key, w_value)], axis=2
    )
    mine = lax.all_to_all(mine, "ctx", split_axis=0, concat_axis=0, tiled=True)
    qkv_w = lax.all_gather(mine.reshape(n * own, 3 * cols), "batch", axis=0, tiled=True)
    gain_attn, gain_query, gain_key, gain_ffn = (
        lax.all_gather(g, ("batch", "ctx"), axis=0, tiled=True).astype(f32)
        for g in (attn_gain, query_gain, key_gain, ffn_gain)
    )
    out_w = lax.all_gather(w_out, ("batch", "ctx"), axis=0, tiled=True).reshape(n, cols, width)
    gate_up = lax.all_gather(
        jnp.concatenate([w_gate, w_up], axis=0), "batch", axis=1, tiled=True
    )
    down = lax.all_gather(w_down, "batch", axis=2, tiled=True)
    qk_gains = lax.dynamic_slice_in_dim(
        jnp.stack([gain_query, gain_key]), here * cols, cols, 1
    ).reshape(2, 1, cols)

    xs = tokens.reshape(seqs, rows, width)
    span_len = lengths.reshape(seqs)
    local_pos = here * rows + jnp.arange(rows, dtype=jnp.int32)
    live = (local_pos[None, :] < span_len[:, None])[:, :, None]
    x_rings = [gather_ring(xs[g]) for g in range(seqs)]
    x_pieces = [x_rings[g][j] for j in range(n) for g in range(seqs)]
    grad_low = jnp.where(live, cotangent.reshape(seqs, rows, width), jnp.zeros((), bf16))

    sent = jnp.stack(
        [
            jnp.swapaxes(expert_ids.reshape(seqs, rows, top), 1, 2),
            jnp.swapaxes(route_levels.reshape(seqs, rows, top), 1, 2),
        ]
    )
    routes = lax.all_gather(sent, "ctx", axis=0, tiled=False)
    order = lax.rem(here - jnp.arange(n, dtype=jnp.int32) + n, n)
    routes = jnp.take(routes, order, axis=0)
    chosen = routes[:, 0].reshape(blocks, top, rows)
    levels = routes[:, 1].reshape(blocks, top, rows).astype(f32)
    share = levels / jnp.sum(levels, axis=1, keepdims=True)
    owned = here * experts + jnp.arange(experts, dtype=jnp.int32)
    hit = chosen[None] == owned[:, None, None, None]
    named = jnp.any(hit, axis=2)
    coef = jnp.sum(jnp.where(hit, share[None], 0.0), axis=2)
    upto = (
        jnp.arange(rows, dtype=jnp.int32)[:, None] <= jnp.arange(rows, dtype=jnp.int32)[None, :]
    ).astype(bf16)
    count = jnp.dot(
        named.astype(bf16).reshape(experts * blocks, rows), upto, preferred_element_type=f32
    )
    rank = jnp.where(named, count.reshape(experts, blocks, rows).astype(jnp.int32) - 1, -1)

    cosines, sines = tables(jnp.arange(n * rows, dtype=jnp.int32))
    cosines = cosines.reshape(n, rows, HEAD_DIM)
    sines = sines.reshape(n, rows, HEAD_DIM)
    normed, qkv, squares = project(x_pieces, gain_attn[None, :], qkv_w)
    squares = squares[:2].reshape(2, n, seqs, rows)
    squares = ctx_sum(jnp.swapaxes(squares, 0, 1))
    inverse = lax.rsqrt(squares / width + EPS)
    inverse = jnp.swapaxes(inverse, 0, 1)[..., None]
    qkv = qkv.reshape(n, seqs, rows, 3 * cols)
    q, k, v, att, lse = attention_forward(
        place, span_len, qkv, inverse, qk_gains, cosines, sines
    )
    att = lax.all_to_all(att, "ctx", split_axis=0, concat_axis=0, tiled=True)
    hidden = xs.astype(f32) + jnp.einsum(
        "ngrd,nde->gre", att, out_w, preferred_element_type=f32
    )
    n2 = (
        hidden * lax.rsqrt(jnp.mean(hidden * hidden, axis=-1, keepdims=True) + EPS) * gain_ffn
    ).astype(bf16)

    g_rings = [gather_ring(grad_low[g]) for g in range(seqs)]
    grad_pieces = [g_rings[g][j] for j in range(n) for g in range(seqs)]
    n_rings = [gather_ring(n2[g]) for g in range(seqs)]
    n_pieces = [n_rings[g][j] for j in range(n) for g in range(seqs)]
    slots_x, gate, upper, active = expert_forward(n_pieces, rank, gate_up, cap)
    y_parts = expert_output(active, rank, coef, down, cap)
    mixture = jnp.stack(
        [reduce_ring([y_parts[j * seqs + g] for j in range(n)]) for g in range(seqs)]
    )
    out = jnp.where(live, hidden + mixture, 0.0).astype(bf16)

    dgate, dupper, grad_down = expert_backward(
        grad_pieces, rank, coef, down, gate, upper, active, cap
    )
    grad_down = lax.psum_scatter(grad_down, "batch", scatter_dimension=2, tiled=True)
    dx_parts = expert_input_grad(dgate, dupper, rank, gate_up, cap)
    grad_gu = expert_weight_grad(slots_x, dgate, dupper)
    grad_gu = lax.psum_scatter(grad_gu, "batch", scatter_dimension=1, tiled=True)
    grad_mid = jnp.stack(
        [reduce_ring([dx_parts[j * seqs + g] for j in range(n)]) for g in range(seqs)]
    )
    back, ffn_terms = norm_back(hidden, gain_ffn, grad_mid)
    grad_hidden = grad_low.astype(f32) + back
    ffn_part = jnp.sum(ffn_terms, axis=(0, 1))
    datt = grad_hidden.astype(bf16)

    do = jnp.einsum("gre,nde->ngrd", datt, out_w, preferred_element_type=f32).astype(bf16)
    do = lax.all_to_all(do, "ctx", split_axis=0, concat_axis=0, tiled=True)
    grad_out = jnp.einsum("ngrd,gre->nde", att, datt, preferred_element_type=f32)
    grad_out = grad_out.astype(bf16).reshape(width, width)
    column = jnp.pad(ffn_part.astype(bf16)[:, None], ((0, 0), (0, LANES - 1)))
    grad_out = lax.psum_scatter(
        jnp.concatenate([grad_out, column], axis=1), "batch", scatter_dimension=0, tiled=True
    )
    grad_out = jnp.sum(to_owner(grad_out).astype(f32), axis=0)

    dzq, dzk, dv, stats, qk_part = attention_backward(
        place, span_len, q, k, v, do, lse, qkv, inverse, qk_gains, cosines, sines
    )
    stats = jnp.sum(stats[..., 0], axis=2)
    stats = ctx_sum(jnp.transpose(stats, (2, 0, 1, 3)))
    stats = jnp.swapaxes(stats, 0, 1)[..., None] / width

    def through_norm(which, dz):
        r = inverse[which]
        raw = qkv[..., which * cols : (which + 1) * cols]
        return (r * qk_gains[which] * dz - raw * (r * r * r) * stats[which]).astype(bf16)

    dqkv = jnp.concatenate([through_norm(0, dzq), through_norm(1, dzk), dv], axis=-1)
    dqkv = dqkv.reshape(blocks * rows, 3 * cols)
    dn1 = dot_nt(dqkv, qkv_w).astype(bf16).reshape(n, seqs, rows, width)
    grad_n1 = jnp.stack([reduce_ring([dn1[j, g] for j in range(n)]) for g in range(seqs)])
    back, _ = norm_back(xs.astype(f32), gain_attn, grad_n1)
    grad_tokens = grad_hidden + back

    grad_qkv = dot_tn(normed, dqkv).astype(bf16)
    qk_rows = lax.dynamic_update_slice_in_dim(
        jnp.zeros((2, width), f32), jnp.sum(qk_part, axis=(1, 2)), here * cols, 1
    )
    qk_column = jnp.pad(qk_rows.T.astype(bf16), ((0, 0), (0, LANES - 2)))
    grad_qkv = lax.psum_scatter(
        jnp.concatenate([grad_qkv, qk_column], axis=1), "batch", scatter_dimension=0, tiled=True
    )
    grad_qkv = to_owner(grad_qkv).astype(f32)
    grad_q, grad_k, grad_v = (
        jnp.swapaxes(grad_qkv[:, :, i * cols : (i + 1) * cols], 0, 1).reshape(own, width)
        for i in range(3)
    )
    qk_sums = jnp.sum(grad_qkv[:, :, 3 * cols :], axis=0)
    grad_attn_gain = (
        jnp.sum(
            w_query.astype(f32) * grad_q
            + w_key.astype(f32) * grad_k
            + w_value.astype(f32) * grad_v,
            axis=1,
        )
        / attn_gain.astype(f32)
    )
    shape = (batches, sequences, rows, width)
    return (
        out.reshape(shape),
        grad_tokens.reshape(shape),
        grad_q,
        grad_k,
        grad_v,
        grad_out[:, :width],
        grad_attn_gain,
        qk_sums[:, 0],
        qk_sums[:, 1],
        grad_out[:, width],
        grad_gu[:experts].astype(f32),
        grad_gu[experts:].astype(f32),
        grad_down.astype(f32),
    )


def solution(mesh):
    rows = P(None, "batch", "ctx", None)
    flat = P(("batch", "ctx"), None)
    line = P(("batch", "ctx"))
    wide = P("ctx", "batch", None)
    tall = P("ctx", None, "batch")
    in_specs = (rows, P(None, "batch"), rows, rows) + (flat,) * 4 + (line,) * 4
    in_specs += (wide, wide, tall, rows)
    out_specs = (rows, rows) + (flat,) * 4 + (line,) * 4 + (wide, wide, tall)
    return jax.shard_map(body, mesh=mesh, in_specs=in_specs, out_specs=out_specs, check_vma=False)
```

```python
import jax
import jax.numpy as jnp
from jax import lax
from jax.experimental import pallas as pl
from jax.experimental.pallas import tpu as pltpu
from jax.sharding import PartitionSpec as P

HEAD_DIM = 128
EPS = 1e-05
THETA = 10000.0
MASKED = -1e30
LANES = 128
ROOM = 58 << 20
SLIM = 1

f32 = jnp.float32
bf16 = jnp.bfloat16


def dot(left, right, contract=((1,), (0,))):
    return lax.dot_general(left, right, (contract, ((), ())), preferred_element_type=f32)


def dot_nt(left, right):
    return dot(left, right, ((1,), (1,)))


def dot_tn(left, right):
    return dot(left, right, ((0,), (0,)))


def struct(shape, dtype):
    return jax.ShapeDtypeStruct(shape, dtype)


def cost(flops, *arrays):
    moved = sum(a.size * a.dtype.itemsize for a in arrays)
    return pl.CostEstimate(
        flops=int(flops) // SLIM, bytes_accessed=int(moved) // SLIM, transcendentals=0
    )


def whole(array):
    zeros = (0,) * len(array.shape)
    return pl.BlockSpec(array.shape, lambda *_: zeros, pipeline_mode=pl.Buffered(1))


def params(axes):
    return pltpu.CompilerParams(
        dimension_semantics=("arbitrary",) * axes, vmem_limit_bytes=ROOM
    )


def chunks_of(blocks, cap):
    parts = max(1, (blocks * cap) // 640)
    while blocks % parts:
        parts -= 1
    return parts


def project(pieces, gain, weight, third, first):
    count, (rows, width) = len(pieces), pieces[0].shape
    total = count * rows
    step = 32
    part = min(total, 512)

    def kernel(*refs):
        xs, (gain_ref, w_ref), (n_ref, out_ref, ss_ref) = (
            refs[:count],
            refs[count : count + 2],
            refs[count + 2 :],
        )

        @pl.when(pl.program_id(0) == 0)
        def _():
            for i in range(count):

                @pl.loop(0, rows // step)
                def _(k):
                    v = xs[i][pl.ds(k * step, step), :].astype(f32)
                    r = lax.rsqrt(jnp.mean(v * v, axis=-1, keepdims=True) + EPS)
                    n_ref[pl.ds(i * rows + k * step, step), :] = (v * r * gain_ref[...]).astype(
                        bf16
                    )

        @pl.loop(0, total // part)
        def _(k):
            at = pl.ds(pl.multiple_of(k * part, part), part)
            p = dot(n_ref[at, :], w_ref[...])
            out_ref[at, :] = p
            ss_ref[0, at, :] = jnp.sum(p * p, axis=-1, keepdims=True)

    outs = (
        struct((total, width), bf16),
        struct((total, 3 * third), f32),
        struct((3, total, 1), f32),
    )
    return pl.pallas_call(
        kernel,
        grid=(3,),
        in_specs=[whole(x) for x in pieces]
        + [whole(gain), pl.BlockSpec((width, third), lambda t: (0, first + t))],
        out_specs=(
            pl.BlockSpec((total, width), lambda t: (0, 0)),
            pl.BlockSpec((total, third), lambda t: (0, t)),
            pl.BlockSpec((1, total, 1), lambda t: (t, 0, 0)),
        ),
        out_shape=outs,
        compiler_params=params(1),
        cost_estimate=cost(2 * total * width * 3 * third, *pieces, *outs[:2]),
        name="project",
    )(*pieces, gain, weight)


def turn(v, cosines, sines):
    return v * cosines + pltpu.roll(v, HEAD_DIM // 2, 1) * sines


def turn_back(v, cosines, sines):
    return v * cosines + pltpu.roll(v * sines, HEAD_DIM // 2, 1)


def allowed_of(start, rows, count, length):
    row = start + lax.broadcasted_iota(jnp.int32, (rows, count), 0)
    col = lax.broadcasted_iota(jnp.int32, (rows, count), 1)
    return (col <= row) & (col < length)


def attention_forward(place, lengths, qkv, inverse, gains, cosines, sines):
    n, seqs, rows, wide = qkv.shape
    cols = wide // 3
    heads = cols // HEAD_DIM
    span = n * rows
    scale = HEAD_DIM ** (-0.5)

    def kernel(place_ref, len_ref, qi, ki, vi, inv, gain_ref, cos_ref, sin_ref, q_o, k_o, v_o, att, lse):
        here = place_ref[0]
        length = len_ref[pl.program_id(0)]
        for p in range(n):
            j = lax.rem(here + (n - p), n)
            at = slice(p * rows, (p + 1) * rows)
            for which, (src, dst) in enumerate(((qi, q_o), (ki, k_o))):
                z = src[j, 0] * inv[which, j, 0] * gain_ref[which]
                dst[0, at, :] = turn(z, cos_ref[p], sin_ref[p]).astype(bf16)
            v_o[0, at, :] = vi[j, 0].astype(bf16)
        for p in range(n):
            at = slice(p * rows, (p + 1) * rows)
            kv = (p + 1) * rows
            s = dot_nt(q_o[0, at, :], k_o[0, :kv, :]) * scale
            s = jnp.where(allowed_of(p * rows, rows, kv, length), s, MASKED)
            peak = jnp.max(s, axis=-1, keepdims=True)
            e = jnp.exp(s - peak)
            z = jnp.sum(e, axis=-1, keepdims=True)
            att[p, 0] = dot((e / z).astype(bf16), v_o[0, :kv, :]).astype(bf16)
            lse[0, 0, at, :] = peak + jnp.log(z)

    def part(k):
        return pl.BlockSpec((n, 1, rows, HEAD_DIM), lambda g, h, *_: (0, g, 0, k * heads + h))

    line = pl.BlockSpec((1, span, HEAD_DIM), lambda g, h, *_: (g, 0, h))
    outs = (struct((seqs, span, cols), bf16),) * 3 + (
        struct((n, seqs, rows, cols), bf16),
        struct((seqs, heads, span, 1), f32),
    )
    return pl.pallas_call(
        kernel,
        grid_spec=pltpu.PrefetchScalarGridSpec(
            num_scalar_prefetch=2,
            grid=(seqs, heads),
            in_specs=[
                part(0),
                part(1),
                part(2),
                pl.BlockSpec((2, n, 1, rows, 1), lambda g, h, *_: (0, 0, g, 0, 0)),
                pl.BlockSpec((2, 1, HEAD_DIM), lambda g, h, *_: (0, 0, h)),
                whole(cosines),
                whole(sines),
            ],
            out_specs=(
                line,
                line,
                line,
                pl.BlockSpec((n, 1, rows, HEAD_DIM), lambda g, h, *_: (0, g, 0, h)),
                pl.BlockSpec((1, 1, span, 1), lambda g, h, *_: (g, h, 0, 0)),
            ),
        ),
        out_shape=outs,
        compiler_params=params(2),
        cost_estimate=cost(3 * seqs * heads * span * span * HEAD_DIM, qkv, *outs[:4]),
        name="attention",
    )(place, lengths, qkv, qkv, qkv, inverse, gains, cosines, sines)


def attention_backward(place, lengths, q, k, v, grad, lse, qkv, inverse, gains, cosines, sines):
    n, seqs, rows, wide = qkv.shape
    cols = wide // 3
    heads = cols // HEAD_DIM
    span = n * rows
    scale = HEAD_DIM ** (-0.5)

    def kernel(
        place_ref, len_ref, q_i, k_i, v_i, do_i, lse_i, qp_i, kp_i, inv, gain_ref, cos_ref, sin_ref,
        dq_o, dk_o, dv_o, st_o, dg_o, dq_s, dk_s, dv_s,
    ):
        here = place_ref[0]
        length = len_ref[pl.program_id(0)]
        dk_s[...] = jnp.zeros_like(dk_s)
        dv_s[...] = jnp.zeros_like(dv_s)
        for p in range(n):
            at = slice(p * rows, (p + 1) * rows)
            kv = (p + 1) * rows
            query, keys, values, do = q_i[0, at, :], k_i[0, :kv, :], v_i[0, :kv, :], do_i[p, 0]
            s = dot_nt(query, keys) * scale
            probs = jnp.where(
                allowed_of(p * rows, rows, kv, length), jnp.exp(s - lse_i[0, 0, at, :]), 0.0
            )
            dp = dot_nt(do, values)
            ds = (probs * (dp - jnp.sum(probs * dp, axis=-1, keepdims=True))).astype(bf16)
            dq_s[at, :] = dot(ds, keys) * scale
            dk_s[:kv, :] += dot_tn(ds, query)
            dv_s[:kv, :] += dot_tn(probs.astype(bf16), do)
        dk_s[...] = dk_s[...] * scale
        sums = [jnp.zeros((1, HEAD_DIM), f32)] * 2
        for p in range(n):
            j = lax.rem(here + (n - p), n)
            at = slice(p * rows, (p + 1) * rows)
            for which, (src, raw, dst) in enumerate(((dq_s, qp_i, dq_o), (dk_s, kp_i, dk_o))):
                dz = turn_back(src[at, :], cos_ref[p], sin_ref[p])
                moved = raw[j, 0] * dz
                dst[j, 0] = dz
                st_o[which, 0, 0, j] = jnp.sum(moved * gain_ref[which], axis=-1, keepdims=True)
                sums[which] += jnp.sum(moved * inv[which, j, 0], axis=0, keepdims=True)
            dv_o[j, 0] = dv_s[at, :].astype(bf16)
        for which in range(2):
            dg_o[which, 0] = sums[which]

    def part(i):
        return pl.BlockSpec((n, 1, rows, HEAD_DIM), lambda g, h, *_: (0, g, 0, i * heads + h))

    line = pl.BlockSpec((1, span, HEAD_DIM), lambda g, h, *_: (g, 0, h))
    block = part(0)
    outs = (
        struct((n, seqs, rows, cols), f32),
        struct((n, seqs, rows, cols), f32),
        struct((n, seqs, rows, cols), bf16),
        struct((2, seqs, heads, n, rows, 1), f32),
        struct((2, seqs, 1, cols), f32),
    )
    return pl.pallas_call(
        kernel,
        grid_spec=pltpu.PrefetchScalarGridSpec(
            num_scalar_prefetch=2,
            grid=(seqs, heads),
            in_specs=[
                line,
                line,
                line,
                block,
                pl.BlockSpec((1, 1, span, 1), lambda g, h, *_: (g, h, 0, 0)),
                part(0),
                part(1),
                pl.BlockSpec((2, n, 1, rows, 1), lambda g, h, *_: (0, 0, g, 0, 0)),
                pl.BlockSpec((2, 1, HEAD_DIM), lambda g, h, *_: (0, 0, h)),
                whole(cosines),
                whole(sines),
            ],
            out_specs=(
                block,
                block,
                block,
                pl.BlockSpec((2, 1, 1, n, rows, 1), lambda g, h, *_: (0, g, h, 0, 0, 0)),
                pl.BlockSpec((2, 1, 1, HEAD_DIM), lambda g, h, *_: (0, g, 0, h)),
            ),
            scratch_shapes=[pltpu.VMEM((span, HEAD_DIM), f32)] * 3,
        ),
        out_shape=outs,
        compiler_params=params(2),
        cost_estimate=cost(7 * seqs * heads * span * span * HEAD_DIM, qkv, *outs[:3]),
        name="attention_back",
    )(place, lengths, q, k, v, grad, lse, qkv, qkv, inverse, gains, cosines, sines)


def back_project(dzq, dzk, dv, qkv, inverse, stats, gains, weight, first, pieces):
    total, third = dv.shape
    width = weight.shape[0]
    rows = total // pieces
    tile = min(512, width)

    def kernel(dzq_i, dzk_i, dv_i, q_i, k_i, inv, st, gain_ref, wq, wk, wv, *rest):
        outs, low = rest[:pieces], rest[pieces]

        @pl.when(pl.program_id(0) == 0)
        def _():
            for which, (dz, raw) in enumerate(((dzq_i, q_i), (dzk_i, k_i))):
                r = inv[which]
                low[:, which * third : (which + 1) * third] = (
                    r * (gain_ref[which] * dz[...]) - raw[...] * (r * r * r * st[which])
                ).astype(bf16)
            low[:, 2 * third :] = dv_i[...]

        for i in range(pieces):
            at = slice(i * rows, (i + 1) * rows)
            outs[i][...] = (
                dot_nt(low[at, :third], wq[...])
                + dot_nt(low[at, third : 2 * third], wk[...])
                + dot_nt(low[at, 2 * third :], wv[...])
            ).astype(bf16)

    def raw(k):
        return pl.BlockSpec((total, third), lambda d: (0, k))

    def taken(k):
        return pl.BlockSpec((tile, third), lambda d: (d, first + k))

    outs = (struct((rows, width), bf16),) * pieces + (struct((total, 3 * third), bf16),)
    return pl.pallas_call(
        kernel,
        grid=(width // tile,),
        in_specs=[whole(dzq), whole(dzk), whole(dv), raw(0), raw(1)]
        + [whole(inverse), whole(stats), whole(gains), taken(0), taken(1), taken(2)],
        out_specs=(pl.BlockSpec((rows, tile), lambda d: (0, d)),) * pieces
        + (pl.BlockSpec((total, 3 * third), lambda d: (0, 0)),),
        out_shape=outs,
        compiler_params=params(1),
        cost_estimate=cost(6 * total * width * third, dzq, dzk, dv, *outs),
        name="back_project",
    )(dzq, dzk, dv, qkv, qkv, inverse, stats, gains, weight, weight, weight)


def out_project(att, rows_in, weight, gain):
    n, rows, cols = att.shape
    width = n * cols

    def kernel(a_i, x_i, w_i, gain_ref, h_o, n_o, acc):
        p = pl.program_id(0)

        @pl.when(p == 0)
        def _():
            acc[...] = x_i[...].astype(f32)

        acc[...] += dot(a_i[0], w_i[...])

        @pl.when(p == n - 1)
        def _():
            h = acc[...]
            h_o[...] = h
            r = lax.rsqrt(jnp.mean(h * h, axis=-1, keepdims=True) + EPS)
            n_o[...] = (h * r * gain_ref[...]).astype(bf16)

    outs = (struct((rows, width), f32), struct((rows, width), bf16))
    return pl.pallas_call(
        kernel,
        grid=(n,),
        in_specs=[
            pl.BlockSpec((1, rows, cols), lambda p: (p, 0, 0)),
            whole(rows_in),
            pl.BlockSpec((cols, width), lambda p: (p, 0)),
            whole(gain),
        ],
        out_specs=(pl.BlockSpec((rows, width), lambda p: (0, 0)),) * 2,
        out_shape=outs,
        scratch_shapes=[pltpu.VMEM((rows, width), f32)],
        compiler_params=params(1),
        cost_estimate=cost(2 * rows * width * width, att, rows_in, *outs),
        name="out_project",
    )(att, rows_in, weight, gain)


def out_back(moved, part, low, hidden, gain, weight, n):
    rows, width = hidden.shape
    cols = width // n

    def kernel(m_i, p_i, l_i, h_i, gain_ref, w_i, gh_o, da_o, do_o, fg_o):
        @pl.when(pl.program_id(0) == 0)
        def _():
            dz = m_i[...].astype(f32) + p_i[...].astype(f32)
            v = h_i[...]
            r = lax.rsqrt(jnp.mean(v * v, axis=-1, keepdims=True) + EPS)
            fg_o[...] = jnp.sum(dz * v * r, axis=0, keepdims=True)
            scaled = dz * gain_ref[...]
            inner = jnp.mean(v * scaled, axis=-1, keepdims=True)
            total = l_i[...].astype(f32) + r * scaled - v * (r * r * r * inner)
            gh_o[...] = total
            da_o[...] = total.astype(bf16)

        do_o[0] = dot_nt(da_o[...], w_i[...]).astype(bf16)

    outs = (
        struct((rows, width), f32),
        struct((rows, width), bf16),
        struct((n, rows, cols), bf16),
        struct((1, width), f32),
    )
    full = pl.BlockSpec((rows, width), lambda p: (0, 0))
    return pl.pallas_call(
        kernel,
        grid=(n,),
        in_specs=[whole(moved), whole(part), whole(low), whole(hidden), whole(gain)]
        + [pl.BlockSpec((cols, width), lambda p: (p, 0))],
        out_specs=(
            full,
            full,
            pl.BlockSpec((1, rows, cols), lambda p: (p, 0, 0)),
            pl.BlockSpec((1, width), lambda p: (0, 0)),
        ),
        out_shape=outs,
        compiler_params=params(1),
        cost_estimate=cost(2 * rows * width * width, hidden, *outs),
        name="out_back",
    )(moved, part, low, hidden, gain, weight)


def attention_weight_grads(atts, datts, normeds, lows, columns):
    count = len(atts)
    n, rows, cols = atts[0].shape
    width = n * cols
    total, wide = lows[0].shape

    def kernel(*refs):
        at, da, nm, lw = (refs[i * count : (i + 1) * count] for i in range(4))
        column_ref, o = refs[4 * count :]
        o[:, :width] = sum(dot_tn(at[g][0], da[g][...]) for g in range(count)).astype(bf16)
        o[:, width : width + wide] = sum(
            dot_tn(nm[g][...], lw[g][...]) for g in range(count)
        ).astype(bf16)
        o[:, width + wide :] = column_ref[...]

    out = struct((width, width + wide + LANES), bf16)
    return pl.pallas_call(
        kernel,
        grid=(n,),
        in_specs=[pl.BlockSpec((1, rows, cols), lambda p: (p, 0, 0)) for _ in atts]
        + [whole(x) for x in datts]
        + [pl.BlockSpec((total, cols), lambda p: (0, p)) for _ in normeds]
        + [whole(x) for x in lows]
        + [pl.BlockSpec((cols, LANES), lambda p: (p, 0))],
        out_specs=pl.BlockSpec((cols, width + wide + LANES), lambda p: (p, 0)),
        out_shape=out,
        compiler_params=params(1),
        cost_estimate=cost(2 * count * width * (rows * width + total * wide), *normeds, *lows, out),
        name="attention_weight_grads",
    )(*atts, *datts, *normeds, *lows, columns)


def picks(rank_ref, nb, cap):
    row = rank_ref[0, nb : nb + 1, :]
    return lax.broadcasted_iota(jnp.int32, (cap, row.shape[1]), 0) == row


def slot_weight(hot, coef_ref, nb):
    return jnp.sum(jnp.where(hot, coef_ref[0, nb : nb + 1, :], 0.0), axis=-1, keepdims=True)


def in_place(arrays, given):
    if arrays is None:
        return (), [], {}
    return (
        tuple(arrays),
        [pl.BlockSpec(memory_space=pl.ANY)] * len(arrays),
        {given + i: i for i in range(len(arrays))},
    )


def expert_forward(pieces, rank, gate_up, cap, start, stop, begun=None):
    experts, blocks, rows = rank.shape
    width, hidden = gate_up.shape[1:]
    slots = blocks * cap
    tile = min(256, hidden)
    parts = chunks_of(blocks, cap)
    part = slots // parts
    more, more_specs, aliases = in_place(begun, blocks + 3)

    def kernel(*refs):
        xs, (rank_ref, wg, wu), (x_o, g_o, u_o, a_o) = (
            refs[:blocks],
            refs[blocks : blocks + 3],
            refs[-4:],
        )

        @pl.when(pl.program_id(1) == 0)
        def _():
            for nb in range(blocks):
                hot = picks(rank_ref, nb, cap).astype(bf16)
                x_o[0, nb * cap : (nb + 1) * cap, :] = dot(hot, xs[nb][...]).astype(bf16)

        @pl.loop(0, parts)
        def _(i):
            at = pl.ds(pl.multiple_of(i * part, part), part)
            x = x_o[0, at, :]
            gate = dot(x, wg[0])
            upper = dot(x, wu[0])
            g_o[0, at, :] = gate.astype(bf16)
            u_o[0, at, :] = upper.astype(bf16)
            a_o[0, at, :] = (gate * jax.nn.sigmoid(gate) * upper).astype(bf16)

    tiled = pl.BlockSpec((1, slots, tile), lambda e, f: (start + e, 0, f))
    outs = (struct((experts, slots, width), bf16),) + (struct((experts, slots, hidden), bf16),) * 3
    return pl.pallas_call(
        kernel,
        grid=(stop - start, hidden // tile),
        in_specs=[whole(x) for x in pieces]
        + [
            pl.BlockSpec((1, blocks, rows), lambda e, f: (start + e, 0, 0)),
            pl.BlockSpec((1, width, tile), lambda e, f: (start + e, 0, f)),
            pl.BlockSpec((1, width, tile), lambda e, f: (experts + start + e, 0, f)),
        ]
        + more_specs,
        out_specs=(
            pl.BlockSpec((1, slots, width), lambda e, f: (start + e, 0, 0)),
            tiled,
            tiled,
            tiled,
        ),
        out_shape=outs,
        input_output_aliases=aliases,
        compiler_params=params(2),
        cost_estimate=cost(4 * (stop - start) * slots * width * hidden, *pieces),
        name="expert_forward",
    )(*pieces, rank, gate_up, gate_up, *more)


def expert_output(active, rank, coef, down, cap):
    experts, blocks, rows = rank.shape
    hidden, width = down.shape[1:]
    slots = blocks * cap
    tile = min(512, width)
    parts = chunks_of(blocks, cap)
    per = blocks // parts

    def kernel(a_i, rank_ref, coef_ref, wd, *rest):
        outs, acc = rest[:blocks], rest[blocks]
        e = pl.program_id(1)

        @pl.when(e == 0)
        def _():
            acc[...] = jnp.zeros_like(acc)

        for i in range(parts):
            y = dot(a_i[0, i * per * cap : (i + 1) * per * cap, :], wd[0])
            for m in range(per):
                nb = i * per + m
                hot = picks(rank_ref, nb, cap)
                weighed = y[m * cap : (m + 1) * cap, :] * slot_weight(hot, coef_ref, nb)
                acc[nb] += dot_tn(hot.astype(bf16), weighed.astype(bf16))

        @pl.when(e == experts - 1)
        def _():
            for nb in range(blocks):
                outs[nb][...] = acc[nb].astype(bf16)

    table = pl.BlockSpec((1, blocks, rows), lambda d, e: (e, 0, 0))
    outs = (struct((rows, width), bf16),) * blocks
    return pl.pallas_call(
        kernel,
        grid=(width // tile, experts),
        in_specs=[
            pl.BlockSpec((1, slots, hidden), lambda d, e: (e, 0, 0)),
            table,
            table,
            pl.BlockSpec((1, hidden, tile), lambda d, e: (e, 0, d)),
        ],
        out_specs=(pl.BlockSpec((rows, tile), lambda d, e: (0, d)),) * blocks,
        out_shape=outs,
        scratch_shapes=[pltpu.VMEM((blocks, rows, tile), f32)],
        compiler_params=params(2),
        cost_estimate=cost(2 * experts * slots * width * hidden, active, down, *outs),
        name="expert_output",
    )(active, rank, coef, down)


def expert_backward(pieces, rank, coef, down, gate, upper, active, cap):
    experts, blocks, rows = rank.shape
    hidden, width = down.shape[1:]
    slots = blocks * cap
    tile = min(256, hidden)
    parts = chunks_of(blocks, cap)
    part = slots // parts

    def kernel(*refs):
        ds, (rank_ref, coef_ref, wd, g_i, u_i, a_i), (dg_o, du_o, dw_o, dy) = (
            refs[:blocks],
            refs[blocks : blocks + 6],
            refs[blocks + 6 :],
        )

        @pl.when(pl.program_id(1) == 0)
        def _():
            for nb in range(blocks):
                hot = picks(rank_ref, nb, cap)
                picked = dot(hot.astype(bf16), ds[nb][...])
                dy[nb * cap : (nb + 1) * cap, :] = (
                    picked * slot_weight(hot, coef_ref, nb)
                ).astype(bf16)

        @pl.loop(0, parts)
        def _(i):
            at = pl.ds(pl.multiple_of(i * part, part), part)
            da = dot_nt(dy[at, :], wd[0])
            g = g_i[0, at, :].astype(f32)
            s = jax.nn.sigmoid(g)
            du_o[0, at, :] = (da * g * s).astype(bf16)
            dg_o[0, at, :] = (
                da * u_i[0, at, :].astype(f32) * s * (1.0 + g * (1.0 - s))
            ).astype(bf16)

        dw_o[0] = dot_tn(a_i[0], dy[...]).astype(bf16)

    table = pl.BlockSpec((1, blocks, rows), lambda e, f: (e, 0, 0))
    tiled = pl.BlockSpec((1, slots, tile), lambda e, f: (e, 0, f))
    line = pl.BlockSpec((1, tile, width), lambda e, f: (e, f, 0))
    outs = (struct((experts, slots, hidden), bf16),) * 2 + (struct((experts, hidden, width), bf16),)
    return pl.pallas_call(
        kernel,
        grid=(experts, hidden // tile),
        in_specs=[whole(x) for x in pieces] + [table, table, line, tiled, tiled, tiled],
        out_specs=(tiled, tiled, line),
        out_shape=outs,
        scratch_shapes=[pltpu.VMEM((slots, width), bf16)],
        compiler_params=params(2),
        cost_estimate=cost(
            4 * experts * slots * width * hidden, *pieces, down, gate, upper, active, *outs
        ),
        name="expert_backward",
    )(*pieces, rank, coef, down, gate, upper, active)


def expert_input_grad(dgate, dupper, rank, gate_up, cap):
    experts, blocks, rows = rank.shape
    width, hidden = gate_up.shape[1:]
    slots = blocks * cap
    tile = min(512, width)
    parts = chunks_of(blocks, cap)
    per = blocks // parts

    def kernel(dg_i, du_i, rank_ref, wg, wu, *rest):
        outs, acc = rest[:blocks], rest[blocks]
        e = pl.program_id(1)

        @pl.when(e == 0)
        def _():
            acc[...] = jnp.zeros_like(acc)

        for i in range(parts):
            at = slice(i * per * cap, (i + 1) * per * cap)
            dx = (dot_nt(dg_i[0, at, :], wg[0]) + dot_nt(du_i[0, at, :], wu[0])).astype(bf16)
            for m in range(per):
                nb = i * per + m
                hot = picks(rank_ref, nb, cap).astype(bf16)
                acc[nb] += dot_tn(hot, dx[m * cap : (m + 1) * cap, :])

        @pl.when(e == experts - 1)
        def _():
            for nb in range(blocks):
                outs[nb][...] = acc[nb].astype(bf16)

    line = pl.BlockSpec((1, slots, hidden), lambda d, e: (e, 0, 0))
    outs = (struct((rows, width), bf16),) * blocks
    return pl.pallas_call(
        kernel,
        grid=(width // tile, experts),
        in_specs=[
            line,
            line,
            pl.BlockSpec((1, blocks, rows), lambda d, e: (e, 0, 0)),
            pl.BlockSpec((1, tile, hidden), lambda d, e: (e, d, 0)),
            pl.BlockSpec((1, tile, hidden), lambda d, e: (experts + e, d, 0)),
        ],
        out_specs=(pl.BlockSpec((rows, tile), lambda d, e: (0, d)),) * blocks,
        out_shape=outs,
        scratch_shapes=[pltpu.VMEM((blocks, rows, tile), f32)],
        compiler_params=params(2),
        cost_estimate=cost(4 * experts * slots * width * hidden, dgate, dupper, gate_up, *outs),
        name="expert_input_grad",
    )(dgate, dupper, rank, gate_up, gate_up)


def expert_weight_grad(x, dgate, dupper, start, stop, begun=None):
    experts, slots, width = x.shape
    hidden = dgate.shape[2]
    tile = min(256, width)
    more, more_specs, aliases = in_place(begun, 3)

    def kernel(x_i, dg_i, du_i, *rest):
        o = rest[-1]
        o[0, 0] = dot_tn(x_i[0], dg_i[0]).astype(bf16)
        o[1, 0] = dot_tn(x_i[0], du_i[0]).astype(bf16)

    line = pl.BlockSpec((1, slots, hidden), lambda e, d: (start + e, 0, 0))
    return pl.pallas_call(
        kernel,
        grid=(stop - start, width // tile),
        in_specs=[pl.BlockSpec((1, slots, tile), lambda e, d: (start + e, 0, d)), line, line]
        + more_specs,
        out_specs=(pl.BlockSpec((2, 1, tile, hidden), lambda e, d: (0, start + e, d, 0)),),
        out_shape=(struct((2, experts, width, hidden), bf16),),
        input_output_aliases=aliases,
        compiler_params=params(2),
        cost_estimate=cost(4 * (stop - start) * slots * width * hidden, x),
        name="expert_weight_grad",
    )(x, dgate, dupper, *more)


def tables(positions):
    half = HEAD_DIM // 2
    inverse = THETA ** (-(jnp.arange(half, dtype=f32) * 2.0) / HEAD_DIM)
    angle = positions.astype(f32)[:, None] * inverse[None, :]
    cosines, sines = jnp.cos(angle), jnp.sin(angle)
    return (
        jnp.concatenate([cosines, cosines], axis=-1),
        jnp.concatenate([-sines, sines], axis=-1),
    )


def norm_back(v, gain, dz):
    r = lax.rsqrt(jnp.mean(v * v, axis=-1, keepdims=True) + EPS)
    moved = dz * gain
    return r * moved - v * (r * r * r) * jnp.mean(v * moved, axis=-1, keepdims=True), dz * v * r


def body(
    tokens, lengths, expert_ids, route_levels, w_query, w_key, w_value, w_out,
    attn_gain, query_gain, key_gain, ffn_gain, w_gate, w_up, w_down, cotangent,
):
    batches, sequences, rows, width = tokens.shape
    top = expert_ids.shape[-1]
    experts = w_gate.shape[0]
    n = lax.axis_size("ctx")
    here = lax.axis_index("ctx")
    seqs = batches * sequences
    cols = width // n
    own = w_query.shape[0]
    cap = rows * top * 5 // (4 * experts * n)
    cap = -(-cap // 16) * 16
    blocks = n * seqs
    up = [(i, (i + 1) % n) for i in range(n)]
    place = here.reshape(1).astype(jnp.int32)

    def after(value, *others):
        return lax.optimization_barrier((value, others))[0]

    class Ring:
        def __init__(self, piece):
            self.held = [piece]

        def hop(self, prev):
            if len(self.held) == n:
                return ()
            self.held.append(lax.ppermute(after(self.held[-1], prev), "ctx", up))
            return (self.held[-1],)

    class Sum:
        def __init__(self, parts):
            self.parts = parts
            self.moved = None
            self.at = 1

        def hop(self, prev):
            if self.at == n:
                return ()
            part = after(self.parts[self.at], prev)
            if self.moved is not None:
                part = (after(self.moved, prev).astype(f32) + part.astype(f32)).astype(bf16)
            self.moved = lax.ppermute(part, "ctx", up)
            self.at += 1
            return (self.moved,)

    def finish(ring, prev):
        while got := ring.hop(prev):
            prev = (prev, got)
        return prev

    def direct(x):
        return [x] + [
            lax.ppermute(x, "ctx", [(i, (i + k) % n) for i in range(n)]) for k in range(1, n)
        ]

    def ctx_sum(x):
        held = direct(x)
        return sum((jnp.roll(held[k], k, axis=0) for k in range(1, n)), held[0])

    def exchange(x):
        return lax.all_to_all(x, "ctx", split_axis=0, concat_axis=0, tiled=True)

    gains = jnp.stack([attn_gain, query_gain, key_gain, ffn_gain], axis=1)
    gains = jnp.pad(gains, ((0, 0), (0, LANES - 4)))
    mine = jnp.concatenate(
        [jnp.broadcast_to(w_out[None], (n, own, width))]
        + [jnp.swapaxes(w.reshape(own, n, cols), 0, 1) for w in (w_query, w_key, w_value)]
        + [jnp.broadcast_to(gains[None], (n, own, LANES))],
        axis=2,
    )
    mine = exchange(mine).reshape(n * own, -1)
    att_w = lax.all_gather(mine, "batch", axis=0, tiled=True)
    all_gains = att_w[:, width + 3 * cols : width + 3 * cols + 4].astype(f32).T
    gain_attn, gain_ffn = all_gains[0], all_gains[3]
    gate_up = lax.all_gather(
        after(jnp.concatenate([w_gate, w_up], axis=0), mine), "batch", axis=1, tiled=True
    )
    down = lax.all_gather(after(w_down, mine), "batch", axis=2, tiled=True)
    qk_gains = lax.dynamic_slice_in_dim(all_gains[1:3], here * cols, cols, 1).reshape(2, 1, cols)

    xs = tokens.reshape(seqs, rows, width)
    span_len = lengths.reshape(seqs)
    local_pos = here * rows + jnp.arange(rows, dtype=jnp.int32)
    live = (local_pos[None, :] < span_len[:, None])[:, :, None]
    grad_low = jnp.where(live, cotangent.reshape(seqs, rows, width), jnp.zeros((), bf16))
    sent = jnp.stack(
        [
            jnp.swapaxes(expert_ids.reshape(seqs, rows, top), 1, 2),
            jnp.swapaxes(route_levels.reshape(seqs, rows, top), 1, 2),
        ]
    )
    routes = jnp.stack(direct(sent))
    chosen = routes[:, 0].reshape(blocks, top, rows)
    levels = routes[:, 1].reshape(blocks, top, rows).astype(f32)
    share = levels / jnp.sum(levels, axis=1, keepdims=True)
    owned = here * experts + jnp.arange(experts, dtype=jnp.int32)
    hit = chosen[None] == owned[:, None, None, None]
    named = jnp.any(hit, axis=2)
    coef = jnp.sum(jnp.where(hit, share[None], 0.0), axis=2)
    upto = (
        jnp.arange(rows, dtype=jnp.int32)[:, None] <= jnp.arange(rows, dtype=jnp.int32)[None, :]
    ).astype(bf16)
    count = jnp.dot(
        named.astype(bf16).reshape(experts * blocks, rows), upto, preferred_element_type=f32
    )
    rank = jnp.where(named, count.reshape(experts, blocks, rows).astype(jnp.int32) - 1, -1)

    cosines, sines = tables(jnp.arange(n * rows, dtype=jnp.int32))
    cosines = cosines.reshape(n, rows, HEAD_DIM)
    sines = sines.reshape(n, rows, HEAD_DIM)
    kept, atts, hiddens = [None] * seqs, [None] * seqs, [None] * seqs
    xr = [Ring(xs[g]) for g in range(seqs)]
    nr = [None] * seqs

    def projected(g, prev):
        normed, qkv, squares = project(
            [after(xr[g].held[0], prev)] + xr[g].held[1:], gain_attn[None, :], att_w, cols, n
        )
        return normed, qkv.reshape(n, 1, rows, 3 * cols), squares

    def scales(squares, prev):
        squares = jnp.swapaxes(squares[:2].reshape(2, n, rows), 0, 1)
        inverse = lax.rsqrt(ctx_sum(after(squares, prev)) / width + EPS)
        return jnp.swapaxes(inverse, 0, 1).reshape(2, n, 1, rows, 1)

    def attended(g, normed, qkv, inverse, prev):
        q, k, v, att, lse = attention_forward(
            place, span_len[g : g + 1], qkv, after(inverse, prev), qk_gains, cosines, sines
        )
        kept[g] = (q, k, v, lse, qkv, inverse, normed)
        return att.reshape(n, rows, cols)

    def out_projected(g, prev):
        hiddens[g], n2 = out_project(
            after(atts[g], prev), xs[g], att_w, gain_ffn[None, :]
        )
        nr[g] = Ring(n2)
        return (n2,)

    stage = xr[0].hop(routes)
    stage = finish(xr[0], stage)
    first = None
    for g in range(seqs):
        last = g + 1 == seqs
        if not last:
            stage = xr[g + 1].hop(stage)
            moving = xr[g + 1].hop(stage)
        else:
            moving = ()
        if first is not None:
            moving = (exchange(after(first, stage)),)
        normed, qkv, squares = projected(g, stage)
        stage = (squares, moving)
        inverse = scales(squares, stage)
        if first is not None:
            atts[g - 1] = moving[0]
            stage = (inverse, out_projected(g - 1, stage))
        else:
            stage = (inverse,)
        moving = () if last else xr[g + 1].hop(stage)
        if first is not None:
            moving += nr[g - 1].hop(stage)
        att = attended(g, normed, qkv, inverse, stage)
        stage = (att, moving)
        if not last:
            stage = finish(xr[g + 1], stage)
        first = att
    g = seqs - 1
    moving = nr[g - 1].hop(stage) if g else ()
    atts[g] = exchange(after(first, stage))
    stage = (atts[g], moving)
    moving = nr[g - 1].hop(stage) if g else ()
    stage = (out_projected(g, stage), moving)
    for one in nr:
        stage = finish(one, stage)

    dr = [Ring(grad_low[g]) for g in range(seqs)]
    n_pieces = [nr[g].held[j] for j in range(n) for g in range(seqs)]
    held = None
    for start, stop in ((0, experts // 2), (experts // 2, experts)):
        moving = [one.hop(stage) for one in dr]
        held = expert_forward(
            n_pieces, after(rank, stage), gate_up, cap, start, stop, held
        )
        stage = (held, moving)
    slots_x, gate, upper, active = held
    moving = [one.hop(stage) for one in dr]
    y_parts = expert_output(after(active, stage), rank, coef, down, cap)
    stage = (y_parts, moving)
    stage = [finish(one, stage) for one in dr] or stage
    grad_pieces = [dr[g].held[j] for j in range(n) for g in range(seqs)]
    yr = [Sum([y_parts[j * seqs + g] for j in range(n)]) for g in range(seqs)]
    moving = [one.hop(stage) for one in yr]
    dgate, dupper, grad_down = expert_backward(
        grad_pieces, after(rank, stage), coef, down, gate, upper, active, cap
    )
    stage = (dgate, moving)
    grad_down = lax.psum_scatter(
        after(grad_down, stage), "batch", scatter_dimension=2, tiled=True
    )
    moving = [one.hop(stage) for one in yr]
    dx_parts = expert_input_grad(after(dgate, stage), dupper, rank, gate_up, cap)
    stage = (dx_parts, moving)
    zr = [Sum([dx_parts[j * seqs + g] for j in range(n)]) for g in range(seqs)]
    held = None
    for i in range(3):
        moving = zr[0].hop(stage)
        held = expert_weight_grad(
            slots_x, after(dgate, stage), dupper, experts * i // 3, experts * (i + 1) // 3, held
        )
        stage = (held, moving)
    gu_local = held[0].reshape(2 * experts, width, -1)
    grad_gu = lax.psum_scatter(
        after(gu_local, stage, grad_down), "batch", scatter_dimension=1, tiled=True
    )
    stage = finish(zr[0], stage)

    grad_hiddens, datts, dos = [None] * seqs, [None] * seqs, [None] * seqs
    lows, dn = [None] * seqs, [None] * seqs
    ffn_part = jnp.zeros((1, width), f32)
    qk_part = jnp.zeros((2, cols), f32)

    def out_backed(g, prev):
        grad_hiddens[g], datts[g], do, one = out_back(
            after(zr[g].moved, prev), dx_parts[g], grad_low[g], hiddens[g], gain_ffn[None, :],
            att_w, n,
        )
        return do, one

    def attention_backed(g, prev):
        q, k, v, lse, qkv, inverse, _ = kept[g]
        *grads, stats, qk_one = attention_backward(
            place, span_len[g : g + 1], after(q, prev), k, v, dos[g].reshape(n, 1, rows, cols),
            lse, qkv, inverse, qk_gains, cosines, sines,
        )
        stats = jnp.sum(stats.reshape(2, cols // HEAD_DIM, n, rows), axis=1)
        return grads, jnp.swapaxes(stats, 0, 1), qk_one.reshape(2, cols)

    def summed_stats(stats, prev):
        return jnp.swapaxes(ctx_sum(after(stats, prev)), 0, 1) / width

    def back_projected(g, grads, stats, prev):
        qkv, inverse = kept[g][4:6]
        *dn1, lows[g] = back_project(
            *(one.reshape(n * rows, cols) for one in grads), qkv.reshape(n * rows, 3 * cols),
            inverse.reshape(2, n * rows, 1), after(stats, prev).reshape(2, n * rows, 1), qk_gains,
            att_w, n, n,
        )
        dn[g] = Sum(dn1)
        return (lows[g],)

    held = None
    for g in range(seqs):
        last = g + 1 == seqs
        if g == 0:
            moving = () if last else zr[1].hop(stage)
            do, one = out_backed(0, stage)
            ffn_part = ffn_part + one
            stage = (do, moving)
        moving = () if last else zr[g + 1].hop(stage)
        dos[g] = exchange(after(do, stage))
        if held is not None:
            moving += back_projected(g - 1, *held, stage)
        stage = (dos[g], moving)
        moving = () if last else zr[g + 1].hop(stage)
        if held is not None:
            moving += dn[g - 1].hop(stage)
        grads, stats, one = attention_backed(g, stage)
        qk_part = qk_part + one
        stage = (stats, moving)
        if not last:
            stage = finish(zr[g + 1], stage)
        stats = summed_stats(stats, stage)
        if not last:
            do, one = out_backed(g + 1, stage)
            ffn_part = ffn_part + one
            stage = (stats, do)
        else:
            stage = (stats,)
        held = (grads, stats)
    g = seqs - 1
    moving = dn[g - 1].hop(stage) if g else ()
    stage = (back_projected(g, *held, stage), moving)
    qk_rows = lax.dynamic_update_slice_in_dim(
        jnp.zeros((2, width), f32), qk_part, here * cols, 1
    )
    columns = jnp.concatenate([qk_rows, ffn_part]).T.astype(bf16)
    columns = jnp.pad(columns, ((0, 0), (0, LANES - 3)))
    moving = dn[g - 1].hop(stage) if g else ()
    att_grads = attention_weight_grads(
        atts, datts, [one[-1] for one in kept], lows, after(columns, stage)
    )
    stage = (att_grads, moving)
    summed = lax.psum_scatter(after(att_grads, grad_gu), "batch", scatter_dimension=0, tiled=True)
    while len(left := [one.hop(stage) for one in dn + yr if one.at < n]):
        stage = left
    outs = [
        jnp.where(
            live[g], hiddens[g] + (yr[g].moved.astype(f32) + y_parts[g].astype(f32)), 0.0
        ).astype(bf16)
        for g in range(seqs)
    ]
    token_grads = []
    for g in range(seqs):
        grad_n1 = dn[g].moved.astype(f32) + dn[g].parts[0].astype(f32)
        back, _ = norm_back(xs[g].astype(f32), gain_attn, grad_n1)
        token_grads.append(grad_hiddens[g] + back)
    summed = exchange(summed.reshape(n, own, -1)).astype(f32)
    grad_out = jnp.sum(summed[:, :, :width], axis=0)
    grad_q, grad_k, grad_v = (
        jnp.swapaxes(summed[:, :, width + i * cols : width + (i + 1) * cols], 0, 1).reshape(
            own, width
        )
        for i in range(3)
    )
    gain_sums = jnp.sum(summed[:, :, width + 3 * cols :], axis=0)
    grad_attn_gain = (
        jnp.sum(
            w_query.astype(f32) * grad_q
            + w_key.astype(f32) * grad_k
            + w_value.astype(f32) * grad_v,
            axis=1,
        )
        / attn_gain.astype(f32)
    )
    shape = (batches, sequences, rows, width)
    return (
        jnp.stack(outs).reshape(shape),
        jnp.stack(token_grads).reshape(shape),
        grad_q,
        grad_k,
        grad_v,
        grad_out,
        grad_attn_gain,
        gain_sums[:, 0],
        gain_sums[:, 1],
        gain_sums[:, 2],
        grad_gu[:experts].astype(f32),
        grad_gu[experts:].astype(f32),
        grad_down.astype(f32),
    )


def solution(mesh):
    rows = P(None, "batch", "ctx", None)
    flat = P(("batch", "ctx"), None)
    line = P(("batch", "ctx"))
    wide = P("ctx", "batch", None)
    tall = P("ctx", None, "batch")
    in_specs = (rows, P(None, "batch"), rows, rows) + (flat,) * 4 + (line,) * 4
    in_specs += (wide, wide, tall, rows)
    out_specs = (rows, rows) + (flat,) * 4 + (line,) * 4 + (wide, wide, tall)
    return jax.shard_map(body, mesh=mesh, in_specs=in_specs, out_specs=out_specs, check_vma=False)
```

```python
import jax
import jax.numpy as jnp
from jax import lax
from jax.experimental import pallas as pl
from jax.experimental.pallas import tpu as pltpu
from jax.sharding import PartitionSpec as P

HEAD_DIM = 128
EPS = 1e-05
THETA = 10000.0
MASKED = -1e30
LANES = 128
ROOM = 58 << 20
SLIM = 8

f32 = jnp.float32
bf16 = jnp.bfloat16


def dot(left, right, contract=((1,), (0,))):
    return lax.dot_general(left, right, (contract, ((), ())), preferred_element_type=f32)


def dot_nt(left, right):
    return dot(left, right, ((1,), (1,)))


def dot_tn(left, right):
    return dot(left, right, ((0,), (0,)))


def struct(shape, dtype):
    return jax.ShapeDtypeStruct(shape, dtype)


def cost(flops, *arrays):
    moved = sum(a.size * a.dtype.itemsize for a in arrays)
    return pl.CostEstimate(
        flops=int(flops) // SLIM, bytes_accessed=int(moved) // SLIM, transcendentals=0
    )


def whole(array):
    zeros = (0,) * len(array.shape)
    return pl.BlockSpec(array.shape, lambda *_: zeros, pipeline_mode=pl.Buffered(1))


def params(axes):
    return pltpu.CompilerParams(
        dimension_semantics=("arbitrary",) * axes, vmem_limit_bytes=ROOM
    )


def project(pieces, gain, weight, third, first):
    count, (rows, width) = len(pieces), pieces[0].shape
    total = count * rows
    step = 32
    part = min(total, 512)

    def kernel(*refs):
        xs, (gain_ref, w_ref), (n_ref, out_ref, ss_ref) = (
            refs[:count],
            refs[count : count + 2],
            refs[count + 2 :],
        )

        @pl.when(pl.program_id(0) == 0)
        def _():
            for i in range(count):

                @pl.loop(0, rows // step)
                def _(k):
                    v = xs[i][pl.ds(k * step, step), :].astype(f32)
                    r = lax.rsqrt(jnp.mean(v * v, axis=-1, keepdims=True) + EPS)
                    n_ref[pl.ds(i * rows + k * step, step), :] = (v * r * gain_ref[...]).astype(
                        bf16
                    )

        @pl.loop(0, total // part)
        def _(k):
            at = pl.ds(pl.multiple_of(k * part, part), part)
            p = dot(n_ref[at, :], w_ref[...])
            out_ref[at, :] = p
            ss_ref[0, at, :] = jnp.sum(p * p, axis=-1, keepdims=True)

    outs = (
        struct((total, width), bf16),
        struct((total, 3 * third), f32),
        struct((3, total, 1), f32),
    )
    return pl.pallas_call(
        kernel,
        grid=(3,),
        in_specs=[whole(x) for x in pieces]
        + [whole(gain), pl.BlockSpec((width, third), lambda t: (0, first + t))],
        out_specs=(
            pl.BlockSpec((total, width), lambda t: (0, 0)),
            pl.BlockSpec((total, third), lambda t: (0, t)),
            pl.BlockSpec((1, total, 1), lambda t: (t, 0, 0)),
        ),
        out_shape=outs,
        compiler_params=params(1),
        cost_estimate=cost(2 * total * width * 3 * third, *pieces, *outs[:2]),
        name="project",
    )(*pieces, gain, weight)


def turn(v, cosines, sines):
    return v * cosines + pltpu.roll(v, HEAD_DIM // 2, 1) * sines


def turn_back(v, cosines, sines):
    return v * cosines + pltpu.roll(v * sines, HEAD_DIM // 2, 1)


def allowed_of(start, rows, count, length):
    row = start + lax.broadcasted_iota(jnp.int32, (rows, count), 0)
    col = lax.broadcasted_iota(jnp.int32, (rows, count), 1)
    return (col <= row) & (col < length)


def attention_forward(place, lengths, qkv, inverse, gains, cosines, sines):
    n, seqs, rows, wide = qkv.shape
    cols = wide // 3
    heads = cols // HEAD_DIM
    span = n * rows
    scale = HEAD_DIM ** (-0.5)

    def kernel(place_ref, len_ref, qi, ki, vi, inv, gain_ref, cos_ref, sin_ref, q_o, k_o, v_o, att, lse):
        here = place_ref[0]
        length = len_ref[pl.program_id(0)]
        for p in range(n):
            j = lax.rem(here + (n - p), n)
            at = slice(p * rows, (p + 1) * rows)
            for which, (src, dst) in enumerate(((qi, q_o), (ki, k_o))):
                z = src[j, 0] * inv[which, j, 0] * gain_ref[which]
                dst[0, at, :] = turn(z, cos_ref[p], sin_ref[p]).astype(bf16)
            v_o[0, at, :] = vi[j, 0].astype(bf16)
        for p in range(n):
            at = slice(p * rows, (p + 1) * rows)
            kv = (p + 1) * rows
            s = dot_nt(q_o[0, at, :], k_o[0, :kv, :]) * scale
            s = jnp.where(allowed_of(p * rows, rows, kv, length), s, MASKED)
            peak = jnp.max(s, axis=-1, keepdims=True)
            e = jnp.exp(s - peak)
            z = jnp.sum(e, axis=-1, keepdims=True)
            att[p, 0] = dot((e / z).astype(bf16), v_o[0, :kv, :]).astype(bf16)
            lse[0, 0, at, :] = peak + jnp.log(z)

    def part(k):
        return pl.BlockSpec((n, 1, rows, HEAD_DIM), lambda g, h, *_: (0, g, 0, k * heads + h))

    line = pl.BlockSpec((1, span, HEAD_DIM), lambda g, h, *_: (g, 0, h))
    outs = (struct((seqs, span, cols), bf16),) * 3 + (
        struct((n, seqs, rows, cols), bf16),
        struct((seqs, heads, span, 1), f32),
    )
    return pl.pallas_call(
        kernel,
        grid_spec=pltpu.PrefetchScalarGridSpec(
            num_scalar_prefetch=2,
            grid=(seqs, heads),
            in_specs=[
                part(0),
                part(1),
                part(2),
                pl.BlockSpec((2, n, 1, rows, 1), lambda g, h, *_: (0, 0, g, 0, 0)),
                pl.BlockSpec((2, 1, HEAD_DIM), lambda g, h, *_: (0, 0, h)),
                whole(cosines),
                whole(sines),
            ],
            out_specs=(
                line,
                line,
                line,
                pl.BlockSpec((n, 1, rows, HEAD_DIM), lambda g, h, *_: (0, g, 0, h)),
                pl.BlockSpec((1, 1, span, 1), lambda g, h, *_: (g, h, 0, 0)),
            ),
        ),
        out_shape=outs,
        compiler_params=params(2),
        cost_estimate=cost(3 * seqs * heads * span * span * HEAD_DIM, qkv, *outs[:4]),
        name="attention",
    )(place, lengths, qkv, qkv, qkv, inverse, gains, cosines, sines)


def attention_backward(place, lengths, q, k, v, grad, lse, qkv, inverse, gains, cosines, sines):
    n, seqs, rows, wide = qkv.shape
    cols = wide // 3
    heads = cols // HEAD_DIM
    span = n * rows
    scale = HEAD_DIM ** (-0.5)

    def kernel(
        place_ref, len_ref, q_i, k_i, v_i, do_i, lse_i, qp_i, kp_i, inv, gain_ref, cos_ref, sin_ref,
        dq_o, dk_o, dv_o, st_o, dg_o, dq_s, dk_s, dv_s,
    ):
        here = place_ref[0]
        length = len_ref[pl.program_id(0)]
        dk_s[...] = jnp.zeros_like(dk_s)
        dv_s[...] = jnp.zeros_like(dv_s)
        for p in range(n):
            at = slice(p * rows, (p + 1) * rows)
            kv = (p + 1) * rows
            query, keys, values, do = q_i[0, at, :], k_i[0, :kv, :], v_i[0, :kv, :], do_i[p, 0]
            s = dot_nt(query, keys) * scale
            probs = jnp.where(
                allowed_of(p * rows, rows, kv, length), jnp.exp(s - lse_i[0, 0, at, :]), 0.0
            )
            dp = dot_nt(do, values)
            ds = (probs * (dp - jnp.sum(probs * dp, axis=-1, keepdims=True))).astype(bf16)
            dq_s[at, :] = dot(ds, keys) * scale
            dk_s[:kv, :] += dot_tn(ds, query)
            dv_s[:kv, :] += dot_tn(probs.astype(bf16), do)
        dk_s[...] = dk_s[...] * scale
        sums = [jnp.zeros((1, HEAD_DIM), f32)] * 2
        for p in range(n):
            j = lax.rem(here + (n - p), n)
            at = slice(p * rows, (p + 1) * rows)
            for which, (src, raw, dst) in enumerate(((dq_s, qp_i, dq_o), (dk_s, kp_i, dk_o))):
                dz = turn_back(src[at, :], cos_ref[p], sin_ref[p])
                moved = raw[j, 0] * dz
                dst[j, 0] = dz
                st_o[which, 0, 0, j] = jnp.sum(moved * gain_ref[which], axis=-1, keepdims=True)
                sums[which] += jnp.sum(moved * inv[which, j, 0], axis=0, keepdims=True)
            dv_o[j, 0] = dv_s[at, :].astype(bf16)
        for which in range(2):
            dg_o[which, 0] = sums[which]

    def part(i):
        return pl.BlockSpec((n, 1, rows, HEAD_DIM), lambda g, h, *_: (0, g, 0, i * heads + h))

    line = pl.BlockSpec((1, span, HEAD_DIM), lambda g, h, *_: (g, 0, h))
    block = part(0)
    outs = (
        struct((n, seqs, rows, cols), f32),
        struct((n, seqs, rows, cols), f32),
        struct((n, seqs, rows, cols), bf16),
        struct((2, seqs, heads, n, rows, 1), f32),
        struct((2, seqs, 1, cols), f32),
    )
    return pl.pallas_call(
        kernel,
        grid_spec=pltpu.PrefetchScalarGridSpec(
            num_scalar_prefetch=2,
            grid=(seqs, heads),
            in_specs=[
                line,
                line,
                line,
                block,
                pl.BlockSpec((1, 1, span, 1), lambda g, h, *_: (g, h, 0, 0)),
                part(0),
                part(1),
                pl.BlockSpec((2, n, 1, rows, 1), lambda g, h, *_: (0, 0, g, 0, 0)),
                pl.BlockSpec((2, 1, HEAD_DIM), lambda g, h, *_: (0, 0, h)),
                whole(cosines),
                whole(sines),
            ],
            out_specs=(
                block,
                block,
                block,
                pl.BlockSpec((2, 1, 1, n, rows, 1), lambda g, h, *_: (0, g, h, 0, 0, 0)),
                pl.BlockSpec((2, 1, 1, HEAD_DIM), lambda g, h, *_: (0, g, 0, h)),
            ),
            scratch_shapes=[pltpu.VMEM((span, HEAD_DIM), f32)] * 3,
        ),
        out_shape=outs,
        compiler_params=params(2),
        cost_estimate=cost(7 * seqs * heads * span * span * HEAD_DIM, qkv, *outs[:3]),
        name="attention_back",
    )(place, lengths, q, k, v, grad, lse, qkv, qkv, inverse, gains, cosines, sines)


def back_project(dzq, dzk, dv, qkv, inverse, stats, gains, weight, first, pieces):
    total, third = dv.shape
    width = weight.shape[0]
    rows = total // pieces
    tile = min(512, width)

    def kernel(dzq_i, dzk_i, dv_i, q_i, k_i, inv, st, gain_ref, wq, wk, wv, *rest):
        outs, low = rest[:pieces], rest[pieces]

        @pl.when(pl.program_id(0) == 0)
        def _():
            for which, (dz, raw) in enumerate(((dzq_i, q_i), (dzk_i, k_i))):
                r = inv[which]
                low[:, which * third : (which + 1) * third] = (
                    r * (gain_ref[which] * dz[...]) - raw[...] * (r * r * r * st[which])
                ).astype(bf16)
            low[:, 2 * third :] = dv_i[...]

        for i in range(pieces):
            at = slice(i * rows, (i + 1) * rows)
            outs[i][...] = (
                dot_nt(low[at, :third], wq[...])
                + dot_nt(low[at, third : 2 * third], wk[...])
                + dot_nt(low[at, 2 * third :], wv[...])
            ).astype(bf16)

    def raw(k):
        return pl.BlockSpec((total, third), lambda d: (0, k))

    def taken(k):
        return pl.BlockSpec((tile, third), lambda d: (d, first + k))

    outs = (struct((rows, width), bf16),) * pieces + (struct((total, 3 * third), bf16),)
    return pl.pallas_call(
        kernel,
        grid=(width // tile,),
        in_specs=[whole(dzq), whole(dzk), whole(dv), raw(0), raw(1)]
        + [whole(inverse), whole(stats), whole(gains), taken(0), taken(1), taken(2)],
        out_specs=(pl.BlockSpec((rows, tile), lambda d: (0, d)),) * pieces
        + (pl.BlockSpec((total, 3 * third), lambda d: (0, 0)),),
        out_shape=outs,
        compiler_params=params(1),
        cost_estimate=cost(6 * total * width * third, dzq, dzk, dv, *outs),
        name="back_project",
    )(dzq, dzk, dv, qkv, qkv, inverse, stats, gains, weight, weight, weight)


def out_project(att, rows_in, weight, gain):
    n, rows, cols = att.shape
    width = n * cols

    def kernel(a_i, x_i, w_i, gain_ref, h_o, n_o, acc):
        p = pl.program_id(0)

        @pl.when(p == 0)
        def _():
            acc[...] = x_i[...].astype(f32)

        acc[...] += dot(a_i[0], w_i[...])

        @pl.when(p == n - 1)
        def _():
            h = acc[...]
            h_o[...] = h
            r = lax.rsqrt(jnp.mean(h * h, axis=-1, keepdims=True) + EPS)
            n_o[...] = (h * r * gain_ref[...]).astype(bf16)

    outs = (struct((rows, width), f32), struct((rows, width), bf16))
    return pl.pallas_call(
        kernel,
        grid=(n,),
        in_specs=[
            pl.BlockSpec((1, rows, cols), lambda p: (p, 0, 0)),
            whole(rows_in),
            pl.BlockSpec((cols, width), lambda p: (p, 0)),
            whole(gain),
        ],
        out_specs=(pl.BlockSpec((rows, width), lambda p: (0, 0)),) * 2,
        out_shape=outs,
        scratch_shapes=[pltpu.VMEM((rows, width), f32)],
        compiler_params=params(1),
        cost_estimate=cost(2 * rows * width * width, att, rows_in, *outs),
        name="out_project",
    )(att, rows_in, weight, gain)


def out_back(moved, part, low, hidden, gain, weight, n):
    rows, width = hidden.shape
    cols = width // n

    def kernel(m_i, p_i, l_i, h_i, gain_ref, w_i, gh_o, da_o, do_o, fg_o):
        @pl.when(pl.program_id(0) == 0)
        def _():
            dz = m_i[...].astype(f32) + p_i[...].astype(f32)
            v = h_i[...]
            r = lax.rsqrt(jnp.mean(v * v, axis=-1, keepdims=True) + EPS)
            fg_o[...] = jnp.sum(dz * v * r, axis=0, keepdims=True)
            scaled = dz * gain_ref[...]
            inner = jnp.mean(v * scaled, axis=-1, keepdims=True)
            total = l_i[...].astype(f32) + r * scaled - v * (r * r * r * inner)
            gh_o[...] = total
            da_o[...] = total.astype(bf16)

        do_o[0] = dot_nt(da_o[...], w_i[...]).astype(bf16)

    outs = (
        struct((rows, width), f32),
        struct((rows, width), bf16),
        struct((n, rows, cols), bf16),
        struct((1, width), f32),
    )
    full = pl.BlockSpec((rows, width), lambda p: (0, 0))
    return pl.pallas_call(
        kernel,
        grid=(n,),
        in_specs=[whole(moved), whole(part), whole(low), whole(hidden), whole(gain)]
        + [pl.BlockSpec((cols, width), lambda p: (p, 0))],
        out_specs=(
            full,
            full,
            pl.BlockSpec((1, rows, cols), lambda p: (p, 0, 0)),
            pl.BlockSpec((1, width), lambda p: (0, 0)),
        ),
        out_shape=outs,
        compiler_params=params(1),
        cost_estimate=cost(2 * rows * width * width, hidden, *outs),
        name="out_back",
    )(moved, part, low, hidden, gain, weight)


def weight_grads(lefts, rights, columns, name):
    count = len(lefts)
    total, wide = rights[0].shape
    folded = len(lefts[0].shape) == 3
    width = columns.shape[0]
    tile = lefts[0].shape[2] if folded else min(512, width)

    def kernel(*refs):
        ls, rs, (column_ref, o) = refs[:count], refs[count : 2 * count], refs[2 * count :]
        o[:, :wide] = sum(
            dot_tn(ls[g][0] if folded else ls[g][...], rs[g][...]) for g in range(count)
        ).astype(bf16)
        o[:, wide:] = column_ref[...]

    if folded:
        left = pl.BlockSpec((1, total, tile), lambda p: (p, 0, 0))
    else:
        left = pl.BlockSpec((total, tile), lambda p: (0, p))
    out = struct((width, wide + LANES), bf16)
    return pl.pallas_call(
        kernel,
        grid=(width // tile,),
        in_specs=[left] * count
        + [whole(x) for x in rights]
        + [pl.BlockSpec((tile, LANES), lambda p: (p, 0))],
        out_specs=pl.BlockSpec((tile, wide + LANES), lambda p: (p, 0)),
        out_shape=out,
        compiler_params=params(1),
        cost_estimate=cost(2 * count * total * width * wide, *lefts, *rights, out),
        name=name,
    )(*lefts, *rights, columns)


def picks(rank_ref, nb, cap):
    row = rank_ref[0, nb : nb + 1, :]
    return lax.broadcasted_iota(jnp.int32, (cap, row.shape[1]), 0) == row


def slot_weight(hot, coef_ref, nb):
    return jnp.sum(jnp.where(hot, coef_ref[0, nb : nb + 1, :], 0.0), axis=-1, keepdims=True)


def in_place(arrays, given):
    if arrays is None:
        return (), [], {}
    return (
        tuple(arrays),
        [pl.BlockSpec(memory_space=pl.ANY)] * len(arrays),
        {given + i: i for i in range(len(arrays))},
    )


def expert_forward(pieces, rank, gate_up, cap, start, stop, begun=None):
    experts, blocks, rows = rank.shape
    width, hidden = gate_up.shape[1:]
    slots = blocks * cap
    tile = min(256, hidden)
    more, more_specs, aliases = in_place(begun, blocks + 3)

    def kernel(*refs):
        xs, (rank_ref, wg, wu), (x_o, g_o, u_o, a_o) = (
            refs[:blocks],
            refs[blocks : blocks + 3],
            refs[-4:],
        )

        @pl.when(pl.program_id(1) == 0)
        def _():
            for nb in range(blocks):
                hot = picks(rank_ref, nb, cap).astype(bf16)
                x_o[0, nb * cap : (nb + 1) * cap, :] = dot(hot, xs[nb][...]).astype(bf16)

        x = x_o[0]
        gate = dot(x, wg[0])
        upper = dot(x, wu[0])
        g_o[0] = gate.astype(bf16)
        u_o[0] = upper.astype(bf16)
        a_o[0] = (gate * jax.nn.sigmoid(gate) * upper).astype(bf16)

    tiled = pl.BlockSpec((1, slots, tile), lambda e, f: (start + e, 0, f))
    outs = (struct((experts, slots, width), bf16),) + (struct((experts, slots, hidden), bf16),) * 3
    return pl.pallas_call(
        kernel,
        grid=(stop - start, hidden // tile),
        in_specs=[whole(x) for x in pieces]
        + [
            pl.BlockSpec((1, blocks, rows), lambda e, f: (start + e, 0, 0)),
            pl.BlockSpec((1, width, tile), lambda e, f: (start + e, 0, f)),
            pl.BlockSpec((1, width, tile), lambda e, f: (experts + start + e, 0, f)),
        ]
        + more_specs,
        out_specs=(
            pl.BlockSpec((1, slots, width), lambda e, f: (start + e, 0, 0)),
            tiled,
            tiled,
            tiled,
        ),
        out_shape=outs,
        input_output_aliases=aliases,
        compiler_params=params(2),
        cost_estimate=cost(4 * (stop - start) * slots * width * hidden, *pieces),
        name="expert_forward",
    )(*pieces, rank, gate_up, gate_up, *more)


def expert_output(active, rank, coef, down, cap):
    experts, blocks, rows = rank.shape
    hidden, width = down.shape[1:]
    slots = blocks * cap
    tile = min(512, width)

    def kernel(a_i, rank_ref, coef_ref, wd, *rest):
        outs, acc = rest[:blocks], rest[blocks]
        e = pl.program_id(1)

        @pl.when(e == 0)
        def _():
            acc[...] = jnp.zeros_like(acc)

        y = dot(a_i[0], wd[0])
        for nb in range(blocks):
            hot = picks(rank_ref, nb, cap)
            weighed = y[nb * cap : (nb + 1) * cap, :] * slot_weight(hot, coef_ref, nb)
            acc[nb] += dot_tn(hot.astype(bf16), weighed.astype(bf16))

        @pl.when(e == experts - 1)
        def _():
            for nb in range(blocks):
                outs[nb][...] = acc[nb].astype(bf16)

    table = pl.BlockSpec((1, blocks, rows), lambda d, e: (e, 0, 0))
    outs = (struct((rows, width), bf16),) * blocks
    return pl.pallas_call(
        kernel,
        grid=(width // tile, experts),
        in_specs=[
            pl.BlockSpec((1, slots, hidden), lambda d, e: (e, 0, 0)),
            table,
            table,
            pl.BlockSpec((1, hidden, tile), lambda d, e: (e, 0, d)),
        ],
        out_specs=(pl.BlockSpec((rows, tile), lambda d, e: (0, d)),) * blocks,
        out_shape=outs,
        scratch_shapes=[pltpu.VMEM((blocks, rows, tile), f32)],
        compiler_params=params(2),
        cost_estimate=cost(2 * experts * slots * width * hidden, active, down, *outs),
        name="expert_output",
    )(active, rank, coef, down)


def expert_backward(pieces, rank, coef, down, gate, upper, active, cap):
    experts, blocks, rows = rank.shape
    hidden, width = down.shape[1:]
    slots = blocks * cap
    tile = min(256, hidden)

    def kernel(*refs):
        ds, (rank_ref, coef_ref, wd, g_i, u_i, a_i), (dg_o, du_o, dw_o, dy) = (
            refs[:blocks],
            refs[blocks : blocks + 6],
            refs[blocks + 6 :],
        )

        @pl.when(pl.program_id(1) == 0)
        def _():
            for nb in range(blocks):
                hot = picks(rank_ref, nb, cap)
                picked = dot(hot.astype(bf16), ds[nb][...])
                dy[nb * cap : (nb + 1) * cap, :] = (
                    picked * slot_weight(hot, coef_ref, nb)
                ).astype(bf16)

        da = dot_nt(dy[...], wd[0])
        g = g_i[0].astype(f32)
        s = jax.nn.sigmoid(g)
        du_o[0] = (da * g * s).astype(bf16)
        dg_o[0] = (da * u_i[0].astype(f32) * s * (1.0 + g * (1.0 - s))).astype(bf16)

        dw_o[0] = dot_tn(a_i[0], dy[...]).astype(bf16)

    table = pl.BlockSpec((1, blocks, rows), lambda e, f: (e, 0, 0))
    tiled = pl.BlockSpec((1, slots, tile), lambda e, f: (e, 0, f))
    line = pl.BlockSpec((1, tile, width), lambda e, f: (e, f, 0))
    outs = (struct((experts, slots, hidden), bf16),) * 2 + (struct((experts, hidden, width), bf16),)
    return pl.pallas_call(
        kernel,
        grid=(experts, hidden // tile),
        in_specs=[whole(x) for x in pieces] + [table, table, line, tiled, tiled, tiled],
        out_specs=(tiled, tiled, line),
        out_shape=outs,
        scratch_shapes=[pltpu.VMEM((slots, width), bf16)],
        compiler_params=params(2),
        cost_estimate=cost(
            4 * experts * slots * width * hidden, *pieces, down, gate, upper, active, *outs
        ),
        name="expert_backward",
    )(*pieces, rank, coef, down, gate, upper, active)


def expert_input_grad(dgate, dupper, rank, gate_up, cap, g, seqs):
    blocks, rows = rank.shape[1:]
    width, hidden = gate_up.shape[1:]
    experts = gate_up.shape[0] // 2
    slots = blocks * cap
    tile = min(1024, width)

    def kernel(dg_i, du_i, rank_ref, wg, wu, *rest):
        outs, acc = rest[:blocks], rest[blocks]
        e = pl.program_id(1)

        @pl.when(e == 0)
        def _():
            acc[...] = jnp.zeros_like(acc)

        dx = (dot_nt(dg_i[0], wg[0]) + dot_nt(du_i[0], wu[0])).astype(bf16)
        for nb in range(blocks):
            hot = picks(rank_ref, nb, cap).astype(bf16)
            acc[nb] += dot_tn(hot, dx[nb * cap : (nb + 1) * cap, :])

        @pl.when(e == experts - 1)
        def _():
            for nb in range(blocks):
                outs[nb][...] = acc[nb].astype(bf16)

    line = pl.BlockSpec((1, slots, hidden), lambda d, e: (e, g, 0))
    outs = (struct((rows, width), bf16),) * blocks
    return pl.pallas_call(
        kernel,
        grid=(width // tile, experts),
        in_specs=[
            line,
            line,
            pl.BlockSpec((1, blocks, rows), lambda d, e: (e * seqs + g, 0, 0)),
            pl.BlockSpec((1, tile, hidden), lambda d, e: (e, d, 0)),
            pl.BlockSpec((1, tile, hidden), lambda d, e: (experts + e, d, 0)),
        ],
        out_specs=(pl.BlockSpec((rows, tile), lambda d, e: (0, d)),) * blocks,
        out_shape=outs,
        scratch_shapes=[pltpu.VMEM((blocks, rows, tile), f32)],
        compiler_params=params(2),
        cost_estimate=cost(4 * experts * slots * width * hidden, gate_up, *outs),
        name="expert_input_grad",
    )(dgate, dupper, rank, gate_up, gate_up)


def expert_weight_grad(x, dgate, dupper, start, stop, begun=None):
    experts, slots, width = x.shape
    hidden = dgate.shape[2]
    tile = min(512, width)
    more, more_specs, aliases = in_place(begun, 3)

    def kernel(x_i, dg_i, du_i, *rest):
        o = rest[-1]
        o[0, 0] = dot_tn(x_i[0], dg_i[0]).astype(bf16)
        o[1, 0] = dot_tn(x_i[0], du_i[0]).astype(bf16)

    line = pl.BlockSpec((1, slots, hidden), lambda e, d: (start + e, 0, 0))
    return pl.pallas_call(
        kernel,
        grid=(stop - start, width // tile),
        in_specs=[pl.BlockSpec((1, slots, tile), lambda e, d: (start + e, 0, d)), line, line]
        + more_specs,
        out_specs=(pl.BlockSpec((2, 1, tile, hidden), lambda e, d: (0, start + e, d, 0)),),
        out_shape=(struct((2, experts, width, hidden), bf16),),
        input_output_aliases=aliases,
        compiler_params=params(2),
        cost_estimate=cost(4 * (stop - start) * slots * width * hidden, x),
        name="expert_weight_grad",
    )(x, dgate, dupper, *more)


def tables(positions):
    half = HEAD_DIM // 2
    inverse = THETA ** (-(jnp.arange(half, dtype=f32) * 2.0) / HEAD_DIM)
    angle = positions.astype(f32)[:, None] * inverse[None, :]
    cosines, sines = jnp.cos(angle), jnp.sin(angle)
    return (
        jnp.concatenate([cosines, cosines], axis=-1),
        jnp.concatenate([-sines, sines], axis=-1),
    )


def norm_back(v, gain, dz):
    r = lax.rsqrt(jnp.mean(v * v, axis=-1, keepdims=True) + EPS)
    moved = dz * gain
    return r * moved - v * (r * r * r) * jnp.mean(v * moved, axis=-1, keepdims=True), dz * v * r


def body(
    tokens, lengths, expert_ids, route_levels, w_query, w_key, w_value, w_out,
    attn_gain, query_gain, key_gain, ffn_gain, w_gate, w_up, w_down, cotangent,
):
    batches, sequences, rows, width = tokens.shape
    top = expert_ids.shape[-1]
    experts = w_gate.shape[0]
    n = lax.axis_size("ctx")
    here = lax.axis_index("ctx")
    seqs = batches * sequences
    cols = width // n
    own = w_query.shape[0]
    cap = rows * top * 5 // (4 * experts * n)
    cap = -(-cap // 16) * 16
    blocks = n * seqs
    up = [(i, (i + 1) % n) for i in range(n)]
    place = here.reshape(1).astype(jnp.int32)

    def after(value, *others):
        return lax.optimization_barrier((value, others))[0]

    class Ring:
        def __init__(self, piece):
            self.held = [piece]

        def hop(self, prev):
            if len(self.held) == n:
                return ()
            self.held.append(lax.ppermute(after(self.held[-1], prev), "ctx", up))
            return (self.held[-1],)

    class Sum:
        def __init__(self, parts):
            self.parts = parts
            self.moved = None
            self.at = 1

        def hop(self, prev):
            if self.at == n:
                return ()
            part = after(self.parts[self.at], prev)
            if self.moved is not None:
                part = (after(self.moved, prev).astype(f32) + part.astype(f32)).astype(bf16)
            self.moved = lax.ppermute(part, "ctx", up)
            self.at += 1
            return (self.moved,)

    def finish(ring, prev):
        while got := ring.hop(prev):
            prev = (prev, got)
        return prev

    def direct(x):
        return [x] + [
            lax.ppermute(x, "ctx", [(i, (i + k) % n) for i in range(n)]) for k in range(1, n)
        ]

    def ctx_sum(x):
        held = direct(x)
        return sum((jnp.roll(held[k], k, axis=0) for k in range(1, n)), held[0])

    def exchange(x):
        return lax.all_to_all(x, "ctx", split_axis=0, concat_axis=0, tiled=True)

    gains = jnp.stack([attn_gain, query_gain, key_gain, ffn_gain], axis=1)
    gains = jnp.pad(gains, ((0, 0), (0, LANES - 4)))
    sent = jnp.stack(
        [
            jnp.swapaxes(expert_ids.reshape(seqs, rows, top), 1, 2),
            jnp.swapaxes(route_levels.reshape(seqs, rows, top), 1, 2),
        ]
    )
    sent = sent.astype(bf16).reshape(own, -1)
    extra = sent.shape[1]
    mine = jnp.concatenate(
        [jnp.broadcast_to(w_out[None], (n, own, width))]
        + [jnp.swapaxes(w.reshape(own, n, cols), 0, 1) for w in (w_query, w_key, w_value)]
        + [jnp.broadcast_to(one[None], (n, *one.shape)) for one in (gains, sent)],
        axis=2,
    )
    mine = exchange(mine)
    routes = mine[:, :, -extra:].reshape(n, 2, seqs, top, rows)
    order = lax.rem(here + n - jnp.arange(n, dtype=jnp.int32), n)
    routes = jnp.take(routes, order, axis=0)
    mine = mine.reshape(n * own, -1)
    att_w = lax.all_gather(mine, "batch", axis=0, tiled=True)
    all_gains = att_w[:, width + 3 * cols : width + 3 * cols + 4].astype(f32).T
    gain_attn, gain_ffn = all_gains[0], all_gains[3]
    qk_gains = lax.dynamic_slice_in_dim(all_gains[1:3], here * cols, cols, 1).reshape(2, 1, cols)

    xs = tokens.reshape(seqs, rows, width)
    span_len = lengths.reshape(seqs)
    local_pos = here * rows + jnp.arange(rows, dtype=jnp.int32)
    live = (local_pos[None, :] < span_len[:, None])[:, :, None]
    grad_low = jnp.where(live, cotangent.reshape(seqs, rows, width), jnp.zeros((), bf16))
    def slots_of(routes):
        chosen = jnp.swapaxes(routes[:, 0], 0, 1).reshape(blocks, top, rows).astype(jnp.int32)
        levels = jnp.swapaxes(routes[:, 1], 0, 1).reshape(blocks, top, rows).astype(f32)
        share = levels / jnp.sum(levels, axis=1, keepdims=True)
        owned = here * experts + jnp.arange(experts, dtype=jnp.int32)
        hit = chosen[None] == owned[:, None, None, None]
        named = jnp.any(hit, axis=2)
        coef = jnp.sum(jnp.where(hit, share[None], 0.0), axis=2)
        at = jnp.arange(rows, dtype=jnp.int32)
        upto = (at[:, None] <= at[None, :]).astype(bf16)
        count = jnp.dot(
            named.astype(bf16).reshape(experts * blocks, rows), upto, preferred_element_type=f32
        )
        count = count.reshape(experts, blocks, rows).astype(jnp.int32)
        return jnp.where(named, count - 1, -1), coef

    cosines, sines = tables(jnp.arange(n * rows, dtype=jnp.int32))
    cosines = cosines.reshape(n, rows, HEAD_DIM)
    sines = sines.reshape(n, rows, HEAD_DIM)
    kept, atts, hiddens = [None] * seqs, [None] * seqs, [None] * seqs
    xr = [Ring(xs[g]) for g in range(seqs)]
    nr = [None] * seqs

    def projected(g, prev):
        normed, qkv, squares = project(
            [after(xr[g].held[0], prev)] + xr[g].held[1:], gain_attn[None, :], att_w, cols, n
        )
        return normed, qkv.reshape(n, 1, rows, 3 * cols), squares

    def scales(squares, prev):
        squares = jnp.swapaxes(squares[:2].reshape(2, n, rows), 0, 1)
        inverse = lax.rsqrt(ctx_sum(after(squares, prev)) / width + EPS)
        return jnp.swapaxes(inverse, 0, 1).reshape(2, n, 1, rows, 1)

    def attended(g, normed, qkv, inverse, prev):
        q, k, v, att, lse = attention_forward(
            place, span_len[g : g + 1], qkv, after(inverse, prev), qk_gains, cosines, sines
        )
        kept[g] = (q, k, v, lse, qkv, inverse, normed)
        return att.reshape(n, rows, cols)

    def out_projected(g, prev):
        hiddens[g], n2 = out_project(
            after(atts[g], prev), xs[g], att_w, gain_ffn[None, :]
        )
        nr[g] = Ring(n2)
        return (n2,)

    stage = (xr[0].hop(()), mine)
    rank, coef = slots_of(after(routes, stage))
    stage = xr[0].hop(stage)
    gate_up = lax.all_gather(
        jnp.concatenate([after(w_gate, stage), w_up], axis=0), "batch", axis=1, tiled=True
    )
    down = lax.all_gather(after(w_down, stage), "batch", axis=2, tiled=True)
    stage = finish(xr[0], stage)
    first = None
    for g in range(seqs):
        last = g + 1 == seqs
        if not last:
            stage = xr[g + 1].hop(stage)
            moving = xr[g + 1].hop(stage)
        else:
            moving = ()
        if first is not None:
            moving = (exchange(after(first, stage)),)
        normed, qkv, squares = projected(g, stage)
        stage = (squares, moving)
        inverse = scales(squares, stage)
        if first is not None:
            atts[g - 1] = moving[0]
            stage = (inverse, out_projected(g - 1, stage))
        else:
            stage = (inverse,)
        moving = () if last else xr[g + 1].hop(stage)
        if first is not None:
            moving += nr[g - 1].hop(stage)
        att = attended(g, normed, qkv, inverse, stage)
        stage = (att, moving)
        if not last:
            stage = finish(xr[g + 1], stage)
        first = att
    g = seqs - 1
    moving = nr[g - 1].hop(stage) if g else ()
    atts[g] = exchange(after(first, stage))
    stage = (atts[g], moving)
    moving = nr[g - 1].hop(stage) if g else ()
    stage = (out_projected(g, stage), moving)
    for one in nr:
        stage = finish(one, stage)

    grad_hiddens, datts, dos = [None] * seqs, [None] * seqs, [None] * seqs
    lows, dn = [None] * seqs, [None] * seqs
    qk_part = jnp.zeros((2, cols), f32)

    def out_backed(g, prev):
        grad_hiddens[g], datts[g], do, one = out_back(
            after(zr[g].moved, prev), dx_parts[g][0], grad_low[g], hiddens[g], gain_ffn[None, :],
            att_w, n,
        )
        return do, one

    def attention_backed(g, prev):
        q, k, v, lse, qkv, inverse, _ = kept[g]
        *grads, stats, qk_one = attention_backward(
            place, span_len[g : g + 1], after(q, prev), k, v, dos[g].reshape(n, 1, rows, cols),
            lse, qkv, inverse, qk_gains, cosines, sines,
        )
        stats = jnp.sum(stats.reshape(2, cols // HEAD_DIM, n, rows), axis=1)
        return grads, jnp.swapaxes(stats, 0, 1), qk_one.reshape(2, cols)

    def summed_stats(stats, prev):
        return jnp.swapaxes(ctx_sum(after(stats, prev)), 0, 1) / width

    def back_projected(g, grads, stats, prev):
        qkv, inverse = kept[g][4:6]
        *dn1, lows[g] = back_project(
            *(one.reshape(n * rows, cols) for one in grads), qkv.reshape(n * rows, 3 * cols),
            inverse.reshape(2, n * rows, 1), after(stats, prev).reshape(2, n * rows, 1), qk_gains,
            att_w, n, n,
        )
        dn[g] = Sum(dn1)
        return (lows[g],)

    dr = [Ring(grad_low[g]) for g in range(seqs)]
    n_pieces = [nr[g].held[j] for g in range(seqs) for j in range(n)]
    held = None
    for start, stop in ((0, experts // 2), (experts // 2, experts)):
        moving = [one.hop(stage) for one in dr]
        held = expert_forward(
            n_pieces, after(rank, stage), gate_up, cap, start, stop, held
        )
        stage = (held, moving)
    slots_x, gate, upper, active = held
    moving = [one.hop(stage) for one in dr]
    y_parts = expert_output(after(active, stage), rank, coef, down, cap)
    stage = (y_parts, moving)
    stage = [finish(one, stage) for one in dr] or stage
    grad_pieces = [dr[g].held[j] for g in range(seqs) for j in range(n)]
    yr = [Sum(y_parts[g * n : (g + 1) * n]) for g in range(seqs)]
    moving = [one.hop(stage) for one in yr]
    dgate, dupper, grad_down = expert_backward(
        grad_pieces, after(rank, stage), coef, down, gate, upper, active, cap
    )
    stage = (dgate, moving)
    grad_down = lax.psum_scatter(
        after(grad_down, stage), "batch", scatter_dimension=2, tiled=True
    )
    rank_rows = rank.reshape(experts * seqs, n, rows)

    def input_grad(g, prev):
        dx_parts.append(
            expert_input_grad(after(dgate, prev), dupper, rank_rows, gate_up, cap, g, seqs)
        )
        zr.append(Sum(dx_parts[g]))
        return dx_parts[g]

    zr, dx_parts = [], []
    moving = [one.hop(stage) for one in yr]
    stage = (input_grad(0, stage), moving)
    held = None
    for start, stop in ((0, experts // 2), (experts // 2, experts)):
        moving = zr[0].hop(stage)
        held = expert_weight_grad(slots_x, after(dgate, stage), dupper, start, stop, held)
        stage = (held, moving)
    gu_local = held[0].reshape(2 * experts, width, -1)
    grad_gu = lax.psum_scatter(
        after(gu_local, stage), "batch", scatter_dimension=1, tiled=True
    )
    for g in range(1, seqs):
        moving = (zr[0].hop(stage), yr[0].hop(stage))
        stage = (input_grad(g, stage), moving)
    stage = (finish(zr[0], stage), grad_down)
    moving = zr[1].hop(stage) if seqs > 1 else ()
    do, ffn_part = out_backed(0, stage)
    stage = (do, moving)

    held = None
    for g in range(seqs):
        last = g + 1 == seqs
        moving = () if last else zr[g + 1].hop(stage)
        dos[g] = exchange(after(do, stage))
        if held is not None:
            moving += back_projected(g - 1, *held, stage)
        if last:
            column = jnp.pad(ffn_part.T.astype(bf16), ((0, 0), (0, LANES - 1)))
            grad_out = weight_grads(atts, datts, after(column, stage), "out_weight_grad")
            moving += (grad_out,)
        stage = (dos[g], moving)
        if last:
            grad_out = lax.psum_scatter(
                after(grad_out, stage), "batch", scatter_dimension=0, tiled=True
            )
        moving = () if last else zr[g + 1].hop(stage)
        if held is not None:
            moving += dn[g - 1].hop(stage)
        grads, stats, one = attention_backed(g, stage)
        qk_part = qk_part + one
        stage = (stats, moving)
        if not last:
            stage = finish(zr[g + 1], stage)
        stats = summed_stats(stats, stage)
        if not last:
            moving = yr[-1].hop(stage)
            do, one = out_backed(g + 1, stage)
            ffn_part = ffn_part + one
            stage = (stats, do, moving)
        else:
            stage = (stats,)
        held = (grads, stats)
    g = seqs - 1
    stage = (stage, grad_gu)
    moving = dn[g - 1].hop(stage) if g else ()
    stage = (back_projected(g, *held, stage), moving)
    qk_rows = lax.dynamic_update_slice_in_dim(
        jnp.zeros((2, width), f32), qk_part, here * cols, 1
    )
    columns = jnp.pad(qk_rows.T.astype(bf16), ((0, 0), (0, LANES - 2)))
    moving = dn[g - 1].hop(stage) if g else ()
    grad_qkv = weight_grads(
        [one[-1] for one in kept], lows, after(columns, stage), "qkv_weight_grad"
    )
    stage = (grad_qkv, moving)
    grad_qkv = lax.psum_scatter(
        after(grad_qkv, stage), "batch", scatter_dimension=0, tiled=True
    )
    while len(left := [one for one in dn[::-1] + yr if one.at < n][:2]):
        stage = ([one.hop(stage) for one in left], grad_out)
    outs = [
        jnp.where(
            live[g], hiddens[g] + (yr[g].moved.astype(f32) + yr[g].parts[0].astype(f32)), 0.0
        ).astype(bf16)
        for g in range(seqs)
    ]
    token_grads = []
    for g in range(seqs):
        grad_n1 = dn[g].moved.astype(f32) + dn[g].parts[0].astype(f32)
        back, _ = norm_back(xs[g].astype(f32), gain_attn, grad_n1)
        token_grads.append(grad_hiddens[g] + back)
    summed = exchange(grad_out.reshape(n, own, -1)).astype(f32)
    grad_out = jnp.sum(summed[:, :, :width], axis=0)
    grad_ffn_gain = jnp.sum(summed[:, :, width], axis=0)
    summed = exchange(grad_qkv.reshape(n, own, -1)).astype(f32)
    grad_q, grad_k, grad_v = (
        jnp.swapaxes(summed[:, :, i * cols : (i + 1) * cols], 0, 1).reshape(own, width)
        for i in range(3)
    )
    gain_sums = jnp.sum(summed[:, :, 3 * cols :], axis=0)
    grad_attn_gain = (
        jnp.sum(
            w_query.astype(f32) * grad_q
            + w_key.astype(f32) * grad_k
            + w_value.astype(f32) * grad_v,
            axis=1,
        )
        / attn_gain.astype(f32)
    )
    shape = (batches, sequences, rows, width)
    return (
        jnp.stack(outs).reshape(shape),
        jnp.stack(token_grads).reshape(shape),
        grad_q,
        grad_k,
        grad_v,
        grad_out,
        grad_attn_gain,
        gain_sums[:, 0],
        gain_sums[:, 1],
        grad_ffn_gain,
        grad_gu[:experts].astype(f32),
        grad_gu[experts:].astype(f32),
        grad_down.astype(f32),
    )


def solution(mesh):
    rows = P(None, "batch", "ctx", None)
    flat = P(("batch", "ctx"), None)
    line = P(("batch", "ctx"))
    wide = P("ctx", "batch", None)
    tall = P("ctx", None, "batch")
    in_specs = (rows, P(None, "batch"), rows, rows) + (flat,) * 4 + (line,) * 4
    in_specs += (wide, wide, tall, rows)
    out_specs = (rows, rows) + (flat,) * 4 + (line,) * 4 + (wide, wide, tall)
    return jax.shard_map(body, mesh=mesh, in_specs=in_specs, out_specs=out_specs, check_vma=False)
```

```python
import jax
import jax.numpy as jnp
from jax import lax
from jax.experimental import pallas as pl
from jax.experimental.pallas import tpu as pltpu
from jax.sharding import PartitionSpec as P

HEAD_DIM = 128
EPS = 1e-05
THETA = 10000.0
MASKED = -1e30
LANES = 128
ROOM = 58 << 20
SLIM = 8

f32 = jnp.float32
bf16 = jnp.bfloat16


def dot(left, right, contract=((1,), (0,))):
    return lax.dot_general(left, right, (contract, ((), ())), preferred_element_type=f32)


def dot_nt(left, right):
    return dot(left, right, ((1,), (1,)))


def dot_tn(left, right):
    return dot(left, right, ((0,), (0,)))


def struct(shape, dtype):
    return jax.ShapeDtypeStruct(shape, dtype)


def cost(flops, *arrays):
    moved = sum(a.size * a.dtype.itemsize for a in arrays)
    return pl.CostEstimate(
        flops=int(flops) // SLIM, bytes_accessed=int(moved) // SLIM, transcendentals=0
    )


def whole(array):
    zeros = (0,) * len(array.shape)
    return pl.BlockSpec(array.shape, lambda *_: zeros, pipeline_mode=pl.Buffered(1))


def params(axes):
    return pltpu.CompilerParams(
        dimension_semantics=("arbitrary",) * axes, vmem_limit_bytes=ROOM
    )


def project(pieces, gain, weight, third, first):
    count, (rows, width) = len(pieces), pieces[0].shape
    total = count * rows
    step = 32
    part = min(total, 512)

    def kernel(*refs):
        xs, (gain_ref, w_ref), (n_ref, out_ref, ss_ref) = (
            refs[:count],
            refs[count : count + 2],
            refs[count + 2 :],
        )

        @pl.when(pl.program_id(0) == 0)
        def _():
            for i in range(count):

                @pl.loop(0, rows // step)
                def _(k):
                    v = xs[i][pl.ds(k * step, step), :].astype(f32)
                    r = lax.rsqrt(jnp.mean(v * v, axis=-1, keepdims=True) + EPS)
                    n_ref[pl.ds(i * rows + k * step, step), :] = (v * r * gain_ref[...]).astype(
                        bf16
                    )

        @pl.loop(0, total // part)
        def _(k):
            at = pl.ds(pl.multiple_of(k * part, part), part)
            p = dot(n_ref[at, :], w_ref[...])
            out_ref[at, :] = p
            ss_ref[0, at, :] = jnp.sum(p * p, axis=-1, keepdims=True)

    outs = (
        struct((total, width), bf16),
        struct((total, 3 * third), f32),
        struct((3, total, 1), f32),
    )
    return pl.pallas_call(
        kernel,
        grid=(3,),
        in_specs=[whole(x) for x in pieces]
        + [whole(gain), pl.BlockSpec((width, third), lambda t: (0, first + t))],
        out_specs=(
            pl.BlockSpec((total, width), lambda t: (0, 0)),
            pl.BlockSpec((total, third), lambda t: (0, t)),
            pl.BlockSpec((1, total, 1), lambda t: (t, 0, 0)),
        ),
        out_shape=outs,
        compiler_params=params(1),
        cost_estimate=cost(2 * total * width * 3 * third, *pieces, *outs[:2]),
        name="project",
    )(*pieces, gain, weight)


def turn(v, cosines, sines):
    return v * cosines + pltpu.roll(v, HEAD_DIM // 2, 1) * sines


def turn_back(v, cosines, sines):
    return v * cosines + pltpu.roll(v * sines, HEAD_DIM // 2, 1)


def allowed_of(start, rows, count, length):
    row = start + lax.broadcasted_iota(jnp.int32, (rows, count), 0)
    col = lax.broadcasted_iota(jnp.int32, (rows, count), 1)
    return (col <= row) & (col < length)


def attention_forward(place, lengths, qkv, inverse, gains, cosines, sines):
    n, seqs, rows, wide = qkv.shape
    cols = wide // 3
    heads = cols // HEAD_DIM
    span = n * rows
    scale = HEAD_DIM ** (-0.5)

    def kernel(place_ref, len_ref, qi, ki, vi, inv, gain_ref, cos_ref, sin_ref, q_o, k_o, v_o, att, lse):
        here = place_ref[0]
        length = len_ref[pl.program_id(0)]
        for p in range(n):
            j = lax.rem(here + (n - p), n)
            at = slice(p * rows, (p + 1) * rows)
            for which, (src, dst) in enumerate(((qi, q_o), (ki, k_o))):
                z = src[j, 0] * inv[which, j, 0] * gain_ref[which]
                dst[0, at, :] = turn(z, cos_ref[p], sin_ref[p]).astype(bf16)
            v_o[0, at, :] = vi[j, 0].astype(bf16)
        for p in range(n):
            at = slice(p * rows, (p + 1) * rows)
            kv = (p + 1) * rows
            s = dot_nt(q_o[0, at, :], k_o[0, :kv, :]) * scale
            s = jnp.where(allowed_of(p * rows, rows, kv, length), s, MASKED)
            peak = jnp.max(s, axis=-1, keepdims=True)
            e = jnp.exp(s - peak)
            z = jnp.sum(e, axis=-1, keepdims=True)
            att[p, 0] = dot((e / z).astype(bf16), v_o[0, :kv, :]).astype(bf16)
            lse[0, 0, at, :] = peak + jnp.log(z)

    def part(k):
        return pl.BlockSpec((n, 1, rows, HEAD_DIM), lambda g, h, *_: (0, g, 0, k * heads + h))

    line = pl.BlockSpec((1, span, HEAD_DIM), lambda g, h, *_: (g, 0, h))
    outs = (struct((seqs, span, cols), bf16),) * 3 + (
        struct((n, seqs, rows, cols), bf16),
        struct((seqs, heads, span, 1), f32),
    )
    return pl.pallas_call(
        kernel,
        grid_spec=pltpu.PrefetchScalarGridSpec(
            num_scalar_prefetch=2,
            grid=(seqs, heads),
            in_specs=[
                part(0),
                part(1),
                part(2),
                pl.BlockSpec((2, n, 1, rows, 1), lambda g, h, *_: (0, 0, g, 0, 0)),
                pl.BlockSpec((2, 1, HEAD_DIM), lambda g, h, *_: (0, 0, h)),
                whole(cosines),
                whole(sines),
            ],
            out_specs=(
                line,
                line,
                line,
                pl.BlockSpec((n, 1, rows, HEAD_DIM), lambda g, h, *_: (0, g, 0, h)),
                pl.BlockSpec((1, 1, span, 1), lambda g, h, *_: (g, h, 0, 0)),
            ),
        ),
        out_shape=outs,
        compiler_params=params(2),
        cost_estimate=cost(3 * seqs * heads * span * span * HEAD_DIM, qkv, *outs[:4]),
        name="attention",
    )(place, lengths, qkv, qkv, qkv, inverse, gains, cosines, sines)


def attention_backward(place, lengths, q, k, v, grad, lse, qkv, inverse, gains, cosines, sines):
    n, seqs, rows, wide = qkv.shape
    cols = wide // 3
    heads = cols // HEAD_DIM
    span = n * rows
    scale = HEAD_DIM ** (-0.5)

    def kernel(
        place_ref, len_ref, q_i, k_i, v_i, do_i, lse_i, qp_i, kp_i, inv, gain_ref, cos_ref, sin_ref,
        dq_o, dk_o, dv_o, st_o, dg_o, dq_s, dk_s, dv_s,
    ):
        here = place_ref[0]
        length = len_ref[pl.program_id(0)]
        dk_s[...] = jnp.zeros_like(dk_s)
        dv_s[...] = jnp.zeros_like(dv_s)
        for p in range(n):
            at = slice(p * rows, (p + 1) * rows)
            kv = (p + 1) * rows
            query, keys, values, do = q_i[0, at, :], k_i[0, :kv, :], v_i[0, :kv, :], do_i[p, 0]
            s = dot_nt(query, keys) * scale
            probs = jnp.where(
                allowed_of(p * rows, rows, kv, length), jnp.exp(s - lse_i[0, 0, at, :]), 0.0
            )
            dp = dot_nt(do, values)
            ds = (probs * (dp - jnp.sum(probs * dp, axis=-1, keepdims=True))).astype(bf16)
            dq_s[at, :] = dot(ds, keys) * scale
            dk_s[:kv, :] += dot_tn(ds, query)
            dv_s[:kv, :] += dot_tn(probs.astype(bf16), do)
        dk_s[...] = dk_s[...] * scale
        sums = [jnp.zeros((1, HEAD_DIM), f32)] * 2
        for p in range(n):
            j = lax.rem(here + (n - p), n)
            at = slice(p * rows, (p + 1) * rows)
            for which, (src, raw, dst) in enumerate(((dq_s, qp_i, dq_o), (dk_s, kp_i, dk_o))):
                dz = turn_back(src[at, :], cos_ref[p], sin_ref[p])
                moved = raw[j, 0] * dz
                dst[j, 0] = dz
                st_o[which, 0, 0, j] = jnp.sum(moved * gain_ref[which], axis=-1, keepdims=True)
                sums[which] += jnp.sum(moved * inv[which, j, 0], axis=0, keepdims=True)
            dv_o[j, 0] = dv_s[at, :].astype(bf16)
        for which in range(2):
            dg_o[which, 0] = sums[which]

    def part(i):
        return pl.BlockSpec((n, 1, rows, HEAD_DIM), lambda g, h, *_: (0, g, 0, i * heads + h))

    line = pl.BlockSpec((1, span, HEAD_DIM), lambda g, h, *_: (g, 0, h))
    block = part(0)
    outs = (
        struct((n, seqs, rows, cols), f32),
        struct((n, seqs, rows, cols), f32),
        struct((n, seqs, rows, cols), bf16),
        struct((2, seqs, heads, n, rows, 1), f32),
        struct((2, seqs, 1, cols), f32),
    )
    return pl.pallas_call(
        kernel,
        grid_spec=pltpu.PrefetchScalarGridSpec(
            num_scalar_prefetch=2,
            grid=(seqs, heads),
            in_specs=[
                line,
                line,
                line,
                block,
                pl.BlockSpec((1, 1, span, 1), lambda g, h, *_: (g, h, 0, 0)),
                part(0),
                part(1),
                pl.BlockSpec((2, n, 1, rows, 1), lambda g, h, *_: (0, 0, g, 0, 0)),
                pl.BlockSpec((2, 1, HEAD_DIM), lambda g, h, *_: (0, 0, h)),
                whole(cosines),
                whole(sines),
            ],
            out_specs=(
                block,
                block,
                block,
                pl.BlockSpec((2, 1, 1, n, rows, 1), lambda g, h, *_: (0, g, h, 0, 0, 0)),
                pl.BlockSpec((2, 1, 1, HEAD_DIM), lambda g, h, *_: (0, g, 0, h)),
            ),
            scratch_shapes=[pltpu.VMEM((span, HEAD_DIM), f32)] * 3,
        ),
        out_shape=outs,
        compiler_params=params(2),
        cost_estimate=cost(7 * seqs * heads * span * span * HEAD_DIM, qkv, *outs[:3]),
        name="attention_back",
    )(place, lengths, q, k, v, grad, lse, qkv, qkv, inverse, gains, cosines, sines)


def back_project(dzq, dzk, dv, qkv, inverse, stats, gains, weight, first, pieces):
    total, third = dv.shape
    width = weight.shape[0]
    rows = total // pieces
    tile = min(512, width)

    def kernel(dzq_i, dzk_i, dv_i, q_i, k_i, inv, st, gain_ref, wq, wk, wv, *rest):
        outs, low = rest[:pieces], rest[pieces]

        @pl.when(pl.program_id(0) == 0)
        def _():
            for which, (dz, raw) in enumerate(((dzq_i, q_i), (dzk_i, k_i))):
                r = inv[which]
                low[:, which * third : (which + 1) * third] = (
                    r * (gain_ref[which] * dz[...]) - raw[...] * (r * r * r * st[which])
                ).astype(bf16)
            low[:, 2 * third :] = dv_i[...]

        for i in range(pieces):
            at = slice(i * rows, (i + 1) * rows)
            outs[i][...] = (
                dot_nt(low[at, :third], wq[...])
                + dot_nt(low[at, third : 2 * third], wk[...])
                + dot_nt(low[at, 2 * third :], wv[...])
            ).astype(bf16)

    def raw(k):
        return pl.BlockSpec((total, third), lambda d: (0, k))

    def taken(k):
        return pl.BlockSpec((tile, third), lambda d: (d, first + k))

    outs = (struct((rows, width), bf16),) * pieces + (struct((total, 3 * third), bf16),)
    return pl.pallas_call(
        kernel,
        grid=(width // tile,),
        in_specs=[whole(dzq), whole(dzk), whole(dv), raw(0), raw(1)]
        + [whole(inverse), whole(stats), whole(gains), taken(0), taken(1), taken(2)],
        out_specs=(pl.BlockSpec((rows, tile), lambda d: (0, d)),) * pieces
        + (pl.BlockSpec((total, 3 * third), lambda d: (0, 0)),),
        out_shape=outs,
        compiler_params=params(1),
        cost_estimate=cost(6 * total * width * third, dzq, dzk, dv, *outs),
        name="back_project",
    )(dzq, dzk, dv, qkv, qkv, inverse, stats, gains, weight, weight, weight)


def out_project(att, rows_in, weight, gain):
    n, rows, cols = att.shape
    width = n * cols

    def kernel(a_i, x_i, w_i, gain_ref, h_o, n_o, acc):
        p = pl.program_id(0)

        @pl.when(p == 0)
        def _():
            acc[...] = x_i[...].astype(f32)

        acc[...] += dot(a_i[0], w_i[...])

        @pl.when(p == n - 1)
        def _():
            h = acc[...]
            h_o[...] = h
            r = lax.rsqrt(jnp.mean(h * h, axis=-1, keepdims=True) + EPS)
            n_o[...] = (h * r * gain_ref[...]).astype(bf16)

    outs = (struct((rows, width), f32), struct((rows, width), bf16))
    return pl.pallas_call(
        kernel,
        grid=(n,),
        in_specs=[
            pl.BlockSpec((1, rows, cols), lambda p: (p, 0, 0)),
            whole(rows_in),
            pl.BlockSpec((cols, width), lambda p: (p, 0)),
            whole(gain),
        ],
        out_specs=(pl.BlockSpec((rows, width), lambda p: (0, 0)),) * 2,
        out_shape=outs,
        scratch_shapes=[pltpu.VMEM((rows, width), f32)],
        compiler_params=params(1),
        cost_estimate=cost(2 * rows * width * width, att, rows_in, *outs),
        name="out_project",
    )(att, rows_in, weight, gain)


def out_back(moved, part, low, hidden, gain, weight, n):
    rows, width = hidden.shape
    cols = width // n

    def kernel(m_i, p_i, l_i, h_i, gain_ref, w_i, gh_o, da_o, do_o, fg_o):
        @pl.when(pl.program_id(0) == 0)
        def _():
            dz = m_i[...].astype(f32) + p_i[...].astype(f32)
            v = h_i[...]
            r = lax.rsqrt(jnp.mean(v * v, axis=-1, keepdims=True) + EPS)
            fg_o[...] = jnp.sum(dz * v * r, axis=0, keepdims=True)
            scaled = dz * gain_ref[...]
            inner = jnp.mean(v * scaled, axis=-1, keepdims=True)
            total = l_i[...].astype(f32) + r * scaled - v * (r * r * r * inner)
            gh_o[...] = total
            da_o[...] = total.astype(bf16)

        do_o[0] = dot_nt(da_o[...], w_i[...]).astype(bf16)

    outs = (
        struct((rows, width), f32),
        struct((rows, width), bf16),
        struct((n, rows, cols), bf16),
        struct((1, width), f32),
    )
    full = pl.BlockSpec((rows, width), lambda p: (0, 0))
    return pl.pallas_call(
        kernel,
        grid=(n,),
        in_specs=[whole(moved), whole(part), whole(low), whole(hidden), whole(gain)]
        + [pl.BlockSpec((cols, width), lambda p: (p, 0))],
        out_specs=(
            full,
            full,
            pl.BlockSpec((1, rows, cols), lambda p: (p, 0, 0)),
            pl.BlockSpec((1, width), lambda p: (0, 0)),
        ),
        out_shape=outs,
        compiler_params=params(1),
        cost_estimate=cost(2 * rows * width * width, hidden, *outs),
        name="out_back",
    )(moved, part, low, hidden, gain, weight)


def weight_grads(lefts, rights, columns, name):
    count = len(lefts)
    total, wide = rights[0].shape
    folded = len(lefts[0].shape) == 3
    width = columns.shape[0]
    tile = lefts[0].shape[2] if folded else min(512, width)

    def kernel(*refs):
        ls, rs, (column_ref, o) = refs[:count], refs[count : 2 * count], refs[2 * count :]
        o[:, :wide] = sum(
            dot_tn(ls[g][0] if folded else ls[g][...], rs[g][...]) for g in range(count)
        ).astype(bf16)
        o[:, wide:] = column_ref[...]

    if folded:
        left = pl.BlockSpec((1, total, tile), lambda p: (p, 0, 0))
    else:
        left = pl.BlockSpec((total, tile), lambda p: (0, p))
    out = struct((width, wide + LANES), bf16)
    return pl.pallas_call(
        kernel,
        grid=(width // tile,),
        in_specs=[left] * count
        + [whole(x) for x in rights]
        + [pl.BlockSpec((tile, LANES), lambda p: (p, 0))],
        out_specs=pl.BlockSpec((tile, wide + LANES), lambda p: (p, 0)),
        out_shape=out,
        compiler_params=params(1),
        cost_estimate=cost(2 * count * total * width * wide, *lefts, *rights, out),
        name=name,
    )(*lefts, *rights, columns)


def picks(rank_ref, nb, cap):
    row = rank_ref[0, nb : nb + 1, :]
    return lax.broadcasted_iota(jnp.int32, (cap, row.shape[1]), 0) == row


def slot_weight(hot, coef_ref, nb):
    return jnp.sum(jnp.where(hot, coef_ref[0, nb : nb + 1, :], 0.0), axis=-1, keepdims=True)


def in_place(arrays, given):
    if arrays is None:
        return (), [], {}
    return (
        tuple(arrays),
        [pl.BlockSpec(memory_space=pl.ANY)] * len(arrays),
        {given + i: i for i in range(len(arrays))},
    )


def expert_forward(pieces, rank, gate_up, cap, start, stop, begun=None):
    experts, blocks, rows = rank.shape
    width, hidden = gate_up.shape[1:]
    slots = blocks * cap
    tile = min(256, hidden)
    more, more_specs, aliases = in_place(begun, blocks + 3)

    def kernel(*refs):
        xs, (rank_ref, wg, wu), (x_o, g_o, u_o, a_o) = (
            refs[:blocks],
            refs[blocks : blocks + 3],
            refs[-4:],
        )

        @pl.when(pl.program_id(1) == 0)
        def _():
            for nb in range(blocks):
                hot = picks(rank_ref, nb, cap).astype(bf16)
                x_o[0, nb * cap : (nb + 1) * cap, :] = dot(hot, xs[nb][...]).astype(bf16)

        x = x_o[0]
        gate = dot(x, wg[0])
        upper = dot(x, wu[0])
        s = jax.nn.sigmoid(gate)
        silu = gate * s
        g_o[0] = (upper * (s + silu * (1.0 - s))).astype(bf16)
        u_o[0] = silu.astype(bf16)
        a_o[0] = (silu * upper).astype(bf16)

    tiled = pl.BlockSpec((1, slots, tile), lambda e, f: (start + e, 0, f))
    outs = (struct((experts, slots, width), bf16),) + (struct((experts, slots, hidden), bf16),) * 3
    return pl.pallas_call(
        kernel,
        grid=(stop - start, hidden // tile),
        in_specs=[whole(x) for x in pieces]
        + [
            pl.BlockSpec((1, blocks, rows), lambda e, f: (start + e, 0, 0)),
            pl.BlockSpec((1, width, tile), lambda e, f: (start + e, 0, f)),
            pl.BlockSpec((1, width, tile), lambda e, f: (experts + start + e, 0, f)),
        ]
        + more_specs,
        out_specs=(
            pl.BlockSpec((1, slots, width), lambda e, f: (start + e, 0, 0)),
            tiled,
            tiled,
            tiled,
        ),
        out_shape=outs,
        input_output_aliases=aliases,
        compiler_params=params(2),
        cost_estimate=cost(4 * (stop - start) * slots * width * hidden, *pieces),
        name="expert_forward",
    )(*pieces, rank, gate_up, gate_up, *more)


def expert_output(active, rank, coef, down, cap):
    experts, blocks, rows = rank.shape
    hidden, width = down.shape[1:]
    slots = blocks * cap
    tile = min(512, width)

    def kernel(a_i, rank_ref, coef_ref, wd, *rest):
        outs, acc = rest[:blocks], rest[blocks]
        e = pl.program_id(1)

        @pl.when(e == 0)
        def _():
            acc[...] = jnp.zeros_like(acc)

        y = dot(a_i[0], wd[0])
        for nb in range(blocks):
            hot = picks(rank_ref, nb, cap)
            weighed = y[nb * cap : (nb + 1) * cap, :] * slot_weight(hot, coef_ref, nb)
            acc[nb] += dot_tn(hot.astype(bf16), weighed.astype(bf16))

        @pl.when(e == experts - 1)
        def _():
            for nb in range(blocks):
                outs[nb][...] = acc[nb].astype(bf16)

    table = pl.BlockSpec((1, blocks, rows), lambda d, e: (e, 0, 0))
    outs = (struct((rows, width), bf16),) * blocks
    return pl.pallas_call(
        kernel,
        grid=(width // tile, experts),
        in_specs=[
            pl.BlockSpec((1, slots, hidden), lambda d, e: (e, 0, 0)),
            table,
            table,
            pl.BlockSpec((1, hidden, tile), lambda d, e: (e, 0, d)),
        ],
        out_specs=(pl.BlockSpec((rows, tile), lambda d, e: (0, d)),) * blocks,
        out_shape=outs,
        scratch_shapes=[pltpu.VMEM((blocks, rows, tile), f32)],
        compiler_params=params(2),
        cost_estimate=cost(2 * experts * slots * width * hidden, active, down, *outs),
        name="expert_output",
    )(active, rank, coef, down)


def expert_backward(pieces, rank, coef, down, gate, upper, active, cap):
    experts, blocks, rows = rank.shape
    hidden, width = down.shape[1:]
    slots = blocks * cap
    tile = min(256, hidden)

    def kernel(*refs):
        ds, (rank_ref, coef_ref, wd, g_i, u_i, a_i), (dg_o, du_o, dw_o, dy) = (
            refs[:blocks],
            refs[blocks : blocks + 6],
            refs[blocks + 6 :],
        )

        @pl.when(pl.program_id(1) == 0)
        def _():
            for nb in range(blocks):
                hot = picks(rank_ref, nb, cap)
                picked = dot(hot.astype(bf16), ds[nb][...])
                dy[nb * cap : (nb + 1) * cap, :] = (
                    picked * slot_weight(hot, coef_ref, nb)
                ).astype(bf16)

        da = dot_nt(dy[...], wd[0])
        du_o[0] = (da * u_i[0].astype(f32)).astype(bf16)
        dg_o[0] = (da * g_i[0].astype(f32)).astype(bf16)

        dw_o[0] = dot_tn(a_i[0], dy[...]).astype(bf16)

    table = pl.BlockSpec((1, blocks, rows), lambda e, f: (e, 0, 0))
    tiled = pl.BlockSpec((1, slots, tile), lambda e, f: (e, 0, f))
    line = pl.BlockSpec((1, tile, width), lambda e, f: (e, f, 0))
    outs = (struct((experts, slots, hidden), bf16),) * 2 + (struct((experts, hidden, width), bf16),)
    return pl.pallas_call(
        kernel,
        grid=(experts, hidden // tile),
        in_specs=[whole(x) for x in pieces] + [table, table, line, tiled, tiled, tiled],
        out_specs=(tiled, tiled, line),
        out_shape=outs,
        scratch_shapes=[pltpu.VMEM((slots, width), bf16)],
        compiler_params=params(2),
        cost_estimate=cost(
            4 * experts * slots * width * hidden, *pieces, down, gate, upper, active, *outs
        ),
        name="expert_backward",
    )(*pieces, rank, coef, down, gate, upper, active)


def expert_input_grad(dgate, dupper, rank, gate_up, cap, g, seqs):
    blocks, rows = rank.shape[1:]
    width, hidden = gate_up.shape[1:]
    experts = gate_up.shape[0] // 2
    slots = blocks * cap
    tile = min(1024, width)

    def kernel(dg_i, du_i, rank_ref, wg, wu, *rest):
        outs, acc = rest[:blocks], rest[blocks]
        e = pl.program_id(1)

        @pl.when(e == 0)
        def _():
            acc[...] = jnp.zeros_like(acc)

        dx = (dot_nt(dg_i[0], wg[0]) + dot_nt(du_i[0], wu[0])).astype(bf16)
        for nb in range(blocks):
            hot = picks(rank_ref, nb, cap).astype(bf16)
            acc[nb] += dot_tn(hot, dx[nb * cap : (nb + 1) * cap, :])

        @pl.when(e == experts - 1)
        def _():
            for nb in range(blocks):
                outs[nb][...] = acc[nb].astype(bf16)

    line = pl.BlockSpec((1, slots, hidden), lambda d, e: (e, g, 0))
    outs = (struct((rows, width), bf16),) * blocks
    return pl.pallas_call(
        kernel,
        grid=(width // tile, experts),
        in_specs=[
            line,
            line,
            pl.BlockSpec((1, blocks, rows), lambda d, e: (e * seqs + g, 0, 0)),
            pl.BlockSpec((1, tile, hidden), lambda d, e: (e, d, 0)),
            pl.BlockSpec((1, tile, hidden), lambda d, e: (experts + e, d, 0)),
        ],
        out_specs=(pl.BlockSpec((rows, tile), lambda d, e: (0, d)),) * blocks,
        out_shape=outs,
        scratch_shapes=[pltpu.VMEM((blocks, rows, tile), f32)],
        compiler_params=params(2),
        cost_estimate=cost(4 * experts * slots * width * hidden, gate_up, *outs),
        name="expert_input_grad",
    )(dgate, dupper, rank, gate_up, gate_up)


def expert_weight_grad(x, dgate, dupper, start, stop, begun=None):
    experts, slots, width = x.shape
    hidden = dgate.shape[2]
    tile = min(512, width)
    more, more_specs, aliases = in_place(begun, 3)

    def kernel(x_i, dg_i, du_i, *rest):
        o = rest[-1]
        o[0, 0] = dot_tn(x_i[0], dg_i[0]).astype(bf16)
        o[1, 0] = dot_tn(x_i[0], du_i[0]).astype(bf16)

    line = pl.BlockSpec((1, slots, hidden), lambda e, d: (start + e, 0, 0))
    return pl.pallas_call(
        kernel,
        grid=(stop - start, width // tile),
        in_specs=[pl.BlockSpec((1, slots, tile), lambda e, d: (start + e, 0, d)), line, line]
        + more_specs,
        out_specs=(pl.BlockSpec((2, 1, tile, hidden), lambda e, d: (0, start + e, d, 0)),),
        out_shape=(struct((2, experts, width, hidden), bf16),),
        input_output_aliases=aliases,
        compiler_params=params(2),
        cost_estimate=cost(4 * (stop - start) * slots * width * hidden, x),
        name="expert_weight_grad",
    )(x, dgate, dupper, *more)


def tables(positions):
    half = HEAD_DIM // 2
    inverse = THETA ** (-(jnp.arange(half, dtype=f32) * 2.0) / HEAD_DIM)
    angle = positions.astype(f32)[:, None] * inverse[None, :]
    cosines, sines = jnp.cos(angle), jnp.sin(angle)
    return (
        jnp.concatenate([cosines, cosines], axis=-1),
        jnp.concatenate([-sines, sines], axis=-1),
    )


def norm_back(v, gain, dz):
    r = lax.rsqrt(jnp.mean(v * v, axis=-1, keepdims=True) + EPS)
    moved = dz * gain
    return r * moved - v * (r * r * r) * jnp.mean(v * moved, axis=-1, keepdims=True), dz * v * r


def body(
    tokens, lengths, expert_ids, route_levels, w_query, w_key, w_value, w_out,
    attn_gain, query_gain, key_gain, ffn_gain, w_gate, w_up, w_down, cotangent,
):
    batches, sequences, rows, width = tokens.shape
    top = expert_ids.shape[-1]
    experts = w_gate.shape[0]
    n = lax.axis_size("ctx")
    here = lax.axis_index("ctx")
    seqs = batches * sequences
    cols = width // n
    own = w_query.shape[0]
    cap = rows * top * 5 // (4 * experts * n)
    cap = -(-cap // 16) * 16
    blocks = n * seqs
    up = [(i, (i + 1) % n) for i in range(n)]
    place = here.reshape(1).astype(jnp.int32)

    def after(value, *others):
        return lax.optimization_barrier((value, others))[0]

    class Ring:
        def __init__(self, piece):
            self.held = [piece]

        def hop(self, prev):
            if len(self.held) == n:
                return ()
            self.held.append(lax.ppermute(after(self.held[-1], prev), "ctx", up))
            return (self.held[-1],)

    class Sum:
        def __init__(self, parts):
            self.parts = parts
            self.moved = None
            self.at = 1

        def hop(self, prev):
            if self.at == n:
                return ()
            part = after(self.parts[self.at], prev)
            if self.moved is not None:
                part = (after(self.moved, prev).astype(f32) + part.astype(f32)).astype(bf16)
            self.moved = lax.ppermute(part, "ctx", up)
            self.at += 1
            return (self.moved,)

    def finish(ring, prev):
        while got := ring.hop(prev):
            prev = (prev, got)
        return prev

    def direct(x):
        return [x] + [
            lax.ppermute(x, "ctx", [(i, (i + k) % n) for i in range(n)]) for k in range(1, n)
        ]

    def ctx_sum(x):
        held = direct(x)
        return sum((jnp.roll(held[k], k, axis=0) for k in range(1, n)), held[0])

    def exchange(x):
        return lax.all_to_all(x, "ctx", split_axis=0, concat_axis=0, tiled=True)

    gains = jnp.stack([attn_gain, query_gain, key_gain, ffn_gain], axis=1)
    gains = jnp.pad(gains, ((0, 0), (0, LANES - 4)))
    sent = jnp.stack(
        [
            jnp.swapaxes(expert_ids.reshape(seqs, rows, top), 1, 2),
            jnp.swapaxes(route_levels.reshape(seqs, rows, top), 1, 2),
        ]
    )
    sent = sent.astype(bf16).reshape(own, -1)
    extra = sent.shape[1]
    mine = jnp.concatenate(
        [jnp.broadcast_to(w_out[None], (n, own, width))]
        + [jnp.swapaxes(w.reshape(own, n, cols), 0, 1) for w in (w_query, w_key, w_value)]
        + [jnp.broadcast_to(one[None], (n, *one.shape)) for one in (gains, sent)],
        axis=2,
    )
    mine = exchange(mine)
    routes = mine[:, :, -extra:].reshape(n, 2, seqs, top, rows)
    order = lax.rem(here + n - jnp.arange(n, dtype=jnp.int32), n)
    routes = jnp.take(routes, order, axis=0)
    mine = mine.reshape(n * own, -1)
    att_w = lax.all_gather(mine, "batch", axis=0, tiled=True)
    all_gains = att_w[:, width + 3 * cols : width + 3 * cols + 4].astype(f32).T
    gain_attn, gain_ffn = all_gains[0], all_gains[3]
    qk_gains = lax.dynamic_slice_in_dim(all_gains[1:3], here * cols, cols, 1).reshape(2, 1, cols)

    xs = tokens.reshape(seqs, rows, width)
    span_len = lengths.reshape(seqs)
    local_pos = here * rows + jnp.arange(rows, dtype=jnp.int32)
    live = (local_pos[None, :] < span_len[:, None])[:, :, None]
    grad_low = jnp.where(live, cotangent.reshape(seqs, rows, width), jnp.zeros((), bf16))
    def slots_of(routes):
        chosen = jnp.swapaxes(routes[:, 0], 0, 1).reshape(blocks, top, rows).astype(jnp.int32)
        levels = jnp.swapaxes(routes[:, 1], 0, 1).reshape(blocks, top, rows).astype(f32)
        share = levels / jnp.sum(levels, axis=1, keepdims=True)
        owned = here * experts + jnp.arange(experts, dtype=jnp.int32)
        hit = chosen[None] == owned[:, None, None, None]
        named = jnp.any(hit, axis=2)
        coef = jnp.sum(jnp.where(hit, share[None], 0.0), axis=2)
        at = jnp.arange(rows, dtype=jnp.int32)
        upto = (at[:, None] <= at[None, :]).astype(bf16)
        count = jnp.dot(
            named.astype(bf16).reshape(experts * blocks, rows), upto, preferred_element_type=f32
        )
        count = count.reshape(experts, blocks, rows).astype(jnp.int32)
        return jnp.where(named, count - 1, -1), coef

    cosines, sines = tables(jnp.arange(n * rows, dtype=jnp.int32))
    cosines = cosines.reshape(n, rows, HEAD_DIM)
    sines = sines.reshape(n, rows, HEAD_DIM)
    kept, atts, hiddens = [None] * seqs, [None] * seqs, [None] * seqs
    xr = [Ring(xs[g]) for g in range(seqs)]
    nr = [None] * seqs

    def projected(g, prev):
        normed, qkv, squares = project(
            [after(xr[g].held[0], prev)] + xr[g].held[1:], gain_attn[None, :], att_w, cols, n
        )
        return normed, qkv.reshape(n, 1, rows, 3 * cols), squares

    def scales(squares, prev):
        squares = jnp.swapaxes(squares[:2].reshape(2, n, rows), 0, 1)
        inverse = lax.rsqrt(ctx_sum(after(squares, prev)) / width + EPS)
        return jnp.swapaxes(inverse, 0, 1).reshape(2, n, 1, rows, 1)

    def attended(g, normed, qkv, inverse, prev):
        q, k, v, att, lse = attention_forward(
            place, span_len[g : g + 1], qkv, after(inverse, prev), qk_gains, cosines, sines
        )
        kept[g] = (q, k, v, lse, qkv, inverse, normed)
        return att.reshape(n, rows, cols)

    def out_projected(g, prev):
        hiddens[g], n2 = out_project(
            after(atts[g], prev), xs[g], att_w, gain_ffn[None, :]
        )
        nr[g] = Ring(n2)
        return (n2,)

    stage = (xr[0].hop(()), mine)
    rank, coef = slots_of(after(routes, stage))
    stage = xr[0].hop(stage)
    gate_up = lax.all_gather(
        jnp.concatenate([after(w_gate, stage), w_up], axis=0), "batch", axis=1, tiled=True
    )
    down = lax.all_gather(after(w_down, stage), "batch", axis=2, tiled=True)
    stage = finish(xr[0], stage)
    first = None
    for g in range(seqs):
        last = g + 1 == seqs
        if not last:
            stage = xr[g + 1].hop(stage)
            moving = xr[g + 1].hop(stage)
        else:
            moving = ()
        if first is not None:
            moving = (exchange(after(first, stage)),)
        normed, qkv, squares = projected(g, stage)
        stage = (squares, moving)
        inverse = scales(squares, stage)
        if first is not None:
            atts[g - 1] = moving[0]
            stage = (inverse, out_projected(g - 1, stage))
        else:
            stage = (inverse,)
        moving = () if last else xr[g + 1].hop(stage)
        if first is not None:
            moving += nr[g - 1].hop(stage)
        att = attended(g, normed, qkv, inverse, stage)
        stage = (att, moving)
        if not last:
            stage = finish(xr[g + 1], stage)
        first = att
    g = seqs - 1
    moving = nr[g - 1].hop(stage) if g else ()
    atts[g] = exchange(after(first, stage))
    stage = (atts[g], moving)
    moving = nr[g - 1].hop(stage) if g else ()
    stage = (out_projected(g, stage), moving)
    for one in nr:
        stage = finish(one, stage)

    grad_hiddens, datts, dos = [None] * seqs, [None] * seqs, [None] * seqs
    lows, dn = [None] * seqs, [None] * seqs
    qk_part = jnp.zeros((2, cols), f32)

    def out_backed(g, prev):
        grad_hiddens[g], datts[g], do, one = out_back(
            after(zr[g].moved, prev), dx_parts[g][0], grad_low[g], hiddens[g], gain_ffn[None, :],
            att_w, n,
        )
        return do, one

    def attention_backed(g, prev):
        q, k, v, lse, qkv, inverse, _ = kept[g]
        *grads, stats, qk_one = attention_backward(
            place, span_len[g : g + 1], after(q, prev), k, v, dos[g].reshape(n, 1, rows, cols),
            lse, qkv, inverse, qk_gains, cosines, sines,
        )
        stats = jnp.sum(stats.reshape(2, cols // HEAD_DIM, n, rows), axis=1)
        return grads, jnp.swapaxes(stats, 0, 1), qk_one.reshape(2, cols)

    def summed_stats(stats, prev):
        return jnp.swapaxes(ctx_sum(after(stats, prev)), 0, 1) / width

    def back_projected(g, grads, stats, prev):
        qkv, inverse = kept[g][4:6]
        *dn1, lows[g] = back_project(
            *(one.reshape(n * rows, cols) for one in grads), qkv.reshape(n * rows, 3 * cols),
            inverse.reshape(2, n * rows, 1), after(stats, prev).reshape(2, n * rows, 1), qk_gains,
            att_w, n, n,
        )
        dn[g] = Sum(dn1)
        return (lows[g],)

    dr = [Ring(grad_low[g]) for g in range(seqs)]
    n_pieces = [nr[g].held[j] for g in range(seqs) for j in range(n)]
    held = None
    for start, stop in ((0, experts // 2), (experts // 2, experts)):
        moving = [one.hop(stage) for one in dr]
        held = expert_forward(
            n_pieces, after(rank, stage), gate_up, cap, start, stop, held
        )
        stage = (held, moving)
    slots_x, by_gate, by_upper, active = held
    moving = [one.hop(stage) for one in dr]
    y_parts = expert_output(after(active, stage), rank, coef, down, cap)
    stage = (y_parts, moving)
    stage = [finish(one, stage) for one in dr] or stage
    grad_pieces = [dr[g].held[j] for g in range(seqs) for j in range(n)]
    yr = [Sum(y_parts[g * n : (g + 1) * n]) for g in range(seqs)]
    moving = [one.hop(stage) for one in yr]
    dgate, dupper, grad_down = expert_backward(
        grad_pieces, after(rank, stage), coef, down, by_gate, by_upper, active, cap
    )
    stage = (dgate, moving)
    grad_down = lax.psum_scatter(
        after(grad_down, stage), "batch", scatter_dimension=2, tiled=True
    )
    rank_rows = rank.reshape(experts * seqs, n, rows)

    def input_grad(g, prev):
        dx_parts.append(
            expert_input_grad(after(dgate, prev), dupper, rank_rows, gate_up, cap, g, seqs)
        )
        zr.append(Sum(dx_parts[g]))
        return dx_parts[g]

    zr, dx_parts = [], []
    moving = [one.hop(stage) for one in yr]
    stage = (input_grad(0, stage), moving)
    held = None
    for start, stop in ((0, experts // 2), (experts // 2, experts)):
        moving = zr[0].hop(stage)
        held = expert_weight_grad(slots_x, after(dgate, stage), dupper, start, stop, held)
        stage = (held, moving)
    gu_local = held[0].reshape(2 * experts, width, -1)
    grad_gu = lax.psum_scatter(
        after(gu_local, stage), "batch", scatter_dimension=1, tiled=True
    )
    for g in range(1, seqs):
        moving = (zr[0].hop(stage), yr[0].hop(stage))
        stage = (input_grad(g, stage), moving)
    stage = (finish(zr[0], stage), grad_down)
    moving = zr[1].hop(stage) if seqs > 1 else ()
    do, ffn_part = out_backed(0, stage)
    stage = (do, moving)

    held = None
    for g in range(seqs):
        last = g + 1 == seqs
        moving = () if last else zr[g + 1].hop(stage)
        dos[g] = exchange(after(do, stage))
        if held is not None:
            moving += back_projected(g - 1, *held, stage)
        if last:
            column = jnp.pad(ffn_part.T.astype(bf16), ((0, 0), (0, LANES - 1)))
            grad_out = weight_grads(atts, datts, after(column, stage), "out_weight_grad")
            moving += (grad_out,)
        stage = (dos[g], moving)
        if last:
            grad_out = lax.psum_scatter(
                after(grad_out, stage), "batch", scatter_dimension=0, tiled=True
            )
        moving = () if last else zr[g + 1].hop(stage)
        if held is not None:
            moving += dn[g - 1].hop(stage)
        grads, stats, one = attention_backed(g, stage)
        qk_part = qk_part + one
        stage = (stats, moving)
        if not last:
            stage = finish(zr[g + 1], stage)
        stats = summed_stats(stats, stage)
        if not last:
            moving = yr[-1].hop(stage)
            do, one = out_backed(g + 1, stage)
            ffn_part = ffn_part + one
            stage = (stats, do, moving)
        else:
            stage = (stats,)
        held = (grads, stats)
    g = seqs - 1
    stage = (stage, grad_gu)
    moving = dn[g - 1].hop(stage) if g else ()
    stage = (back_projected(g, *held, stage), moving)
    qk_rows = lax.dynamic_update_slice_in_dim(
        jnp.zeros((2, width), f32), qk_part, here * cols, 1
    )
    columns = jnp.pad(qk_rows.T.astype(bf16), ((0, 0), (0, LANES - 2)))
    moving = dn[g - 1].hop(stage) if g else ()
    grad_qkv = weight_grads(
        [one[-1] for one in kept], lows, after(columns, stage), "qkv_weight_grad"
    )
    stage = (grad_qkv, moving)
    grad_qkv = lax.psum_scatter(
        after(grad_qkv, stage), "batch", scatter_dimension=0, tiled=True
    )
    while len(left := [one for one in dn[::-1] + yr if one.at < n][:2]):
        stage = ([one.hop(stage) for one in left], grad_out)
    outs = [
        jnp.where(
            live[g], hiddens[g] + (yr[g].moved.astype(f32) + yr[g].parts[0].astype(f32)), 0.0
        ).astype(bf16)
        for g in range(seqs)
    ]
    token_grads = []
    for g in range(seqs):
        grad_n1 = dn[g].moved.astype(f32) + dn[g].parts[0].astype(f32)
        back, _ = norm_back(xs[g].astype(f32), gain_attn, grad_n1)
        token_grads.append(grad_hiddens[g] + back)
    grad_out, summed = lax.optimization_barrier(
        (exchange(grad_out.reshape(n, own, -1)), exchange(grad_qkv.reshape(n, own, -1)))
    )
    grad_out, summed = grad_out.astype(f32), summed.astype(f32)
    grad_ffn_gain = jnp.sum(grad_out[:, :, width], axis=0)
    grad_out = jnp.sum(grad_out[:, :, :width], axis=0)
    grad_q, grad_k, grad_v = (
        jnp.swapaxes(summed[:, :, i * cols : (i + 1) * cols], 0, 1).reshape(own, width)
        for i in range(3)
    )
    gain_sums = jnp.sum(summed[:, :, 3 * cols :], axis=0)
    grad_attn_gain = (
        jnp.sum(
            w_query.astype(f32) * grad_q
            + w_key.astype(f32) * grad_k
            + w_value.astype(f32) * grad_v,
            axis=1,
        )
        / attn_gain.astype(f32)
    )
    shape = (batches, sequences, rows, width)
    return (
        jnp.stack(outs).reshape(shape),
        jnp.stack(token_grads).reshape(shape),
        grad_q,
        grad_k,
        grad_v,
        grad_out,
        grad_attn_gain,
        gain_sums[:, 0],
        gain_sums[:, 1],
        grad_ffn_gain,
        grad_gu[:experts].astype(f32),
        grad_gu[experts:].astype(f32),
        grad_down.astype(f32),
    )


def solution(mesh):
    rows = P(None, "batch", "ctx", None)
    flat = P(("batch", "ctx"), None)
    line = P(("batch", "ctx"))
    wide = P("ctx", "batch", None)
    tall = P("ctx", None, "batch")
    in_specs = (rows, P(None, "batch"), rows, rows) + (flat,) * 4 + (line,) * 4
    in_specs += (wide, wide, tall, rows)
    out_specs = (rows, rows) + (flat,) * 4 + (line,) * 4 + (wide, wide, tall)
    return jax.shard_map(body, mesh=mesh, in_specs=in_specs, out_specs=out_specs, check_vma=False)
```

```python
import jax
import jax.numpy as jnp
from jax import lax
from jax.experimental import pallas as pl
from jax.experimental.pallas import tpu as pltpu
from jax.sharding import PartitionSpec as P

HEAD_DIM = 128
EPS = 1e-05
THETA = 10000.0
MASKED = -1e30
LANES = 128
ROOM = 58 << 20
SLIM = 8

f32 = jnp.float32
bf16 = jnp.bfloat16


def dot(left, right, contract=((1,), (0,))):
    return lax.dot_general(left, right, (contract, ((), ())), preferred_element_type=f32)


def dot_nt(left, right):
    return dot(left, right, ((1,), (1,)))


def dot_tn(left, right):
    return dot(left, right, ((0,), (0,)))


def struct(shape, dtype):
    return jax.ShapeDtypeStruct(shape, dtype)


def cost(flops, *arrays):
    moved = sum(a.size * a.dtype.itemsize for a in arrays)
    return pl.CostEstimate(
        flops=int(flops) // SLIM, bytes_accessed=int(moved) // SLIM, transcendentals=0
    )


def whole(array):
    zeros = (0,) * len(array.shape)
    return pl.BlockSpec(array.shape, lambda *_: zeros, pipeline_mode=pl.Buffered(1))


def params(axes):
    return pltpu.CompilerParams(
        dimension_semantics=("arbitrary",) * axes, vmem_limit_bytes=ROOM
    )


def project(pieces, gain, weight, third, first):
    count, (rows, width) = len(pieces), pieces[0].shape
    total = count * rows
    step = 32
    part = min(total, 512)

    def kernel(*refs):
        xs, (gain_ref, w_ref), (n_ref, out_ref, ss_ref) = (
            refs[:count],
            refs[count : count + 2],
            refs[count + 2 :],
        )

        @pl.when(pl.program_id(0) == 0)
        def _():
            for i in range(count):

                @pl.loop(0, rows // step)
                def _(k):
                    v = xs[i][pl.ds(k * step, step), :].astype(f32)
                    r = lax.rsqrt(jnp.mean(v * v, axis=-1, keepdims=True) + EPS)
                    n_ref[pl.ds(i * rows + k * step, step), :] = (v * r * gain_ref[...]).astype(
                        bf16
                    )

        @pl.loop(0, total // part)
        def _(k):
            at = pl.ds(pl.multiple_of(k * part, part), part)
            p = dot(n_ref[at, :], w_ref[...])
            out_ref[at, :] = p
            ss_ref[0, at, :] = jnp.sum(p * p, axis=-1, keepdims=True)

    outs = (
        struct((total, width), bf16),
        struct((total, 3 * third), f32),
        struct((3, total, 1), f32),
    )
    return pl.pallas_call(
        kernel,
        grid=(3,),
        in_specs=[whole(x) for x in pieces]
        + [whole(gain), pl.BlockSpec((width, third), lambda t: (0, first + t))],
        out_specs=(
            pl.BlockSpec((total, width), lambda t: (0, 0)),
            pl.BlockSpec((total, third), lambda t: (0, t)),
            pl.BlockSpec((1, total, 1), lambda t: (t, 0, 0)),
        ),
        out_shape=outs,
        compiler_params=params(1),
        cost_estimate=cost(2 * total * width * 3 * third, *pieces, *outs[:2]),
        name="project",
    )(*pieces, gain, weight)


def turn(v, cosines, sines):
    return v * cosines + pltpu.roll(v, HEAD_DIM // 2, 1) * sines


def turn_back(v, cosines, sines):
    return v * cosines + pltpu.roll(v * sines, HEAD_DIM // 2, 1)


def allowed_of(start, rows, count, length):
    row = start + lax.broadcasted_iota(jnp.int32, (rows, count), 0)
    col = lax.broadcasted_iota(jnp.int32, (rows, count), 1)
    return (col <= row) & (col < length)


def attention_forward(place, lengths, qkv, inverse, gains, cosines, sines):
    n, seqs, rows, wide = qkv.shape
    cols = wide // 3
    heads = cols // HEAD_DIM
    span = n * rows
    scale = HEAD_DIM ** (-0.5)

    def kernel(place_ref, len_ref, qi, ki, vi, inv, gain_ref, cos_ref, sin_ref, q_o, k_o, v_o, att, lse):
        here = place_ref[0]
        length = len_ref[pl.program_id(0)]
        for p in range(n):
            j = lax.rem(here + (n - p), n)
            at = slice(p * rows, (p + 1) * rows)
            for which, (src, dst) in enumerate(((qi, q_o), (ki, k_o))):
                z = src[j, 0] * inv[which, j, 0] * gain_ref[which]
                dst[0, at, :] = turn(z, cos_ref[p], sin_ref[p]).astype(bf16)
            v_o[0, at, :] = vi[j, 0].astype(bf16)
        for p in range(n):
            at = slice(p * rows, (p + 1) * rows)
            kv = (p + 1) * rows
            s = dot_nt(q_o[0, at, :], k_o[0, :kv, :]) * scale
            s = jnp.where(allowed_of(p * rows, rows, kv, length), s, MASKED)
            peak = jnp.max(s, axis=-1, keepdims=True)
            e = jnp.exp(s - peak)
            z = jnp.sum(e, axis=-1, keepdims=True)
            att[p, 0] = dot((e / z).astype(bf16), v_o[0, :kv, :]).astype(bf16)
            lse[0, 0, at, :] = peak + jnp.log(z)

    def part(k):
        return pl.BlockSpec((n, 1, rows, HEAD_DIM), lambda g, h, *_: (0, g, 0, k * heads + h))

    line = pl.BlockSpec((1, span, HEAD_DIM), lambda g, h, *_: (g, 0, h))
    outs = (struct((seqs, span, cols), bf16),) * 3 + (
        struct((n, seqs, rows, cols), bf16),
        struct((seqs, heads, span, 1), f32),
    )
    return pl.pallas_call(
        kernel,
        grid_spec=pltpu.PrefetchScalarGridSpec(
            num_scalar_prefetch=2,
            grid=(seqs, heads),
            in_specs=[
                part(0),
                part(1),
                part(2),
                pl.BlockSpec((2, n, 1, rows, 1), lambda g, h, *_: (0, 0, g, 0, 0)),
                pl.BlockSpec((2, 1, HEAD_DIM), lambda g, h, *_: (0, 0, h)),
                whole(cosines),
                whole(sines),
            ],
            out_specs=(
                line,
                line,
                line,
                pl.BlockSpec((n, 1, rows, HEAD_DIM), lambda g, h, *_: (0, g, 0, h)),
                pl.BlockSpec((1, 1, span, 1), lambda g, h, *_: (g, h, 0, 0)),
            ),
        ),
        out_shape=outs,
        compiler_params=params(2),
        cost_estimate=cost(3 * seqs * heads * span * span * HEAD_DIM, qkv, *outs[:4]),
        name="attention",
    )(place, lengths, qkv, qkv, qkv, inverse, gains, cosines, sines)


def attention_backward(place, lengths, q, k, v, grad, lse, qkv, inverse, gains, cosines, sines):
    n, seqs, rows, wide = qkv.shape
    cols = wide // 3
    heads = cols // HEAD_DIM
    span = n * rows
    scale = HEAD_DIM ** (-0.5)

    def kernel(
        place_ref, len_ref, q_i, k_i, v_i, do_i, lse_i, qp_i, kp_i, inv, gain_ref, cos_ref, sin_ref,
        dq_o, dk_o, dv_o, st_o, dg_o, dq_s, dk_s, dv_s,
    ):
        here = place_ref[0]
        length = len_ref[pl.program_id(0)]
        dk_s[...] = jnp.zeros_like(dk_s)
        dv_s[...] = jnp.zeros_like(dv_s)
        for p in range(n):
            at = slice(p * rows, (p + 1) * rows)
            kv = (p + 1) * rows
            query, keys, values, do = q_i[0, at, :], k_i[0, :kv, :], v_i[0, :kv, :], do_i[p, 0]
            s = dot_nt(keys, query) * scale
            col = lax.broadcasted_iota(jnp.int32, (kv, rows), 0)
            row = p * rows + lax.broadcasted_iota(jnp.int32, (kv, rows), 1)
            allowed = (col <= row) & (col < length)
            probs = jnp.where(allowed, jnp.exp(s - lse_i[0, 0, :, at]), 0.0)
            dp = dot_nt(values, do)
            ds = (probs * (dp - jnp.sum(probs * dp, axis=0, keepdims=True))).astype(bf16)
            dq_s[at, :] = dot_tn(ds, keys) * scale
            dk_s[:kv, :] += dot(ds, query)
            dv_s[:kv, :] += dot(probs.astype(bf16), do)
        dk_s[...] = dk_s[...] * scale
        sums = [jnp.zeros((1, HEAD_DIM), f32)] * 2
        for p in range(n):
            j = lax.rem(here + (n - p), n)
            at = slice(p * rows, (p + 1) * rows)
            for which, (src, raw, dst) in enumerate(((dq_s, qp_i, dq_o), (dk_s, kp_i, dk_o))):
                dz = turn_back(src[at, :], cos_ref[p], sin_ref[p])
                moved = raw[j, 0] * dz
                dst[j, 0] = dz
                st_o[which, 0, 0, j] = jnp.sum(moved * gain_ref[which], axis=-1, keepdims=True)
                sums[which] += jnp.sum(moved * inv[which, j, 0], axis=0, keepdims=True)
            dv_o[j, 0] = dv_s[at, :].astype(bf16)
        for which in range(2):
            dg_o[which, 0] = sums[which]

    def part(i):
        return pl.BlockSpec((n, 1, rows, HEAD_DIM), lambda g, h, *_: (0, g, 0, i * heads + h))

    line = pl.BlockSpec((1, span, HEAD_DIM), lambda g, h, *_: (g, 0, h))
    block = part(0)
    outs = (
        struct((n, seqs, rows, cols), f32),
        struct((n, seqs, rows, cols), f32),
        struct((n, seqs, rows, cols), bf16),
        struct((2, seqs, heads, n, rows, 1), f32),
        struct((2, seqs, 1, cols), f32),
    )
    return pl.pallas_call(
        kernel,
        grid_spec=pltpu.PrefetchScalarGridSpec(
            num_scalar_prefetch=2,
            grid=(seqs, heads),
            in_specs=[
                line,
                line,
                line,
                block,
                pl.BlockSpec((1, 1, 1, span), lambda g, h, *_: (g, h, 0, 0)),
                part(0),
                part(1),
                pl.BlockSpec((2, n, 1, rows, 1), lambda g, h, *_: (0, 0, g, 0, 0)),
                pl.BlockSpec((2, 1, HEAD_DIM), lambda g, h, *_: (0, 0, h)),
                whole(cosines),
                whole(sines),
            ],
            out_specs=(
                block,
                block,
                block,
                pl.BlockSpec((2, 1, 1, n, rows, 1), lambda g, h, *_: (0, g, h, 0, 0, 0)),
                pl.BlockSpec((2, 1, 1, HEAD_DIM), lambda g, h, *_: (0, g, 0, h)),
            ),
            scratch_shapes=[pltpu.VMEM((span, HEAD_DIM), f32)] * 3,
        ),
        out_shape=outs,
        compiler_params=params(2),
        cost_estimate=cost(7 * seqs * heads * span * span * HEAD_DIM, qkv, *outs[:3]),
        name="attention_back",
    )(
        place, lengths, q, k, v, grad, lse.reshape(seqs, heads, 1, span), qkv, qkv, inverse, gains,
        cosines, sines,
    )


def back_project(dzq, dzk, dv, qkv, inverse, stats, gains, weight, first, pieces):
    total, third = dv.shape
    width = weight.shape[0]
    rows = total // pieces
    tile = min(512, width)

    def kernel(dzq_i, dzk_i, dv_i, q_i, k_i, inv, st, gain_ref, wq, wk, wv, *rest):
        outs, low = rest[:pieces], rest[pieces]

        @pl.when(pl.program_id(0) == 0)
        def _():
            for which, (dz, raw) in enumerate(((dzq_i, q_i), (dzk_i, k_i))):
                r = inv[which]
                low[:, which * third : (which + 1) * third] = (
                    r * (gain_ref[which] * dz[...]) - raw[...] * (r * r * r * st[which])
                ).astype(bf16)
            low[:, 2 * third :] = dv_i[...]

        for i in range(pieces):
            at = slice(i * rows, (i + 1) * rows)
            outs[i][...] = (
                dot_nt(low[at, :third], wq[...])
                + dot_nt(low[at, third : 2 * third], wk[...])
                + dot_nt(low[at, 2 * third :], wv[...])
            ).astype(bf16)

    def raw(k):
        return pl.BlockSpec((total, third), lambda d: (0, k))

    def taken(k):
        return pl.BlockSpec((tile, third), lambda d: (d, first + k))

    outs = (struct((rows, width), bf16),) * pieces + (struct((total, 3 * third), bf16),)
    return pl.pallas_call(
        kernel,
        grid=(width // tile,),
        in_specs=[whole(dzq), whole(dzk), whole(dv), raw(0), raw(1)]
        + [whole(inverse), whole(stats), whole(gains), taken(0), taken(1), taken(2)],
        out_specs=(pl.BlockSpec((rows, tile), lambda d: (0, d)),) * pieces
        + (pl.BlockSpec((total, 3 * third), lambda d: (0, 0)),),
        out_shape=outs,
        compiler_params=params(1),
        cost_estimate=cost(6 * total * width * third, dzq, dzk, dv, *outs),
        name="back_project",
    )(dzq, dzk, dv, qkv, qkv, inverse, stats, gains, weight, weight, weight)


def out_project(att, rows_in, weight, gain):
    n, rows, cols = att.shape
    width = n * cols

    def kernel(a_i, x_i, w_i, gain_ref, h_o, n_o, acc):
        p = pl.program_id(0)

        @pl.when(p == 0)
        def _():
            acc[...] = x_i[...].astype(f32)

        acc[...] += dot(a_i[0], w_i[...])

        @pl.when(p == n - 1)
        def _():
            h = acc[...]
            h_o[...] = h
            r = lax.rsqrt(jnp.mean(h * h, axis=-1, keepdims=True) + EPS)
            n_o[...] = (h * r * gain_ref[...]).astype(bf16)

    outs = (struct((rows, width), f32), struct((rows, width), bf16))
    return pl.pallas_call(
        kernel,
        grid=(n,),
        in_specs=[
            pl.BlockSpec((1, rows, cols), lambda p: (p, 0, 0)),
            whole(rows_in),
            pl.BlockSpec((cols, width), lambda p: (p, 0)),
            whole(gain),
        ],
        out_specs=(pl.BlockSpec((rows, width), lambda p: (0, 0)),) * 2,
        out_shape=outs,
        scratch_shapes=[pltpu.VMEM((rows, width), f32)],
        compiler_params=params(1),
        cost_estimate=cost(2 * rows * width * width, att, rows_in, *outs),
        name="out_project",
    )(att, rows_in, weight, gain)


def out_back(moved, part, low, hidden, gain, weight, n):
    rows, width = hidden.shape
    cols = width // n

    def kernel(m_i, p_i, l_i, h_i, gain_ref, w_i, gh_o, da_o, do_o, fg_o):
        @pl.when(pl.program_id(0) == 0)
        def _():
            dz = m_i[...].astype(f32) + p_i[...].astype(f32)
            v = h_i[...]
            r = lax.rsqrt(jnp.mean(v * v, axis=-1, keepdims=True) + EPS)
            fg_o[...] = jnp.sum(dz * v * r, axis=0, keepdims=True)
            scaled = dz * gain_ref[...]
            inner = jnp.mean(v * scaled, axis=-1, keepdims=True)
            total = l_i[...].astype(f32) + r * scaled - v * (r * r * r * inner)
            gh_o[...] = total
            da_o[...] = total.astype(bf16)

        do_o[0] = dot_nt(da_o[...], w_i[...]).astype(bf16)

    outs = (
        struct((rows, width), f32),
        struct((rows, width), bf16),
        struct((n, rows, cols), bf16),
        struct((1, width), f32),
    )
    full = pl.BlockSpec((rows, width), lambda p: (0, 0))
    return pl.pallas_call(
        kernel,
        grid=(n,),
        in_specs=[whole(moved), whole(part), whole(low), whole(hidden), whole(gain)]
        + [pl.BlockSpec((cols, width), lambda p: (p, 0))],
        out_specs=(
            full,
            full,
            pl.BlockSpec((1, rows, cols), lambda p: (p, 0, 0)),
            pl.BlockSpec((1, width), lambda p: (0, 0)),
        ),
        out_shape=outs,
        compiler_params=params(1),
        cost_estimate=cost(2 * rows * width * width, hidden, *outs),
        name="out_back",
    )(moved, part, low, hidden, gain, weight)


def weight_grads(lefts, rights, columns, name):
    count = len(lefts)
    total, wide = rights[0].shape
    folded = len(lefts[0].shape) == 3
    width = columns.shape[0]
    tile = lefts[0].shape[2] if folded else min(512, width)

    def kernel(*refs):
        ls, rs, (column_ref, o) = refs[:count], refs[count : 2 * count], refs[2 * count :]
        o[:, :wide] = sum(
            dot_tn(ls[g][0] if folded else ls[g][...], rs[g][...]) for g in range(count)
        ).astype(bf16)
        o[:, wide:] = column_ref[...]

    if folded:
        left = pl.BlockSpec((1, total, tile), lambda p: (p, 0, 0))
    else:
        left = pl.BlockSpec((total, tile), lambda p: (0, p))
    out = struct((width, wide + LANES), bf16)
    return pl.pallas_call(
        kernel,
        grid=(width // tile,),
        in_specs=[left] * count
        + [whole(x) for x in rights]
        + [pl.BlockSpec((tile, LANES), lambda p: (p, 0))],
        out_specs=pl.BlockSpec((tile, wide + LANES), lambda p: (p, 0)),
        out_shape=out,
        compiler_params=params(1),
        cost_estimate=cost(2 * count * total * width * wide, *lefts, *rights, out),
        name=name,
    )(*lefts, *rights, columns)


def picks(rank_ref, nb, cap):
    row = rank_ref[0, nb : nb + 1, :]
    return lax.broadcasted_iota(jnp.int32, (cap, row.shape[1]), 0) == row


def slot_weight(hot, coef_ref, nb):
    return jnp.sum(jnp.where(hot, coef_ref[0, nb : nb + 1, :], 0.0), axis=-1, keepdims=True)


def in_place(arrays, given):
    if arrays is None:
        return (), [], {}
    return (
        tuple(arrays),
        [pl.BlockSpec(memory_space=pl.ANY)] * len(arrays),
        {given + i: i for i in range(len(arrays))},
    )


def expert_forward(pieces, rank, gate_up, cap, start, stop, begun=None):
    experts, blocks, rows = rank.shape
    width, hidden = gate_up.shape[1:]
    slots = blocks * cap
    tile = min(256, hidden)
    more, more_specs, aliases = in_place(begun, blocks + 3)

    def kernel(*refs):
        xs, (rank_ref, wg, wu), (x_o, g_o, u_o, a_o) = (
            refs[:blocks],
            refs[blocks : blocks + 3],
            refs[-4:],
        )

        @pl.when(pl.program_id(1) == 0)
        def _():
            for nb in range(blocks):
                hot = picks(rank_ref, nb, cap).astype(bf16)
                x_o[0, nb * cap : (nb + 1) * cap, :] = dot(hot, xs[nb][...]).astype(bf16)

        x = x_o[0]
        gate = dot(x, wg[0])
        upper = dot(x, wu[0])
        s = jax.nn.sigmoid(gate)
        silu = gate * s
        g_o[0] = (upper * (s + silu * (1.0 - s))).astype(bf16)
        u_o[0] = silu.astype(bf16)
        a_o[0] = (silu * upper).astype(bf16)

    tiled = pl.BlockSpec((1, slots, tile), lambda e, f: (start + e, 0, f))
    outs = (struct((experts, slots, width), bf16),) + (struct((experts, slots, hidden), bf16),) * 3
    return pl.pallas_call(
        kernel,
        grid=(stop - start, hidden // tile),
        in_specs=[whole(x) for x in pieces]
        + [
            pl.BlockSpec((1, blocks, rows), lambda e, f: (start + e, 0, 0)),
            pl.BlockSpec((1, width, tile), lambda e, f: (start + e, 0, f)),
            pl.BlockSpec((1, width, tile), lambda e, f: (experts + start + e, 0, f)),
        ]
        + more_specs,
        out_specs=(
            pl.BlockSpec((1, slots, width), lambda e, f: (start + e, 0, 0)),
            tiled,
            tiled,
            tiled,
        ),
        out_shape=outs,
        input_output_aliases=aliases,
        compiler_params=params(2),
        cost_estimate=cost(4 * (stop - start) * slots * width * hidden, *pieces),
        name="expert_forward",
    )(*pieces, rank, gate_up, gate_up, *more)


def expert_output(active, rank, coef, down, cap):
    experts, blocks, rows = rank.shape
    hidden, width = down.shape[1:]
    slots = blocks * cap
    tile = min(512, width)

    def kernel(a_i, rank_ref, coef_ref, wd, *rest):
        outs, acc = rest[:blocks], rest[blocks]
        e = pl.program_id(1)

        @pl.when(e == 0)
        def _():
            acc[...] = jnp.zeros_like(acc)

        y = dot(a_i[0], wd[0])
        for nb in range(blocks):
            hot = picks(rank_ref, nb, cap)
            weighed = y[nb * cap : (nb + 1) * cap, :] * slot_weight(hot, coef_ref, nb)
            acc[nb] += dot_tn(hot.astype(bf16), weighed.astype(bf16))

        @pl.when(e == experts - 1)
        def _():
            for nb in range(blocks):
                outs[nb][...] = acc[nb].astype(bf16)

    table = pl.BlockSpec((1, blocks, rows), lambda d, e: (e, 0, 0))
    outs = (struct((rows, width), bf16),) * blocks
    return pl.pallas_call(
        kernel,
        grid=(width // tile, experts),
        in_specs=[
            pl.BlockSpec((1, slots, hidden), lambda d, e: (e, 0, 0)),
            table,
            table,
            pl.BlockSpec((1, hidden, tile), lambda d, e: (e, 0, d)),
        ],
        out_specs=(pl.BlockSpec((rows, tile), lambda d, e: (0, d)),) * blocks,
        out_shape=outs,
        scratch_shapes=[pltpu.VMEM((blocks, rows, tile), f32)],
        compiler_params=params(2),
        cost_estimate=cost(2 * experts * slots * width * hidden, active, down, *outs),
        name="expert_output",
    )(active, rank, coef, down)


def expert_backward(pieces, rank, coef, down, gate, upper, active, cap):
    experts, blocks, rows = rank.shape
    hidden, width = down.shape[1:]
    slots = blocks * cap
    tile = min(256, hidden)

    def kernel(*refs):
        ds, (rank_ref, coef_ref, wd, g_i, u_i, a_i), (dg_o, du_o, dw_o, dy) = (
            refs[:blocks],
            refs[blocks : blocks + 6],
            refs[blocks + 6 :],
        )

        @pl.when(pl.program_id(1) == 0)
        def _():
            for nb in range(blocks):
                hot = picks(rank_ref, nb, cap)
                picked = dot(hot.astype(bf16), ds[nb][...])
                dy[nb * cap : (nb + 1) * cap, :] = (
                    picked * slot_weight(hot, coef_ref, nb)
                ).astype(bf16)

        da = dot_nt(dy[...], wd[0])
        du_o[0] = (da * u_i[0].astype(f32)).astype(bf16)
        dg_o[0] = (da * g_i[0].astype(f32)).astype(bf16)

        dw_o[0] = dot_tn(a_i[0], dy[...]).astype(bf16)

    table = pl.BlockSpec((1, blocks, rows), lambda e, f: (e, 0, 0))
    tiled = pl.BlockSpec((1, slots, tile), lambda e, f: (e, 0, f))
    line = pl.BlockSpec((1, tile, width), lambda e, f: (e, f, 0))
    outs = (struct((experts, slots, hidden), bf16),) * 2 + (struct((experts, hidden, width), bf16),)
    return pl.pallas_call(
        kernel,
        grid=(experts, hidden // tile),
        in_specs=[whole(x) for x in pieces] + [table, table, line, tiled, tiled, tiled],
        out_specs=(tiled, tiled, line),
        out_shape=outs,
        scratch_shapes=[pltpu.VMEM((slots, width), bf16)],
        compiler_params=params(2),
        cost_estimate=cost(
            4 * experts * slots * width * hidden, *pieces, down, gate, upper, active, *outs
        ),
        name="expert_backward",
    )(*pieces, rank, coef, down, gate, upper, active)


def expert_input_grad(dgate, dupper, rank, gate_up, cap, g, seqs):
    blocks, rows = rank.shape[1:]
    width, hidden = gate_up.shape[1:]
    experts = gate_up.shape[0] // 2
    slots = blocks * cap
    tile = min(1024, width)

    def kernel(dg_i, du_i, rank_ref, wg, wu, *rest):
        outs, acc = rest[:blocks], rest[blocks]
        e = pl.program_id(1)

        @pl.when(e == 0)
        def _():
            acc[...] = jnp.zeros_like(acc)

        dx = (dot_nt(dg_i[0], wg[0]) + dot_nt(du_i[0], wu[0])).astype(bf16)
        for nb in range(blocks):
            hot = picks(rank_ref, nb, cap).astype(bf16)
            acc[nb] += dot_tn(hot, dx[nb * cap : (nb + 1) * cap, :])

        @pl.when(e == experts - 1)
        def _():
            for nb in range(blocks):
                outs[nb][...] = acc[nb].astype(bf16)

    line = pl.BlockSpec((1, slots, hidden), lambda d, e: (e, g, 0))
    outs = (struct((rows, width), bf16),) * blocks
    return pl.pallas_call(
        kernel,
        grid=(width // tile, experts),
        in_specs=[
            line,
            line,
            pl.BlockSpec((1, blocks, rows), lambda d, e: (e * seqs + g, 0, 0)),
            pl.BlockSpec((1, tile, hidden), lambda d, e: (e, d, 0)),
            pl.BlockSpec((1, tile, hidden), lambda d, e: (experts + e, d, 0)),
        ],
        out_specs=(pl.BlockSpec((rows, tile), lambda d, e: (0, d)),) * blocks,
        out_shape=outs,
        scratch_shapes=[pltpu.VMEM((blocks, rows, tile), f32)],
        compiler_params=params(2),
        cost_estimate=cost(4 * experts * slots * width * hidden, gate_up, *outs),
        name="expert_input_grad",
    )(dgate, dupper, rank, gate_up, gate_up)


def expert_weight_grad(x, dgate, dupper, start, stop, begun=None):
    experts, slots, width = x.shape
    hidden = dgate.shape[2]
    tile = min(512, width)
    more, more_specs, aliases = in_place(begun, 3)

    def kernel(x_i, dg_i, du_i, *rest):
        o = rest[-1]
        o[0, 0] = dot_tn(x_i[0], dg_i[0]).astype(bf16)
        o[1, 0] = dot_tn(x_i[0], du_i[0]).astype(bf16)

    line = pl.BlockSpec((1, slots, hidden), lambda e, d: (start + e, 0, 0))
    return pl.pallas_call(
        kernel,
        grid=(stop - start, width // tile),
        in_specs=[pl.BlockSpec((1, slots, tile), lambda e, d: (start + e, 0, d)), line, line]
        + more_specs,
        out_specs=(pl.BlockSpec((2, 1, tile, hidden), lambda e, d: (0, start + e, d, 0)),),
        out_shape=(struct((2, experts, width, hidden), bf16),),
        input_output_aliases=aliases,
        compiler_params=params(2),
        cost_estimate=cost(4 * (stop - start) * slots * width * hidden, x),
        name="expert_weight_grad",
    )(x, dgate, dupper, *more)


def tables(positions):
    half = HEAD_DIM // 2
    inverse = THETA ** (-(jnp.arange(half, dtype=f32) * 2.0) / HEAD_DIM)
    angle = positions.astype(f32)[:, None] * inverse[None, :]
    cosines, sines = jnp.cos(angle), jnp.sin(angle)
    return (
        jnp.concatenate([cosines, cosines], axis=-1),
        jnp.concatenate([-sines, sines], axis=-1),
    )


def norm_back(v, gain, dz):
    r = lax.rsqrt(jnp.mean(v * v, axis=-1, keepdims=True) + EPS)
    moved = dz * gain
    return r * moved - v * (r * r * r) * jnp.mean(v * moved, axis=-1, keepdims=True), dz * v * r


def body(
    tokens, lengths, expert_ids, route_levels, w_query, w_key, w_value, w_out,
    attn_gain, query_gain, key_gain, ffn_gain, w_gate, w_up, w_down, cotangent,
):
    batches, sequences, rows, width = tokens.shape
    top = expert_ids.shape[-1]
    experts = w_gate.shape[0]
    n = lax.axis_size("ctx")
    here = lax.axis_index("ctx")
    seqs = batches * sequences
    cols = width // n
    own = w_query.shape[0]
    cap = rows * top * 5 // (4 * experts * n)
    cap = -(-cap // 16) * 16
    blocks = n * seqs
    up = [(i, (i + 1) % n) for i in range(n)]
    place = here.reshape(1).astype(jnp.int32)

    def after(value, *others):
        return lax.optimization_barrier((value, others))[0]

    class Ring:
        def __init__(self, piece):
            self.held = [piece]

        def hop(self, prev):
            if len(self.held) == n:
                return ()
            self.held.append(lax.ppermute(after(self.held[-1], prev), "ctx", up))
            return (self.held[-1],)

    class Sum:
        def __init__(self, parts):
            self.parts = parts
            self.moved = None
            self.at = 1

        def hop(self, prev):
            if self.at == n:
                return ()
            part = after(self.parts[self.at], prev)
            if self.moved is not None:
                part = (after(self.moved, prev).astype(f32) + part.astype(f32)).astype(bf16)
            self.moved = lax.ppermute(part, "ctx", up)
            self.at += 1
            return (self.moved,)

    def finish(ring, prev):
        while got := ring.hop(prev):
            prev = (prev, got)
        return prev

    def direct(x):
        return [x] + [
            lax.ppermute(x, "ctx", [(i, (i + k) % n) for i in range(n)]) for k in range(1, n)
        ]

    def ctx_sum(x):
        held = direct(x)
        return sum((jnp.roll(held[k], k, axis=0) for k in range(1, n)), held[0])

    def exchange(x):
        return lax.all_to_all(x, "ctx", split_axis=0, concat_axis=0, tiled=True)

    gains = jnp.stack([attn_gain, query_gain, key_gain, ffn_gain], axis=1)
    gains = jnp.pad(gains, ((0, 0), (0, LANES - 4)))
    sent = jnp.stack(
        [
            jnp.swapaxes(expert_ids.reshape(seqs, rows, top), 1, 2),
            jnp.swapaxes(route_levels.reshape(seqs, rows, top), 1, 2),
        ]
    )
    sent = sent.astype(bf16).reshape(own, -1)
    extra = sent.shape[1]
    mine = jnp.concatenate(
        [jnp.broadcast_to(w_out[None], (n, own, width))]
        + [jnp.swapaxes(w.reshape(own, n, cols), 0, 1) for w in (w_query, w_key, w_value)]
        + [jnp.broadcast_to(one[None], (n, *one.shape)) for one in (gains, sent)],
        axis=2,
    )
    mine = exchange(mine)
    routes = mine[:, :, -extra:].reshape(n, 2, seqs, top, rows)
    order = lax.rem(here + n - jnp.arange(n, dtype=jnp.int32), n)
    routes = jnp.take(routes, order, axis=0)
    mine = mine.reshape(n * own, -1)
    att_w = lax.all_gather(mine, "batch", axis=0, tiled=True)
    all_gains = att_w[:, width + 3 * cols : width + 3 * cols + 4].astype(f32).T
    gain_attn, gain_ffn = all_gains[0], all_gains[3]
    qk_gains = lax.dynamic_slice_in_dim(all_gains[1:3], here * cols, cols, 1).reshape(2, 1, cols)

    xs = tokens.reshape(seqs, rows, width)
    span_len = lengths.reshape(seqs)
    local_pos = here * rows + jnp.arange(rows, dtype=jnp.int32)
    live = (local_pos[None, :] < span_len[:, None])[:, :, None]
    grad_low = jnp.where(live, cotangent.reshape(seqs, rows, width), jnp.zeros((), bf16))
    def slots_of(routes):
        chosen = jnp.swapaxes(routes[:, 0], 0, 1).reshape(blocks, top, rows).astype(jnp.int32)
        levels = jnp.swapaxes(routes[:, 1], 0, 1).reshape(blocks, top, rows).astype(f32)
        share = levels / jnp.sum(levels, axis=1, keepdims=True)
        owned = here * experts + jnp.arange(experts, dtype=jnp.int32)
        hit = chosen[None] == owned[:, None, None, None]
        named = jnp.any(hit, axis=2)
        coef = jnp.sum(jnp.where(hit, share[None], 0.0), axis=2)
        at = jnp.arange(rows, dtype=jnp.int32)
        upto = (at[:, None] <= at[None, :]).astype(bf16)
        count = jnp.dot(
            named.astype(bf16).reshape(experts * blocks, rows), upto, preferred_element_type=f32
        )
        count = count.reshape(experts, blocks, rows).astype(jnp.int32)
        return jnp.where(named, count - 1, -1), coef

    cosines, sines = tables(jnp.arange(n * rows, dtype=jnp.int32))
    cosines = cosines.reshape(n, rows, HEAD_DIM)
    sines = sines.reshape(n, rows, HEAD_DIM)
    kept, atts, hiddens = [None] * seqs, [None] * seqs, [None] * seqs
    xr = [Ring(xs[g]) for g in range(seqs)]
    nr = [None] * seqs

    def projected(g, prev):
        normed, qkv, squares = project(
            [after(xr[g].held[0], prev)] + xr[g].held[1:], gain_attn[None, :], att_w, cols, n
        )
        return normed, qkv.reshape(n, 1, rows, 3 * cols), squares

    def scales(squares, prev):
        squares = jnp.swapaxes(squares[:2].reshape(2, n, rows), 0, 1)
        inverse = lax.rsqrt(ctx_sum(after(squares, prev)) / width + EPS)
        return jnp.swapaxes(inverse, 0, 1).reshape(2, n, 1, rows, 1)

    def attended(g, normed, qkv, inverse, prev):
        q, k, v, att, lse = attention_forward(
            place, span_len[g : g + 1], qkv, after(inverse, prev), qk_gains, cosines, sines
        )
        kept[g] = (q, k, v, lse, qkv, inverse, normed)
        return att.reshape(n, rows, cols)

    def out_projected(g, prev):
        hiddens[g], n2 = out_project(
            after(atts[g], prev), xs[g], att_w, gain_ffn[None, :]
        )
        nr[g] = Ring(n2)
        return (n2,)

    stage = (xr[0].hop(()), mine)
    rank, coef = slots_of(after(routes, stage))
    stage = xr[0].hop(stage)
    gate_up = lax.all_gather(
        jnp.concatenate([after(w_gate, stage), w_up], axis=0), "batch", axis=1, tiled=True
    )
    down = lax.all_gather(after(w_down, stage), "batch", axis=2, tiled=True)
    stage = finish(xr[0], stage)
    first = None
    for g in range(seqs):
        last = g + 1 == seqs
        if not last:
            stage = xr[g + 1].hop(stage)
            moving = xr[g + 1].hop(stage)
        else:
            moving = ()
        if first is not None:
            moving = (exchange(after(first, stage)),)
        normed, qkv, squares = projected(g, stage)
        stage = (squares, moving)
        inverse = scales(squares, stage)
        if first is not None:
            atts[g - 1] = moving[0]
            stage = (inverse, out_projected(g - 1, stage))
        else:
            stage = (inverse,)
        moving = () if last else xr[g + 1].hop(stage)
        if first is not None:
            moving += nr[g - 1].hop(stage)
        att = attended(g, normed, qkv, inverse, stage)
        stage = (att, moving)
        if not last:
            stage = finish(xr[g + 1], stage)
        first = att
    g = seqs - 1
    moving = nr[g - 1].hop(stage) if g else ()
    atts[g] = exchange(after(first, stage))
    stage = (atts[g], moving)
    moving = nr[g - 1].hop(stage) if g else ()
    stage = (out_projected(g, stage), moving)
    for one in nr:
        stage = finish(one, stage)

    grad_hiddens, datts, dos = [None] * seqs, [None] * seqs, [None] * seqs
    lows, dn = [None] * seqs, [None] * seqs
    qk_part = jnp.zeros((2, cols), f32)

    def out_backed(g, prev):
        grad_hiddens[g], datts[g], do, one = out_back(
            after(zr[g].moved, prev), dx_parts[g][0], grad_low[g], hiddens[g], gain_ffn[None, :],
            att_w, n,
        )
        return do, one

    def attention_backed(g, prev):
        q, k, v, lse, qkv, inverse, _ = kept[g]
        *grads, stats, qk_one = attention_backward(
            place, span_len[g : g + 1], after(q, prev), k, v, dos[g].reshape(n, 1, rows, cols),
            lse, qkv, inverse, qk_gains, cosines, sines,
        )
        stats = jnp.sum(stats.reshape(2, cols // HEAD_DIM, n, rows), axis=1)
        return grads, jnp.swapaxes(stats, 0, 1), qk_one.reshape(2, cols)

    def summed_stats(stats, prev):
        return jnp.swapaxes(ctx_sum(after(stats, prev)), 0, 1) / width

    def back_projected(g, grads, stats, prev):
        qkv, inverse = kept[g][4:6]
        *dn1, lows[g] = back_project(
            *(one.reshape(n * rows, cols) for one in grads), qkv.reshape(n * rows, 3 * cols),
            inverse.reshape(2, n * rows, 1), after(stats, prev).reshape(2, n * rows, 1), qk_gains,
            att_w, n, n,
        )
        dn[g] = Sum(dn1)
        return (lows[g],)

    dr = [Ring(grad_low[g]) for g in range(seqs)]
    n_pieces = [nr[g].held[j] for g in range(seqs) for j in range(n)]
    held = None
    for start, stop in ((0, experts // 2), (experts // 2, experts)):
        moving = [one.hop(stage) for one in dr]
        held = expert_forward(
            n_pieces, after(rank, stage), gate_up, cap, start, stop, held
        )
        stage = (held, moving)
    slots_x, by_gate, by_upper, active = held
    moving = [one.hop(stage) for one in dr]
    y_parts = expert_output(after(active, stage), rank, coef, down, cap)
    stage = (y_parts, moving)
    stage = [finish(one, stage) for one in dr] or stage
    grad_pieces = [dr[g].held[j] for g in range(seqs) for j in range(n)]
    yr = [Sum(y_parts[g * n : (g + 1) * n]) for g in range(seqs)]
    moving = [one.hop(stage) for one in yr]
    dgate, dupper, grad_down = expert_backward(
        grad_pieces, after(rank, stage), coef, down, by_gate, by_upper, active, cap
    )
    stage = (dgate, moving)
    grad_down = lax.psum_scatter(
        after(grad_down, stage), "batch", scatter_dimension=2, tiled=True
    )
    rank_rows = rank.reshape(experts * seqs, n, rows)

    def input_grad(g, prev):
        dx_parts.append(
            expert_input_grad(after(dgate, prev), dupper, rank_rows, gate_up, cap, g, seqs)
        )
        zr.append(Sum(dx_parts[g]))
        return dx_parts[g]

    zr, dx_parts = [], []
    moving = [one.hop(stage) for one in yr]
    stage = (input_grad(0, stage), moving)
    held = None
    for start, stop in ((0, experts // 2), (experts // 2, experts)):
        moving = zr[0].hop(stage)
        held = expert_weight_grad(slots_x, after(dgate, stage), dupper, start, stop, held)
        stage = (held, moving)
    gu_local = held[0].reshape(2 * experts, width, -1)
    grad_gu = lax.psum_scatter(
        after(gu_local, stage), "batch", scatter_dimension=1, tiled=True
    )
    for g in range(1, seqs):
        moving = (zr[0].hop(stage), yr[0].hop(stage))
        stage = (input_grad(g, stage), moving)
    stage = (finish(zr[0], stage), grad_down)
    moving = zr[1].hop(stage) if seqs > 1 else ()
    do, ffn_part = out_backed(0, stage)
    stage = (do, moving)

    held = None
    for g in range(seqs):
        last = g + 1 == seqs
        moving = () if last else zr[g + 1].hop(stage)
        dos[g] = exchange(after(do, stage))
        if held is not None:
            moving += back_projected(g - 1, *held, stage)
        if last:
            column = jnp.pad(ffn_part.T.astype(bf16), ((0, 0), (0, LANES - 1)))
            grad_out = weight_grads(atts, datts, after(column, stage), "out_weight_grad")
            moving += (grad_out,)
        stage = (dos[g], moving)
        if last:
            grad_out = lax.psum_scatter(
                after(grad_out, stage), "batch", scatter_dimension=0, tiled=True
            )
        moving = () if last else zr[g + 1].hop(stage)
        if held is not None:
            moving += dn[g - 1].hop(stage)
        grads, stats, one = attention_backed(g, stage)
        qk_part = qk_part + one
        stage = (stats, moving)
        if not last:
            stage = finish(zr[g + 1], stage)
        stats = summed_stats(stats, stage)
        if not last:
            moving = yr[-1].hop(stage)
            do, one = out_backed(g + 1, stage)
            ffn_part = ffn_part + one
            stage = (stats, do, moving)
        else:
            stage = (stats,)
        held = (grads, stats)
    g = seqs - 1
    stage = (stage, grad_gu)
    moving = dn[g - 1].hop(stage) if g else ()
    stage = (back_projected(g, *held, stage), moving)
    qk_rows = lax.dynamic_update_slice_in_dim(
        jnp.zeros((2, width), f32), qk_part, here * cols, 1
    )
    columns = jnp.pad(qk_rows.T.astype(bf16), ((0, 0), (0, LANES - 2)))
    moving = dn[g - 1].hop(stage) if g else ()
    grad_qkv = weight_grads(
        [one[-1] for one in kept], lows, after(columns, stage), "qkv_weight_grad"
    )
    stage = (grad_qkv, moving)
    grad_qkv = lax.psum_scatter(
        after(grad_qkv, stage), "batch", scatter_dimension=0, tiled=True
    )
    while len(left := [one for one in dn[::-1] + yr if one.at < n][:2]):
        stage = ([one.hop(stage) for one in left], grad_out)
    outs = [
        jnp.where(
            live[g], hiddens[g] + (yr[g].moved.astype(f32) + yr[g].parts[0].astype(f32)), 0.0
        ).astype(bf16)
        for g in range(seqs)
    ]
    token_grads = []
    for g in range(seqs):
        grad_n1 = dn[g].moved.astype(f32) + dn[g].parts[0].astype(f32)
        back, _ = norm_back(xs[g].astype(f32), gain_attn, grad_n1)
        token_grads.append(grad_hiddens[g] + back)
    grad_out, summed = lax.optimization_barrier(
        (exchange(grad_out.reshape(n, own, -1)), exchange(grad_qkv.reshape(n, own, -1)))
    )
    grad_out, summed = grad_out.astype(f32), summed.astype(f32)
    grad_ffn_gain = jnp.sum(grad_out[:, :, width], axis=0)
    grad_out = jnp.sum(grad_out[:, :, :width], axis=0)
    grad_q, grad_k, grad_v = (
        jnp.swapaxes(summed[:, :, i * cols : (i + 1) * cols], 0, 1).reshape(own, width)
        for i in range(3)
    )
    gain_sums = jnp.sum(summed[:, :, 3 * cols :], axis=0)
    grad_attn_gain = (
        jnp.sum(
            w_query.astype(f32) * grad_q
            + w_key.astype(f32) * grad_k
            + w_value.astype(f32) * grad_v,
            axis=1,
        )
        / attn_gain.astype(f32)
    )
    shape = (batches, sequences, rows, width)
    return (
        jnp.stack(outs).reshape(shape),
        jnp.stack(token_grads).reshape(shape),
        grad_q,
        grad_k,
        grad_v,
        grad_out,
        grad_attn_gain,
        gain_sums[:, 0],
        gain_sums[:, 1],
        grad_ffn_gain,
        grad_gu[:experts].astype(f32),
        grad_gu[experts:].astype(f32),
        grad_down.astype(f32),
    )


def solution(mesh):
    rows = P(None, "batch", "ctx", None)
    flat = P(("batch", "ctx"), None)
    line = P(("batch", "ctx"))
    wide = P("ctx", "batch", None)
    tall = P("ctx", None, "batch")
    in_specs = (rows, P(None, "batch"), rows, rows) + (flat,) * 4 + (line,) * 4
    in_specs += (wide, wide, tall, rows)
    out_specs = (rows, rows) + (flat,) * 4 + (line,) * 4 + (wide, wide, tall)
    return jax.shard_map(body, mesh=mesh, in_specs=in_specs, out_specs=out_specs, check_vma=False)
```
